32 devices in a mesh: fsdp: 32 (over z, y, x, core).
Axes of the slice: x: 2, y: 2, z: 4, core: 2. Of those that a mesh axis runs over, the one named last changes fastest.
Arguments:
- block_input: bfloat16 [32768, 768], P('fsdp'), may hold values from -6 to 6
- seg_ids: int32 [64, 512], P('fsdp'), may hold values from 0 to 3, never falling along the last dimension, each value on 1 to 256 neighbouring positions
- masked: int32 [64, 512], P('fsdp'), may hold values 0 or 1
- out_grad: bfloat16 [32768, 768], P('fsdp'), may hold values from -6 to 6
- att_master: float32 [18496, 128], P('fsdp'), may hold values from -3 to 3, as said below
- att_moment: float32 [18496, 128], P('fsdp'), as said below
- att_average: float32 [18496, 128], P('fsdp'), may hold values from -3 to 3, as said below
- ffn_master: float32 [36928, 128], P('fsdp'), may hold values from -1 to 2, as said below
- ffn_moment: float32 [36928, 128], P('fsdp'), as said below
- ffn_average: float32 [36928, 128], P('fsdp'), may hold values from -1 to 2, as said below
Outputs:
- block_output: bfloat16 [32768, 768], P('fsdp')
- input_grad: float32 [32768, 768], P('fsdp')
- att_master_new: float32 [18496, 128], P('fsdp')
- att_moment_new: float32 [18496, 128], P('fsdp')
- att_average_new: float32 [18496, 128], P('fsdp')
- att_master_low: bfloat16 [18496, 128], P('fsdp')
- ffn_master_new: float32 [36928, 128], P('fsdp')
- ffn_moment_new: float32 [36928, 128], P('fsdp')
- ffn_average_new: float32 [36928, 128], P('fsdp')
- ffn_master_low: bfloat16 [36928, 128], P('fsdp')
The draws below stay inside these ranges and needn't reach their ends.
Inputs may be any that keep to these rules, and one draw needn't show every extreme that they name: `att_master`: entries after the first 2363904 of the vector are zero. `att_average`: entries after the first 2363904 of the vector are zero. `att_moment`: entries after the first 2363904 of the vector are zero; the others have a spread of the order of the root of 32768. `ffn_master`: entries after the first 4723968 of the vector are zero. `ffn_average`: entries after the first 4723968 of the vector are zero. `ffn_moment`: entries after the first 4723968 of the vector are zero; the others have a spread of the order of the root of 32768.
All inputs are finite; a program needn't handle non-finite values. No bound on the sum of `masked` on one device may be relied on, other than what follows from the above.
Results may differ from the reference program's by a relative error of at most 0.012.
The reference program's roundings to bfloat16 on the way count: a program that leaves them out, or rounds other values in their place, can miss the bound.
Values may be sent and summed in bfloat16 or wider, within the bound.
No kernel may reach another device: no remote copies, remote signals or barrier semaphores. Data moves between devices by JAX's collectives and lax.ppermute only.
A program may use at most 192 MiB of HBM per device.

```python
import math
import jax
import jax.numpy as jnp
import numpy as np
from jax import lax

D = 768
HEADS = 12
HEAD_DIM = 64
FF = 3072
SEQ_LEN = 512
DOCS = 4
SEQ_DEV = 2
TOK_DEV = 1024
SEQUENCES = 64
TOKENS = 32768
ATT_ROWS = 18496
FFN_ROWS = 36928
N_FSDP = 32


def drawn_noise(key, length):
    return jax.random.truncated_normal(key, -3.0, 3.0, (length,), jnp.float32)


def layout(key, pieces, row_count, noise):
    blocks = []
    filled = 0
    for position in range(len(pieces)):
        length, center, spread = pieces[position]
        blocks.append(center + spread * noise(jax.random.fold_in(key, position), length))
        filled = filled + length
    blocks.append(jnp.zeros((row_count * 128 - filled,), jnp.float32))
    return jnp.concatenate(blocks).reshape(row_count, 128)


def att_weight_pieces():
    return [(3 * D * D, 0.0, D ** (-0.5)), (D * D, 0.0, (D // 32) ** (-0.5)), (D, 0.0, 0.2), (D, 0.0, 0.2), (D, 0.0, 0.2), (D, 1.0, 0.15), (D, 0.0, 0.2), (D, 0.0, 1.0)]


def ffn_weight_pieces():
    return [(D * FF, 0.0, D ** (-0.5)), (FF * D, 0.0, FF ** (-0.5)), (FF, 0.0, 0.2), (D, 0.0, 0.2), (D, 1.0, 0.15), (D, 0.0, 0.2)]


def att_moment_pieces():
    matrix_scale = 0.3 * TOKENS ** 0.5
    small_scale = 0.5 * TOKENS ** 0.5
    return [(4 * D * D, 0.0, matrix_scale), (6 * D, 0.0, small_scale)]


def ffn_moment_pieces():
    matrix_scale = 0.3 * TOKENS ** 0.5
    small_scale = 0.5 * TOKENS ** 0.5
    return [(2 * D * FF, 0.0, matrix_scale), (FF + 3 * D, 0.0, small_scale)]


def draw_att_master(key, part):
    folded = jax.random.fold_in(key, 11)
    return layout(folded, att_weight_pieces(), ATT_ROWS, drawn_noise)


def draw_att_average(key, part):
    folded = jax.random.fold_in(key, 12)
    return layout(folded, att_weight_pieces(), ATT_ROWS, drawn_noise)


def draw_att_moment(key, part):
    folded = jax.random.fold_in(key, 13)
    return layout(folded, att_moment_pieces(), ATT_ROWS, drawn_noise)


def draw_ffn_master(key, part):
    folded = jax.random.fold_in(key, 21)
    return layout(folded, ffn_weight_pieces(), FFN_ROWS, drawn_noise)


def draw_ffn_average(key, part):
    folded = jax.random.fold_in(key, 22)
    return layout(folded, ffn_weight_pieces(), FFN_ROWS, drawn_noise)


def draw_ffn_moment(key, part):
    folded = jax.random.fold_in(key, 23)
    return layout(folded, ffn_moment_pieces(), FFN_ROWS, drawn_noise)


def touch_ends(values, key, least, top_value):
    extent = values.shape
    index_at = [jax.random.randint(jax.random.fold_in(key, axis), (), 0, extent[axis]) for axis in range(len(extent))]
    values = values.at[tuple(index_at)].set(least)
    longest = extent.index(max(extent))
    index_at[longest] = (index_at[longest] + 1) % extent[longest]
    return values.at[tuple(index_at)].set(top_value)


def shard_levels(rng, shape, split, smallest, high):
    def one(axis_at, parts):
        steps = jax.random.uniform(jax.random.fold_in(jax.random.fold_in(rng, 6), axis_at), (parts,), jnp.float32, smallest / len(split), high / len(split))
        return jnp.repeat(jnp.exp(steps), shape[axis_at] // parts).reshape((-1,) + (1,) * (len(shape) - axis_at - 1))

    level = one(*split[0])
    for cut in split[1:]:
        level = level * one(*cut)
    return level


def length_profile(amount, total, most, slope):
    weights = [(1 << 20) // math.isqrt(standing ** slope) + 1 for standing in range(2, amount + 1)]
    rest, counts = total - most - (amount - 1), [1] * (amount - 1)
    while rest > 0:
        candidates = [i for i in range(amount - 1) if counts[i] < most]
        mass, remaining = sum([weights[i] for i in candidates]), rest
        for i in candidates:
            addition = min(most - counts[i], max(1, remaining * weights[i] // mass), rest)
            counts[i] = counts[i] + addition
            rest = rest - addition
    return np.array([most] + counts)


def ragged(key, number_of, total, most, lean):
    if number_of == 2:
        one = jax.random.randint(key, (), max(1, total - most), min(most, total - 1) + 1)
        return jnp.stack([one, total - one])
    lengths = jnp.asarray(length_profile(number_of, total, most, lean), jnp.int32)
    twos = (number_of - 1) // 2
    source_of, taker = lengths[1:1 + 2 * twos:2], lengths[2:2 + 2 * twos:2]
    room = jnp.minimum(source_of - 1, most - taker)
    moved = jax.random.randint(jax.random.fold_in(key, 1), (twos,), 0, 1 << 20) % (room + 1)
    lengths = lengths.at[1:1 + 2 * twos:2].set(source_of - moved).at[2:2 + 2 * twos:2].set(taker + moved)
    return lengths[jax.random.permutation(jax.random.fold_in(key, 2), number_of)]


def normal_values(rng, dims, scale, most, cuts=(), kind=jnp.bfloat16):
    values = jax.random.normal(rng, dims, jnp.float32) * scale
    if len(cuts) > 0:
        values = shard_levels(rng, dims, cuts, -0.22, 0.18) * values
    return jnp.clip(values, min=-most, max=most).astype(kind)


def setup_inputs(seed: int = 0) -> dict:
    key_of = jax.random.split(jax.random.key(seed), 11)
    block_input = normal_values(key_of[0], (TOKENS, D), 1.0, 6.0, ((0, 32),))
    seg_ids = jax.vmap(lambda own: jnp.searchsorted(jnp.cumsum(ragged(own, DOCS, SEQ_LEN, SEQ_LEN // 2, 2)), jnp.arange(SEQ_LEN), side="right"))(jax.random.split(key_of[1], SEQUENCES)).reshape((SEQUENCES, SEQ_LEN)).astype(jnp.int32)
    masked = touch_ends((jax.random.randint(key_of[2], (SEQUENCES, SEQ_LEN), 0, 100) < 15).astype(jnp.int32), jax.random.fold_in(key_of[2], 1), 0, 1)
    out_grad = normal_values(key_of[3], (TOKENS, D), 1.0, 6.0, ((0, 32),))
    att_master = draw_att_master(jax.random.fold_in(key_of[10], 71), 0)
    att_moment = draw_att_moment(jax.random.fold_in(key_of[10], 71), 0)
    att_average = draw_att_average(jax.random.fold_in(key_of[10], 71), 0)
    ffn_master = draw_ffn_master(jax.random.fold_in(key_of[10], 71), 0)
    ffn_moment = draw_ffn_moment(jax.random.fold_in(key_of[10], 71), 0)
    ffn_average = draw_ffn_average(jax.random.fold_in(key_of[10], 71), 0)
    return dict(block_input=block_input, seg_ids=seg_ids, masked=masked, out_grad=out_grad, att_master=att_master, att_moment=att_moment, att_average=att_average, ffn_master=ffn_master, ffn_moment=ffn_moment, ffn_average=ffn_average)


@jax.custom_vjp
def low(v):
    return lax.optimization_barrier(v.astype(jnp.bfloat16)).astype(jnp.float32)

@jax.custom_vjp
def low_back(v):
    return v

def low_keep(v):
    return (low(v), None)

def low_pass(kept, grad):
    return (grad,)

def back_keep(v):
    return (v, None)

def back_low(kept, grad):
    return (low(grad),)
low.defvjp(low_keep, low_pass)
low_back.defvjp(back_keep, back_low)
EPSILON = 1e-05
MASKED_SCORE = -1e+30
HIGHEST_PRECISION = lax.Precision.HIGHEST

def layer_norm(pre_norm, gain, shift):
    center = pre_norm - lax.optimization_barrier(jnp.mean(pre_norm, axis=-1, keepdims=True))
    spread = lax.optimization_barrier(jnp.mean(center * center, axis=-1, keepdims=True))
    return center * lax.rsqrt(spread + EPSILON) * gain + shift

def gelu_exact(inputs):
    return jax.nn.gelu(inputs, approximate=False)

def unpack_attention(flat_att, model_width):
    square = model_width * model_width
    att_mats = flat_att[:4 * square].reshape(4, model_width, model_width)
    small_params = flat_att[4 * square:4 * square + 6 * model_width].reshape(6, model_width)
    return (att_mats, small_params)

def unpack_ffn(flat_ffn, model_width, hidden):
    size_in = model_width * hidden
    weight_in = flat_ffn[:size_in].reshape(model_width, hidden)
    weight_out = flat_ffn[size_in:2 * size_in].reshape(hidden, model_width)
    offset = 2 * size_in
    bias_in = flat_ffn[offset:offset + hidden]
    small_params = flat_ffn[offset + hidden:offset + hidden + 3 * model_width].reshape(3, model_width)
    return (weight_in, weight_out, bias_in, small_params)

def attend(block_items):
    query_block, key_block, value_block, doc_block = block_items
    scores = low_back(jnp.einsum('qhd,khd->hqk', query_block, key_block, precision=HIGHEST_PRECISION))
    same_doc = doc_block[:, None] == doc_block[None, :]
    attn_probs = low(jax.nn.softmax(jnp.where(same_doc[None], scores, MASKED_SCORE), axis=-1))
    return jnp.einsum('hqk,khd->qhd', attn_probs, value_block, precision=HIGHEST_PRECISION)

def encoder_layer(flat_att, flat_ffn, x_input, doc_ids, mask_rows):
    att_mats, att_small = unpack_attention(flat_att, D)
    weight_in, weight_out, bias_in, ffn_small = unpack_ffn(flat_ffn, D, FF)
    stream_in = jnp.where(mask_rows[:, None] == 1, att_small[5][None, :], x_input)
    stream_low = low(stream_in)
    queries = low(low_back((jnp.dot(stream_low, att_mats[0], precision=HIGHEST_PRECISION) + att_small[0]) * 0.125))
    key_rows = low(low_back(jnp.dot(stream_low, att_mats[1], precision=HIGHEST_PRECISION)))
    values = low(low_back(jnp.dot(stream_low, att_mats[2], precision=HIGHEST_PRECISION) + att_small[1]))
    head_shape = (SEQ_DEV, SEQ_LEN, HEADS, HEAD_DIM)
    context = lax.map(jax.checkpoint(attend), (queries.reshape(head_shape), key_rows.reshape(head_shape), values.reshape(head_shape), doc_ids))
    context = low(low_back(context.reshape(TOK_DEV, D)))
    pre_one = stream_in + low_back(jnp.dot(context, att_mats[3], precision=HIGHEST_PRECISION) + att_small[2])
    normed_one = layer_norm(pre_one, att_small[3], att_small[4])
    hid_pre = low_back(jnp.dot(low(normed_one), weight_in, precision=HIGHEST_PRECISION) + bias_in)
    hid_act = low(gelu_exact(hid_pre))
    pre_two = normed_one + low_back(jnp.dot(hid_act, weight_out, precision=HIGHEST_PRECISION) + ffn_small[0])
    return layer_norm(pre_two, ffn_small[1], ffn_small[2])

def nesterov(master, moment, average, gradient, step_rate):
    moment_new = 0.5 * moment + gradient
    master_new = master - step_rate * (gradient + 0.5 * moment_new)
    average_new = 0.5 * average + 0.5 * master_new
    return (master_new, moment_new, average_new, master_new.astype(jnp.bfloat16))

def reference(block_input, seg_ids, masked, out_grad, att_master, att_moment, att_average, ffn_master, ffn_moment, ffn_average):
    flat_att = low(att_master.reshape(-1))
    flat_ffn = low(ffn_master.reshape(-1))
    x_groups = block_input.astype(jnp.float32).reshape(N_FSDP, TOK_DEV, D)
    doc_groups = seg_ids.reshape(N_FSDP, SEQ_DEV, SEQ_LEN)
    mask_groups = masked.reshape(N_FSDP, TOK_DEV)
    cot_groups = out_grad.astype(jnp.float32).reshape(N_FSDP, TOK_DEV, D)

    def group_step(running, group_items):
        att_total, ffn_total = running
        x_input, doc_ids, mask_rows, cotangent = group_items

        def local_layer(att_arg, ffn_arg, x_arg):
            return encoder_layer(att_arg, ffn_arg, x_arg, doc_ids, mask_rows)
        result, pull_back = jax.vjp(local_layer, flat_att, flat_ffn, x_input)
        grad_att, grad_ffn, grad_x = pull_back(cotangent)
        return ((att_total + grad_att, ffn_total + grad_ffn), (result, grad_x))
    initial = (jnp.zeros_like(flat_att), jnp.zeros_like(flat_ffn))
    totals, outputs = lax.scan(group_step, initial, (x_groups, doc_groups, mask_groups, cot_groups))
    att_grad = totals[0].reshape(ATT_ROWS, 128)
    ffn_grad = totals[1].reshape(FFN_ROWS, 128)
    block_output = outputs[0].reshape(TOKENS, D).astype(jnp.bfloat16)
    input_grad = outputs[1].reshape(TOKENS, D)
    step_rate = 0.05 / math.sqrt(TOKENS)
    att_new = nesterov(att_master, att_moment, att_average, att_grad, step_rate)
    ffn_new = nesterov(ffn_master, ffn_moment, ffn_average, ffn_grad, step_rate)
    return (block_output, input_grad, att_new[0], att_new[1], att_new[2], att_new[3], ffn_new[0], ffn_new[1], ffn_new[2], ffn_new[3])
```

```python
import functools
import math

import jax
import jax.numpy as jnp
from jax import lax
from jax.experimental import pallas as pl
from jax.experimental.pallas import tpu as pltpu
from jax.sharding import PartitionSpec as P

HEAD_DIM = 64
FF = 3072


EPSILON = 1e-05
MASKED_SCORE = -1e30


def layer_norm(pre_norm, gain, shift):
    center = pre_norm - jnp.mean(pre_norm, axis=-1, keepdims=True)
    spread = jnp.mean(center * center, axis=-1, keepdims=True)
    return center * lax.rsqrt(spread + EPSILON) * gain + shift


def gelu_exact(inputs):
    return jax.nn.gelu(inputs, approximate=False)


def unpack_attention(flat_att, model_width):
    square = model_width * model_width
    att_mats = flat_att[: 4 * square].reshape(4, model_width, model_width)
    small_params = flat_att[4 * square : 4 * square + 6 * model_width].reshape(6, model_width)
    return (att_mats, small_params)


def unpack_ffn(flat_ffn, model_width, hidden):
    size_in = model_width * hidden
    weight_in = flat_ffn[:size_in].reshape(model_width, hidden)
    weight_out = flat_ffn[size_in : 2 * size_in].reshape(hidden, model_width)
    offset = 2 * size_in
    bias_in = flat_ffn[offset : offset + hidden]
    small_params = flat_ffn[offset + hidden : offset + hidden + 3 * model_width].reshape(
        3, model_width
    )
    return (weight_in, weight_out, bias_in, small_params)


def pack_rows(pieces, row_count):
    filled = sum((piece.shape[0] for piece in pieces))
    padding = jnp.zeros((row_count * 128 - filled,), jnp.float32)
    return jnp.concatenate(list(pieces) + [padding]).reshape(row_count, 128)


def attend_forward(block_items):
    query_block, key_block, value_block, doc_block = block_items
    scores = jnp.einsum("qhd,khd->hqk", query_block, key_block, preferred_element_type=jnp.float32)
    same_doc = doc_block[:, None] == doc_block[None, :]
    scores = jnp.where(same_doc[None], scores, MASKED_SCORE)
    row_max = jnp.max(scores, axis=-1, keepdims=True)
    exponent = jnp.exp(scores - row_max)
    row_total = jnp.sum(exponent, axis=-1, keepdims=True)
    attn_probs = (exponent / row_total).astype(jnp.bfloat16)
    context = jnp.einsum(
        "hqk,khd->qhd", attn_probs, value_block, preferred_element_type=jnp.float32
    )
    return (context.astype(jnp.bfloat16), (row_max + jnp.log(row_total))[..., 0])


def attend_backward(block_items):
    query_block, key_block, value_block, doc_block, log_total, grad_context = block_items
    scores = jnp.einsum("qhd,khd->hqk", query_block, key_block, preferred_element_type=jnp.float32)
    same_doc = doc_block[:, None] == doc_block[None, :]
    scores = jnp.where(same_doc[None], scores, MASKED_SCORE)
    attn_probs = jnp.exp(scores - log_total[..., None])
    probs_low = attn_probs.astype(jnp.bfloat16)
    grad_probs = jnp.einsum(
        "qhd,khd->hqk", grad_context, value_block, preferred_element_type=jnp.float32
    )
    row_inner = jnp.sum(grad_probs * attn_probs, axis=-1, keepdims=True)
    grad_scores = (attn_probs * (grad_probs - row_inner)).astype(jnp.bfloat16)
    grad_query = jnp.einsum(
        "hqk,khd->qhd", grad_scores, key_block, preferred_element_type=jnp.float32
    ).astype(jnp.bfloat16)
    grad_key = jnp.einsum(
        "hqk,qhd->khd", grad_scores, query_block, preferred_element_type=jnp.float32
    ).astype(jnp.bfloat16)
    grad_value = jnp.einsum(
        "hqk,qhd->khd", probs_low, grad_context, preferred_element_type=jnp.float32
    ).astype(jnp.bfloat16)
    return (grad_query, grad_key, grad_value)


def nesterov(master, moment, average, gradient, step_rate):
    moment_new = 0.5 * moment + gradient
    master_new = master - step_rate * (gradient + 0.5 * moment_new)
    average_new = 0.5 * average + 0.5 * master_new
    return (master_new, moment_new, average_new, master_new.astype(jnp.bfloat16))


def local(
    block_input,
    seg_ids,
    masked,
    out_grad,
    att_master,
    att_moment,
    att_average,
    ffn_master,
    ffn_moment,
    ffn_average,
):
    tok_rows, model_width = block_input.shape
    seq_count, seq_length = seg_ids.shape
    head_count = model_width // HEAD_DIM
    devices = lax.axis_size("fsdp")
    att_rows = att_master.shape[0] * devices
    ffn_rows = ffn_master.shape[0] * devices
    head_shape = (seq_count, seq_length, head_count, HEAD_DIM)
    att_whole = lax.all_gather(att_master.astype(jnp.bfloat16), "fsdp", axis=0, tiled=True)
    att_mats, att_small_low = unpack_attention(att_whole.reshape(-1), model_width)
    att_small = att_small_low.astype(jnp.float32)
    masked_rows = masked.reshape(tok_rows, 1) == 1
    stream_in = jnp.where(masked_rows, att_small[5][None, :], block_input.astype(jnp.float32))
    stream_low = stream_in.astype(jnp.bfloat16)
    projected = jnp.einsum(
        "td,cde->cte", stream_low, att_mats[:3], preferred_element_type=jnp.float32
    )
    queries = ((projected[0] + att_small[0]) * 0.125).astype(jnp.bfloat16).reshape(head_shape)
    key_rows = projected[1].astype(jnp.bfloat16).reshape(head_shape)
    values = (projected[2] + att_small[1]).astype(jnp.bfloat16).reshape(head_shape)
    context, log_total = lax.map(attend_forward, (queries, key_rows, values, seg_ids))
    context_flat = context.reshape(tok_rows, model_width)
    pre_one = (
        stream_in
        + jnp.dot(context_flat, att_mats[3], preferred_element_type=jnp.float32)
        + att_small[2]
    )
    normed_one = layer_norm(pre_one, att_small[3], att_small[4])
    normed_low = normed_one.astype(jnp.bfloat16)
    ffn_whole = lax.all_gather(ffn_master.astype(jnp.bfloat16), "fsdp", axis=0, tiled=True)
    weight_in, weight_out, bias_in_low, ffn_small_low = unpack_ffn(
        ffn_whole.reshape(-1), model_width, FF
    )
    bias_in = bias_in_low.astype(jnp.float32)
    ffn_small = ffn_small_low.astype(jnp.float32)
    hid_pre = jnp.dot(normed_low, weight_in, preferred_element_type=jnp.float32) + bias_in
    hid_act = gelu_exact(hid_pre).astype(jnp.bfloat16)
    pre_two = (
        normed_one + jnp.dot(hid_act, weight_out, preferred_element_type=jnp.float32) + ffn_small[0]
    )
    normed_two, norm_two_pull = jax.vjp(layer_norm, pre_two, ffn_small[1], ffn_small[2])
    block_output = normed_two.astype(jnp.bfloat16)
    ffn_back = lax.all_gather(ffn_master.astype(jnp.bfloat16), "fsdp", axis=0, tiled=True)
    back_in, back_out, bias_unused, small_unused = unpack_ffn(ffn_back.reshape(-1), model_width, FF)
    grad_pre_two, grad_gain_two, grad_shift_two = norm_two_pull(out_grad.astype(jnp.float32))
    grad_branch_two = grad_pre_two.astype(jnp.bfloat16)
    grad_w_out = jnp.einsum(
        "tf,td->fd", hid_act, grad_branch_two, preferred_element_type=jnp.float32
    )
    grad_b_out = jnp.sum(grad_branch_two, axis=0, dtype=jnp.float32)
    grad_act = jnp.einsum(
        "td,fd->tf", grad_branch_two, back_out, preferred_element_type=jnp.float32
    )
    hid_unused, gelu_pull = jax.vjp(gelu_exact, hid_pre)
    grad_hidden = gelu_pull(grad_act)[0].astype(jnp.bfloat16)
    grad_w_in = jnp.einsum("td,tf->df", normed_low, grad_hidden, preferred_element_type=jnp.float32)
    grad_b_in = jnp.sum(grad_hidden, axis=0, dtype=jnp.float32)
    grad_normed_one = grad_pre_two + jnp.einsum(
        "tf,df->td", grad_hidden, back_in, preferred_element_type=jnp.float32
    )
    ffn_flat_grad = pack_rows(
        (
            grad_w_in.reshape(-1),
            grad_w_out.reshape(-1),
            grad_b_in,
            grad_b_out,
            grad_gain_two,
            grad_shift_two,
        ),
        ffn_rows,
    )
    ffn_grad = lax.psum_scatter(ffn_flat_grad, "fsdp", scatter_dimension=0, tiled=True)
    att_back = lax.all_gather(att_master.astype(jnp.bfloat16), "fsdp", axis=0, tiled=True)
    back_mats, small_back = unpack_attention(att_back.reshape(-1), model_width)
    pre_unused, norm_one_pull = jax.vjp(layer_norm, pre_one, att_small[3], att_small[4])
    grad_pre_one, grad_gain_one, grad_shift_one = norm_one_pull(grad_normed_one)
    grad_branch_one = grad_pre_one.astype(jnp.bfloat16)
    grad_w_o = jnp.einsum(
        "td,te->de", context_flat, grad_branch_one, preferred_element_type=jnp.float32
    )
    grad_b_o = jnp.sum(grad_branch_one, axis=0, dtype=jnp.float32)
    grad_context = jnp.einsum(
        "te,de->td", grad_branch_one, back_mats[3], preferred_element_type=jnp.float32
    ).astype(jnp.bfloat16)
    grad_q4, grad_k4, grad_v4 = lax.map(
        attend_backward,
        (queries, key_rows, values, seg_ids, log_total, grad_context.reshape(head_shape)),
    )
    grad_queries = grad_q4.reshape(tok_rows, model_width) * 0.125
    grad_keys = grad_k4.reshape(tok_rows, model_width)
    grad_values = grad_v4.reshape(tok_rows, model_width)
    grad_projected = jnp.stack([grad_queries, grad_keys, grad_values])
    grad_w_qkv = jnp.einsum(
        "td,cte->cde", stream_low, grad_projected, preferred_element_type=jnp.float32
    )
    grad_b_q = jnp.sum(grad_queries, axis=0, dtype=jnp.float32)
    grad_b_v = jnp.sum(grad_values, axis=0, dtype=jnp.float32)
    grad_stream = grad_pre_one + jnp.einsum(
        "cte,cde->td", grad_projected, back_mats[:3], preferred_element_type=jnp.float32
    )
    grad_mask_vector = jnp.sum(jnp.where(masked_rows, grad_stream, 0.0), axis=0)
    input_grad = jnp.where(masked_rows, 0.0, grad_stream)
    att_flat_grad = pack_rows(
        (
            grad_w_qkv.reshape(-1),
            grad_w_o.reshape(-1),
            grad_b_q,
            grad_b_v,
            grad_b_o,
            grad_gain_one,
            grad_shift_one,
            grad_mask_vector,
        ),
        att_rows,
    )
    att_grad = lax.psum_scatter(att_flat_grad, "fsdp", scatter_dimension=0, tiled=True)
    step_rate = 0.05 / math.sqrt(tok_rows * devices)
    att_new = nesterov(att_master, att_moment, att_average, att_grad, step_rate)
    ffn_new = nesterov(ffn_master, ffn_moment, ffn_average, ffn_grad, step_rate)
    return (
        block_output,
        input_grad,
        att_new[0],
        att_new[1],
        att_new[2],
        att_new[3],
        ffn_new[0],
        ffn_new[1],
        ffn_new[2],
        ffn_new[3],
    )


BF = jnp.bfloat16
F32 = jnp.float32
LANES = 128
SLOT = 96
TILE = 256
EXTRA = 16
MIB = 1 << 20


def params(limit):
    return pltpu.CompilerParams(vmem_limit_bytes=limit * MIB)


def spec_any():
    return pl.BlockSpec(memory_space=pl.ANY)


def spec_vmem():
    return pl.BlockSpec(memory_space=pltpu.VMEM)


def spec_whole(shape):
    return pl.BlockSpec(shape, lambda *ids: (0,) * len(shape))


def dot_nn(left, right):
    return lax.dot_general(left, right, (((1,), (0,)), ((), ())), preferred_element_type=F32)


def dot_nt(left, right):
    return lax.dot_general(left, right, (((1,), (1,)), ((), ())), preferred_element_type=F32)


def dot_tn(left, right):
    return lax.dot_general(left, right, (((0,), (0,)), ((), ())), preferred_element_type=F32)


def slot_of(chunk, me):
    diff = lax.bitwise_xor(me, chunk)
    far_core = lax.bitwise_and(diff, 1)
    x_bit = lax.bitwise_and(lax.shift_right_logical(diff, 1), 1)
    y_bit = lax.bitwise_and(lax.shift_right_logical(diff, 2), 1)
    z_low = lax.bitwise_and(lax.shift_right_logical(diff, 3), 1)
    z_high = lax.shift_right_logical(diff, 4)
    core = lax.bitwise_xor(lax.bitwise_and(me, 1), far_core)
    third = x_bit + core * (y_bit - x_bit)
    fourth = y_bit + core * (x_bit - y_bit)
    return far_core, z_high + 2 * z_low + 4 * third + 8 * fourth


def stage_perm(stage):
    if stage == 0:
        return [(i, i ^ 16) for i in range(32)]
    if stage == 1:
        return [(i, i ^ 8) for i in range(32)]
    if stage == 2:
        return [(i, i ^ (4 if i & 1 else 2)) for i in range(32)]
    if stage == 3:
        return [(i, i ^ (2 if i & 1 else 4)) for i in range(32)]
    return [(i, i ^ 1) for i in range(32)]


def exchange(array, stage):
    return lax.ppermute(array, "fsdp", stage_perm(stage))


def gather_chunks(chunk, small=None):
    held = chunk
    for stage in range(4):
        rows = held.shape[0]
        sent = held if small is None else jnp.concatenate([held, small])
        got = exchange(sent, stage)
        held = jnp.concatenate([held, got[:rows]])
        if small is not None:
            small = small + got[rows:]
    if small is not None:
        held = jnp.concatenate([held, small])
    return held, exchange(held, 4)


def scatter_chunks(sent, kept, small=None):
    rows = 16 * SLOT
    got = exchange(sent, 4)
    for stage in (3, 2, 1, 0):
        half = rows // 2
        total_high = kept[half:].astype(F32) + got[half:rows].astype(F32)
        kept = kept[:half].astype(F32) + got[:half].astype(F32)
        high = total_high.astype(BF)
        if small is not None:
            small = small + got[rows:].astype(F32)
            high = jnp.concatenate([high, small.astype(BF)])
        if stage > 0:
            kept = kept.astype(BF)
        got = exchange(high, stage)
        rows = half
    total = kept.astype(F32) + got[:rows].astype(F32)
    if small is not None:
        return total, small + got[rows:].astype(F32)
    return total


def prep_kernel(last, att_mats, ffn_mats, att_ref, ffn_ref, tail_ref, att_out, small_out, ffn_a, ffn_b, att_buf, ffn_buf):
    me = lax.axis_index("fsdp")
    att_rows = att_ref.shape[0]
    ffn_rows = ffn_ref.shape[0]
    att_buf[0:64, :] = tail_ref[0:64, :]
    att_buf[64 : 64 + att_rows, :] = att_ref[...]
    ffn_buf[0:64, :] = tail_ref[64:128, :]
    ffn_buf[64 : 64 + ffn_rows, :] = ffn_ref[...]
    start = 64 - 2 * me
    for part in range(6):
        cols = slice(part * LANES, (part + 1) * LANES)
        att_out[:, cols] = att_buf[pl.ds(start + part, SLOT, stride=6), :].astype(BF)
    first = me < 16

    @pl.when(first)
    def _():
        for block in range(4):
            out = ffn_a if block < 2 else ffn_b
            rows = slice((block % 2) * 48, (block % 2) * 48 + 48)
            for part in range(6):
                cols = slice(part * LANES, (part + 1) * LANES)
                piece = ffn_buf[pl.ds(start + 6 * block + part, 48, stride=24), :]
                out[rows, cols] = piece.astype(BF)

    @pl.when(jnp.logical_not(first))
    def _():
        for part in range(6):
            cols = slice(part * LANES, (part + 1) * LANES)
            ffn_a[:, cols] = ffn_buf[pl.ds(start + part, SLOT, stride=6), :].astype(BF)
            ffn_b[:, cols] = ffn_buf[pl.ds(start + 6 * SLOT + part, SLOT, stride=6), :].astype(BF)

    small_out[...] = jnp.zeros_like(small_out)

    @pl.when(me == last)
    def _():
        att_at = 64 + att_mats - last * att_rows
        ffn_at = 64 + ffn_mats - last * ffn_rows
        for part in range(6):
            cols = slice(part * LANES, (part + 1) * LANES)
            upper = att_buf[pl.ds(att_at + part, 6, stride=6), :]
            lower = ffn_buf[pl.ds(ffn_at + part, 7, stride=6), :]
            both = jnp.concatenate([upper, lower, jnp.zeros((3, LANES), F32)])
            small_out[:, cols] = both.astype(BF)


def prepare(att_master, ffn_master, tails, devices, width):
    att_mats = 4 * width * width // LANES
    ffn_mats = 2 * width * FF // LANES
    att_rows, ffn_rows = att_master.shape[0], ffn_master.shape[0]
    body = functools.partial(prep_kernel, devices - 1, att_mats, ffn_mats)
    return pl.pallas_call(
        body,
        out_shape=(
            jax.ShapeDtypeStruct((SLOT, width), BF),
            jax.ShapeDtypeStruct((EXTRA, width), BF),
            jax.ShapeDtypeStruct((SLOT, width), BF),
            jax.ShapeDtypeStruct((SLOT, width), BF),
        ),
        in_specs=[spec_vmem()] * 3,
        out_specs=(spec_vmem(),) * 4,
        scratch_shapes=[
            pltpu.VMEM((64 + att_rows + 6, LANES), F32),
            pltpu.VMEM((64 + ffn_rows + 6, LANES), F32),
        ],
        compiler_params=params(16),
        name="prep",
    )(att_master, ffn_master, tails)


def start_copy(lo, hi, far_core, src_rows, dst, sem):
    @pl.when(far_core == 0)
    def _():
        pltpu.make_async_copy(lo.at[src_rows, :], dst, sem).start()

    @pl.when(far_core == 1)
    def _():
        pltpu.make_async_copy(hi.at[src_rows, :], dst, sem).start()


def load_att(lo, hi, dst, sem, first, last):
    me = lax.axis_index("fsdp")

    def body(chunk, carry):
        far_core, slot = slot_of(chunk, me)
        src = pl.ds(pl.multiple_of(slot * SLOT, 32), SLOT)
        at = pl.multiple_of((chunk - first) * SLOT, 32)
        start_copy(lo, hi, far_core, src, dst.at[pl.ds(at, SLOT), :], sem)
        return carry

    lax.fori_loop(first, last, body, 0)


def load_ffn(units, w_in, w_out, sem_in, sem_out):
    me = lax.axis_index("fsdp")

    def body_in(chunk, carry):
        far_core, slot = slot_of(chunk, me)
        at = pl.multiple_of(chunk * 48, 16)
        for unit in range(2):
            lo, hi = units[unit]
            for part in range(2):
                src = pl.ds(pl.multiple_of(slot * SLOT + part * 48, 16), 48)
                dst = w_in.at[2 * unit + part, pl.ds(at, 48), :]
                start_copy(lo, hi, far_core, src, dst, sem_in)
        return carry

    def body_out(chunk, carry):
        far_core, slot = slot_of(chunk, me)
        for unit in range(2):
            lo, hi = units[unit]
            src = pl.ds(pl.multiple_of(slot * SLOT, 32), SLOT)
            at = pl.multiple_of((chunk - 16) * 192 + unit * SLOT, 32)
            start_copy(lo, hi, far_core, src, w_out.at[pl.ds(at, SLOT), :], sem_out)
        return carry

    lax.fori_loop(0, 16, body_in, 0)
    lax.fori_loop(16, 32, body_out, 0)


def wait_whole(ref, sem):
    pltpu.make_async_copy(ref, ref, sem).wait()


def head_mask(rows):
    lane = lax.broadcasted_iota(jnp.int32, (rows, LANES), 1)
    return lane < HEAD_DIM


def forward_kernel(
    x_ref,
    masked_ref,
    seg_col_ref,
    seg_row_ref,
    lo_ref,
    hi_ref,
    stream_ref,
    q_ref,
    k_ref,
    v_ref,
    ctx_ref,
    lse_ref,
    pre_ref,
    small_ref,
    weights,
    small_lo,
    small_hi,
    sem,
    small_sem,
):
    width = x_ref.shape[1]
    seq = x_ref.shape[0]

    @pl.when(pl.program_id(0) == 0)
    def _():
        load_att(lo_ref, hi_ref, weights, sem, 0, 32)
        one = pltpu.make_async_copy(lo_ref.at[pl.ds(16 * SLOT, EXTRA), :], small_lo, small_sem.at[0])
        two = pltpu.make_async_copy(hi_ref.at[pl.ds(16 * SLOT, EXTRA), :], small_hi, small_sem.at[1])
        one.start()
        two.start()
        one.wait()
        two.wait()
        small_ref[...] = small_lo[...].astype(F32) + small_hi[...].astype(F32)
        wait_whole(weights, sem)

    small = small_ref[...]
    stream = jnp.where(masked_ref[...] == 1, small[5:6], x_ref[...].astype(F32)).astype(BF)
    stream_ref[...] = stream
    q_ref[...] = ((dot_nn(stream, weights[0:width]) + small[0:1]) * 0.125).astype(BF)
    k_ref[...] = dot_nn(stream, weights[width : 2 * width]).astype(BF)
    v_ref[...] = (dot_nn(stream, weights[2 * width : 3 * width]) + small[1:2]).astype(BF)
    left = head_mask(seq)
    same = seg_col_ref[...] == seg_row_ref[0]

    def pair(index, carry):
        cols = pl.ds(pl.multiple_of(index * LANES, LANES), LANES)
        queries = q_ref[:, cols]
        keys = k_ref[:, cols]
        values_t = v_ref[:, cols].T
        outs = []
        for head in range(2):
            keep = left if head == 0 else jnp.logical_not(left)
            own = jnp.where(keep, queries, jnp.zeros_like(queries))
            scores = jnp.where(same, dot_nt(keys, own), MASKED_SCORE)
            top = jnp.max(scores, axis=0, keepdims=True)
            exponent = jnp.exp(scores - top)
            total = jnp.sum(exponent, axis=0, keepdims=True)
            probs = (exponent * (1.0 / total)).astype(BF)
            lse_ref[0, pl.ds(2 * index + head, 1), :] = top + jnp.log(total)
            outs.append(dot_nn(values_t[head * HEAD_DIM : (head + 1) * HEAD_DIM], probs))
        ctx_ref[:, cols] = jnp.concatenate(outs).T.astype(BF)
        return carry

    lax.fori_loop(0, width // LANES, pair, 0)
    out = dot_nn(ctx_ref[...], weights[3 * width :])
    pre_ref[...] = stream_ref[...].astype(F32) + out + small[2:3]


def attention_forward(block_input, masked_col, seg_col, seg_row, lo, hi):
    tok, width = block_input.shape
    seq_count, seq = seg_row.shape[0], seg_row.shape[2]
    heads = width // HEAD_DIM
    tile = lambda: pl.BlockSpec((seq, width), lambda s: (s, 0))
    col = lambda: pl.BlockSpec((seq, 1), lambda s: (s, 0))
    bf = jax.ShapeDtypeStruct((tok, width), BF)
    return pl.pallas_call(
        forward_kernel,
        grid=(seq_count,),
        out_shape=(
            bf,
            bf,
            bf,
            bf,
            bf,
            jax.ShapeDtypeStruct((seq_count, 16, seq), F32),
            jax.ShapeDtypeStruct((tok, width), F32),
            jax.ShapeDtypeStruct((EXTRA, width), F32),
        ),
        in_specs=[
            tile(),
            col(),
            col(),
            pl.BlockSpec((1, 1, seq), lambda s: (s, 0, 0)),
            spec_any(),
            spec_any(),
        ],
        out_specs=(
            tile(),
            tile(),
            tile(),
            tile(),
            tile(),
            pl.BlockSpec((1, 16, seq), lambda s: (s, 0, 0)),
            tile(),
            spec_whole((EXTRA, width)),
        ),
        scratch_shapes=[
            pltpu.VMEM((4 * width, width), BF),
            pltpu.VMEM((EXTRA, width), BF),
            pltpu.VMEM((EXTRA, width), BF),
            pltpu.SemaphoreType.DMA,
            pltpu.SemaphoreType.DMA((2,)),
        ],
        compiler_params=params(40),
        cost_estimate=pl.CostEstimate(
            flops=2 * tok * width * width * 4 + 4 * tok * seq * width,
            bytes_accessed=40 * MIB,
            transcendentals=tok * seq * heads,
        ),
        name="attention_forward",
    )(block_input, masked_col, seg_col, seg_row, lo, hi)


def norm_stats(pre_norm):
    center = pre_norm - jnp.mean(pre_norm, axis=-1, keepdims=True)
    scale = lax.rsqrt(jnp.mean(center * center, axis=-1, keepdims=True) + EPSILON)
    return center * scale, scale


def norm_back(grad, gain, normed, scale):
    scaled = grad * gain
    mean_one = jnp.mean(scaled, axis=-1, keepdims=True)
    mean_two = jnp.mean(scaled * normed, axis=-1, keepdims=True)
    return scale * (scaled - mean_one - normed * mean_two)


def column_sum(array):
    return jnp.sum(array, axis=0, keepdims=True)


def gelu_pair(inputs):
    phi_cdf = 0.5 + 0.5 * lax.erf(inputs * math.sqrt(0.5))
    density = jnp.exp(inputs * inputs * -0.5) * (1.0 / math.sqrt(2.0 * math.pi))
    return inputs * phi_cdf, phi_cdf + inputs * density


def ffn_kernel(
    pre_ref,
    grad_ref,
    small_ref,
    att_lo,
    att_hi,
    lo_a,
    hi_a,
    lo_b,
    hi_b,
    y_ref,
    x1_ref,
    hid_ref,
    dhid_ref,
    dfb_ref,
    dpre_ref,
    dob_ref,
    dctx_ref,
    sums_ref,
    w_in,
    w_out,
    w_o,
    slope,
    sem_in,
    sem_out,
    sem_o,
):
    width = pre_ref.shape[1]
    blocks = FF // width
    step = pl.program_id(0)

    @pl.when(step == 0)
    def _():
        load_ffn(((lo_a, hi_a), (lo_b, hi_b)), w_in, w_out, sem_in, sem_out)
        load_att(att_lo, att_hi, w_o, sem_o, 24, 32)
        sums_ref[...] = jnp.zeros_like(sums_ref)

    small = small_ref[...]
    normed_one, scale_one = norm_stats(pre_ref[...])
    x_one = normed_one * small[3:4] + small[4:5]
    x_low = x_one.astype(BF)
    x1_ref[...] = x_low

    @pl.when(step == 0)
    def _():
        wait_whole(w_in, sem_in)
        wait_whole(w_out, sem_out)
        wait_whole(w_o, sem_o)

    total = x_one + small[10:11]
    for block in range(blocks):
        cols = slice(block * width, (block + 1) * width)
        hidden, gate = gelu_pair(dot_nn(x_low, w_in[block]) + small[6 + block : 7 + block])
        hidden = hidden.astype(BF)
        hid_ref[:, cols] = hidden
        slope[block] = gate
        total = total + dot_nn(hidden, w_out[cols, :])
    normed_two, scale_two = norm_stats(total)
    y_ref[...] = (normed_two * small[11:12] + small[12:13]).astype(BF)
    grad_out = grad_ref[...].astype(F32)
    grad_two = norm_back(grad_out, small[11:12], normed_two, scale_two)
    grad_low = grad_two.astype(BF)
    dfb_ref[...] = grad_low
    sums_ref[10:11] += column_sum(grad_low.astype(F32))
    sums_ref[11:12] += column_sum(grad_out * normed_two)
    sums_ref[12:13] += column_sum(grad_out)
    grad_one = grad_two
    for block in range(blocks):
        cols = slice(block * width, (block + 1) * width)
        dhid = (dot_nt(grad_low, w_out[cols, :]) * slope[block]).astype(BF)
        dhid_ref[:, cols] = dhid
        sums_ref[6 + block : 7 + block] += column_sum(dhid.astype(F32))
        grad_one = grad_one + dot_nt(dhid, w_in[block])
    sums_ref[3:4] += column_sum(grad_one * normed_one)
    sums_ref[4:5] += column_sum(grad_one)
    grad_pre = norm_back(grad_one, small[3:4], normed_one, scale_one)
    dpre_ref[...] = grad_pre
    dob = grad_pre.astype(BF)
    dob_ref[...] = dob
    sums_ref[2:3] += column_sum(dob.astype(F32))
    dctx_ref[...] = dot_nt(dob, w_o[...]).astype(BF)


def feed_forward(pre_one, out_grad, small, att, unit_a, unit_b):
    tok, width = pre_one.shape
    tile = lambda cols: pl.BlockSpec((TILE, cols), lambda i: (i, 0))
    bf = lambda cols: jax.ShapeDtypeStruct((tok, cols), BF)
    return pl.pallas_call(
        ffn_kernel,
        grid=(tok // TILE,),
        out_shape=(
            bf(width),
            bf(width),
            bf(FF),
            bf(FF),
            bf(width),
            jax.ShapeDtypeStruct((tok, width), F32),
            bf(width),
            bf(width),
            jax.ShapeDtypeStruct((EXTRA, width), F32),
        ),
        in_specs=[tile(width), tile(width), spec_whole((EXTRA, width))] + [spec_any()] * 6,
        out_specs=(
            tile(width),
            tile(width),
            tile(FF),
            tile(FF),
            tile(width),
            tile(width),
            tile(width),
            tile(width),
            spec_whole((EXTRA, width)),
        ),
        scratch_shapes=[
            pltpu.VMEM((FF // width, width, width), BF),
            pltpu.VMEM((FF, width), BF),
            pltpu.VMEM((width, width), BF),
            pltpu.VMEM((FF // width, TILE, width), F32),
            pltpu.SemaphoreType.DMA,
            pltpu.SemaphoreType.DMA,
            pltpu.SemaphoreType.DMA,
        ],
        compiler_params=params(48),
        cost_estimate=pl.CostEstimate(
            flops=8 * tok * width * FF, bytes_accessed=40 * MIB, transcendentals=2 * tok * FF
        ),
        name="feed_forward",
    )(pre_one, out_grad, small, *att, *unit_a, *unit_b)


def put_slot(sent, kept, far_core, row, value):
    rows = value.shape[0]
    at = pl.ds(pl.multiple_of(row, 16), rows)

    @pl.when(far_core == 1)
    def _():
        sent[at, :] = value

    @pl.when(far_core == 0)
    def _():
        kept[at, :] = value


def ffn_grad_kernel(x_ref, hid_ref, dhid_ref, dfb_ref, sent_a, kept_a, sent_b, kept_b):
    width = x_ref.shape[1]
    me = lax.axis_index("fsdp")
    step = pl.program_id(0)
    units = ((sent_a, kept_a), (sent_b, kept_b))

    @pl.when(step < 4)
    def _():
        product = dot_tn(hid_ref[...], dfb_ref[...]).astype(BF)
        for piece in range(8):
            chunk = 16 + 4 * step + piece // 2
            far_core, slot = slot_of(chunk, me)
            sent, kept = units[piece % 2]
            put_slot(sent, kept, far_core, slot * SLOT, product[piece * SLOT : (piece + 1) * SLOT])

    for block in range(4):

        @pl.when(step == 4 + block)
        def _():
            product = dot_tn(x_ref[...], dhid_ref[...]).astype(BF)
            sent, kept = units[block // 2]
            for chunk in range(16):
                far_core, slot = slot_of(chunk, me)
                row = slot * SLOT + (block % 2) * 48
                put_slot(sent, kept, far_core, row, product[chunk * 48 : (chunk + 1) * 48])


def ffn_grads(x_low, hidden, dhid, dfb):
    tok, width = x_low.shape
    out = jax.ShapeDtypeStruct((16 * SLOT, width), BF)
    return pl.pallas_call(
        ffn_grad_kernel,
        grid=(8,),
        out_shape=(out,) * 4,
        in_specs=[
            spec_whole((tok, width)),
            pl.BlockSpec((tok, width), lambda i: (0, jnp.minimum(i, 3))),
            pl.BlockSpec((tok, width), lambda i: (0, jnp.maximum(i - 4, 0))),
            spec_whole((tok, width)),
        ],
        out_specs=(spec_whole((16 * SLOT, width)),) * 4,
        compiler_params=params(48),
        cost_estimate=pl.CostEstimate(
            flops=4 * tok * width * FF, bytes_accessed=30 * MIB, transcendentals=0
        ),
        name="ffn_grads",
    )(x_low, hidden, dhid, dfb)


def backward_kernel(q_ref, k_ref, v_ref, dctx_ref, lse_ref, seg_col_ref, seg_row_ref, dq_ref, dk_ref, dv_ref):
    seq, width = q_ref.shape
    left = head_mask(seq)
    same = seg_col_ref[...] == seg_row_ref[0]

    def pair(index, carry):
        cols = pl.ds(pl.multiple_of(index * LANES, LANES), LANES)
        queries = q_ref[:, cols]
        keys = k_ref[:, cols]
        values = v_ref[:, cols]
        grads = dctx_ref[:, cols]
        keys_t = keys.T
        grad_q = []
        grad_k = jnp.zeros((seq, LANES), F32)
        grad_v = jnp.zeros((seq, LANES), F32)
        for head in range(2):
            keep = left if head == 0 else jnp.logical_not(left)
            own = jnp.where(keep, queries, jnp.zeros_like(queries))
            own_grad = jnp.where(keep, grads, jnp.zeros_like(grads))
            log_total = lse_ref[0, pl.ds(2 * index + head, 1), :]
            scores = jnp.where(same, dot_nt(keys, own), MASKED_SCORE)
            probs = jnp.exp(scores - log_total)
            grad_probs = dot_nt(values, own_grad)
            inner = jnp.sum(grad_probs * probs, axis=0, keepdims=True)
            grad_scores = (probs * (grad_probs - inner)).astype(BF)
            grad_v = grad_v + dot_nn(probs.astype(BF), own_grad)
            grad_k = grad_k + dot_nn(grad_scores, own)
            grad_q.append(dot_nn(keys_t[head * HEAD_DIM : (head + 1) * HEAD_DIM], grad_scores))
        dq_ref[:, cols] = (jnp.concatenate(grad_q).T.astype(BF) * 0.125).astype(BF)
        dk_ref[:, cols] = grad_k.astype(BF)
        dv_ref[:, cols] = grad_v.astype(BF)
        return carry

    lax.fori_loop(0, width // LANES, pair, 0)


def attention_backward(q, k, v, dctx, lse, seg_col, seg_row):
    tok, width = q.shape
    seq_count, seq = seg_row.shape[0], seg_row.shape[2]
    heads = width // HEAD_DIM
    tile = lambda: pl.BlockSpec((seq, width), lambda s: (s, 0))
    return pl.pallas_call(
        backward_kernel,
        grid=(seq_count,),
        out_shape=(jax.ShapeDtypeStruct((tok, width), BF),) * 3,
        in_specs=[
            tile(),
            tile(),
            tile(),
            tile(),
            pl.BlockSpec((1, 16, seq), lambda s: (s, 0, 0)),
            pl.BlockSpec((seq, 1), lambda s: (s, 0)),
            pl.BlockSpec((1, 1, seq), lambda s: (s, 0, 0)),
        ],
        out_specs=(tile(), tile(), tile()),
        compiler_params=params(40),
        cost_estimate=pl.CostEstimate(
            flops=10 * tok * seq * width,
            bytes_accessed=12 * MIB,
            transcendentals=tok * seq * heads,
        ),
        name="attention_backward",
    )(q, k, v, dctx, lse, seg_col, seg_row)


def att_grad_kernel(
    stream_ref,
    dq_ref,
    dk_ref,
    dv_ref,
    ctx_ref,
    dob_ref,
    dpre_ref,
    masked_ref,
    sums_ref,
    lo_ref,
    hi_ref,
    sent_ref,
    kept_ref,
    small_ref,
    dx_ref,
    weights,
    sem,
):
    tok, width = stream_ref.shape
    me = lax.axis_index("fsdp")
    load_att(lo_ref, hi_ref, weights, sem, 0, 24)
    for matrix in range(4):
        source = (dq_ref, dk_ref, dv_ref, dob_ref)[matrix]
        inputs = ctx_ref if matrix == 3 else stream_ref
        product = dot_tn(inputs[...], source[...]).astype(BF)
        for piece in range(8):
            far_core, slot = slot_of(8 * matrix + piece, me)
            put_slot(
                sent_ref, kept_ref, far_core, slot * SLOT, product[piece * SLOT : (piece + 1) * SLOT]
            )
    wait_whole(weights, sem)
    small_ref[...] = sums_ref[...]

    def tile(index, carry):
        rows = pl.ds(pl.multiple_of(index * TILE, TILE), TILE)
        dq = dq_ref[rows, :]
        dv = dv_ref[rows, :]
        grad = dpre_ref[rows, :] + dot_nt(dq, weights[0:width])
        grad = grad + dot_nt(dk_ref[rows, :], weights[width : 2 * width])
        grad = grad + dot_nt(dv, weights[2 * width : 3 * width])
        chosen = masked_ref[rows, :] == 1
        dx_ref[rows, :] = jnp.where(chosen, 0.0, grad)
        small_ref[0:1] += column_sum(dq.astype(F32))
        small_ref[1:2] += column_sum(dv.astype(F32))
        small_ref[5:6] += column_sum(jnp.where(chosen, grad, 0.0))
        return carry

    lax.fori_loop(0, tok // TILE, tile, 0)
    sent_ref[pl.ds(16 * SLOT, EXTRA), :] = small_ref[...].astype(BF)


def att_grads(stream, dq, dk, dv, ctx, dob, dpre, masked_col, sums, lo, hi):
    tok, width = stream.shape
    return pl.pallas_call(
        att_grad_kernel,
        out_shape=(
            jax.ShapeDtypeStruct((16 * SLOT + EXTRA, width), BF),
            jax.ShapeDtypeStruct((16 * SLOT, width), BF),
            jax.ShapeDtypeStruct((EXTRA, width), F32),
            jax.ShapeDtypeStruct((tok, width), F32),
        ),
        in_specs=[spec_vmem()] * 9 + [spec_any()] * 2,
        out_specs=(spec_vmem(),) * 4,
        scratch_shapes=[pltpu.VMEM((3 * width, width), BF), pltpu.SemaphoreType.DMA],
        compiler_params=params(48),
        cost_estimate=pl.CostEstimate(
            flops=14 * tok * width * width, bytes_accessed=30 * MIB, transcendentals=0
        ),
        name="att_grads",
    )(stream, dq, dk, dv, ctx, dob, dpre, masked_col, sums, lo, hi)


def flat_att_kernel(grad_ref, out_ref):
    for part in range(6):
        out_ref[pl.ds(part, SLOT, stride=6), :] = grad_ref[:, part * LANES : (part + 1) * LANES]


def flat_ffn_kernel(a_ref, b_ref, out_ref):
    first = lax.axis_index("fsdp") < 16

    @pl.when(first)
    def _():
        for block in range(4):
            source = a_ref if block < 2 else b_ref
            rows = slice((block % 2) * 48, (block % 2) * 48 + 48)
            for part in range(6):
                cols = slice(part * LANES, (part + 1) * LANES)
                out_ref[pl.ds(6 * block + part, 48, stride=24), :] = source[rows, cols]

    @pl.when(jnp.logical_not(first))
    def _():
        for part in range(6):
            cols = slice(part * LANES, (part + 1) * LANES)
            out_ref[pl.ds(part, SLOT, stride=6), :] = a_ref[:, cols]
            out_ref[pl.ds(6 * SLOT + part, SLOT, stride=6), :] = b_ref[:, cols]


def flatten(kernel, rows, *pieces):
    return pl.pallas_call(
        kernel,
        out_shape=jax.ShapeDtypeStruct((rows, LANES), F32),
        in_specs=[spec_vmem()] * len(pieces),
        out_specs=spec_vmem(),
        compiler_params=params(16),
        name="flatten",
    )(*pieces)


def update_kernel(last, small_at, rate, flat_ref, head_ref, small_ref, w_ref, m_ref, a_ref, w_out, m_out, a_out, low_out, buf):
    me = lax.axis_index("fsdp")
    aligned = flat_ref.shape[0]
    own = w_ref.shape[0]
    count = small_at[1]
    buf[0:aligned, :] = flat_ref[...]
    buf[aligned : aligned + 64, :] = head_ref[...]

    @pl.when(me == last)
    def _():
        buf[aligned : aligned + 64, :] = jnp.zeros((64, LANES), F32)
        for part in range(6):
            cols = slice(part * LANES, (part + 1) * LANES)
            buf[pl.ds(aligned + part, count, stride=6), :] = small_ref[
                small_at[0] : small_at[0] + count, cols
            ]

    grad = buf[pl.ds(2 * me, own), :]
    moment = 0.5 * m_ref[...] + grad
    master = w_ref[...] - rate * (grad + 0.5 * moment)
    m_out[...] = moment
    w_out[...] = master
    a_out[...] = 0.5 * a_ref[...] + 0.5 * master
    low_out[...] = master.astype(BF)


def update(flat, head, small, small_at, rate, devices, master, moment, average):
    own = master.shape[0]
    f32 = jax.ShapeDtypeStruct((own, LANES), F32)
    body = functools.partial(update_kernel, devices - 1, small_at, rate)
    return pl.pallas_call(
        body,
        out_shape=(f32, f32, f32, jax.ShapeDtypeStruct((own, LANES), BF)),
        in_specs=[spec_vmem()] * 6,
        out_specs=(spec_vmem(),) * 4,
        scratch_shapes=[pltpu.VMEM((flat.shape[0] + 64, LANES), F32)],
        compiler_params=params(16),
        name="update",
    )(flat, head, small, master, moment, average)


def local_exchange(
    block_input,
    seg_ids,
    masked,
    out_grad,
    att_master,
    att_moment,
    att_average,
    ffn_master,
    ffn_moment,
    ffn_average,
):
    tok, width = block_input.shape
    seq_count, seq = seg_ids.shape
    devices = lax.axis_size("fsdp")
    up = [(i, i + 1) for i in range(devices - 1)]
    down = [(i + 1, i) for i in range(devices - 1)]
    tails = lax.ppermute(jnp.concatenate([att_master[-64:], ffn_master[-64:]]), "fsdp", up)
    masked_col = masked.reshape(tok, 1)
    seg_col = seg_ids.reshape(tok, 1)
    seg_row = seg_ids.reshape(seq_count, 1, seq)
    att_chunk, small_chunk, chunk_a, chunk_b = prepare(att_master, ffn_master, tails, devices, width)
    att = gather_chunks(att_chunk, small_chunk)
    unit_a = gather_chunks(chunk_a)
    unit_b = gather_chunks(chunk_b)
    stream, q, k, v, ctx, lse, pre_one, small = attention_forward(
        block_input, masked_col, seg_col, seg_row, *att
    )
    block_output, x_low, hidden, dhid, dfb, dpre, dob, dctx, sums = feed_forward(
        pre_one, out_grad, small, att, unit_a, unit_b
    )
    sent_a, kept_a, sent_b, kept_b = ffn_grads(x_low, hidden, dhid, dfb)
    grad_a = scatter_chunks(sent_a, kept_a)
    grad_b = scatter_chunks(sent_b, kept_b)
    dq, dk, dv = attention_backward(q, k, v, dctx, lse, seg_col, seg_row)
    sent, kept, small_grads, input_grad = att_grads(
        stream, dq, dk, dv, ctx, dob, dpre, masked_col, sums, *att
    )
    grad_att, small_total = scatter_chunks(sent, kept, small_grads)
    rate = 0.05 / math.sqrt(tok * devices)
    ffn_flat = flatten(flat_ffn_kernel, 12 * SLOT, grad_a, grad_b)
    ffn_head = lax.ppermute(ffn_flat[:64], "fsdp", down)
    att_flat = flatten(flat_att_kernel, 6 * SLOT, grad_att)
    att_head = lax.ppermute(att_flat[:64], "fsdp", down)
    ffn_new = update(
        ffn_flat, ffn_head, small_total, (6, 7), rate, devices, ffn_master, ffn_moment, ffn_average
    )
    att_new = update(
        att_flat, att_head, small_total, (0, 6), rate, devices, att_master, att_moment, att_average
    )
    return (block_output, input_grad) + tuple(att_new) + tuple(ffn_new)


def chunked(mesh):
    return mesh.shape["fsdp"] == 32


def solution(mesh):
    in_specs = (
        P("fsdp", None),
        P("fsdp", None),
        P("fsdp", None),
        P("fsdp", None),
        P("fsdp", None),
        P("fsdp", None),
        P("fsdp", None),
        P("fsdp", None),
        P("fsdp", None),
        P("fsdp", None),
    )
    out_specs = (
        P("fsdp", None),
        P("fsdp", None),
        P("fsdp", None),
        P("fsdp", None),
        P("fsdp", None),
        P("fsdp", None),
        P("fsdp", None),
        P("fsdp", None),
        P("fsdp", None),
        P("fsdp", None),
    )
    body = local_exchange if chunked(mesh) else local
    return jax.shard_map(body, mesh=mesh, in_specs=in_specs, out_specs=out_specs, check_vma=False)
```

```python
import functools
import math

import jax
import jax.numpy as jnp
from jax import lax
from jax.experimental import pallas as pl
from jax.experimental.pallas import tpu as pltpu
from jax.sharding import PartitionSpec as P

HEAD_DIM = 64
FF = 3072


EPSILON = 1e-05
MASKED_SCORE = -1e30


def layer_norm(pre_norm, gain, shift):
    center = pre_norm - jnp.mean(pre_norm, axis=-1, keepdims=True)
    spread = jnp.mean(center * center, axis=-1, keepdims=True)
    return center * lax.rsqrt(spread + EPSILON) * gain + shift


def gelu_exact(inputs):
    return jax.nn.gelu(inputs, approximate=False)


def unpack_attention(flat_att, model_width):
    square = model_width * model_width
    att_mats = flat_att[: 4 * square].reshape(4, model_width, model_width)
    small_params = flat_att[4 * square : 4 * square + 6 * model_width].reshape(6, model_width)
    return (att_mats, small_params)


def unpack_ffn(flat_ffn, model_width, hidden):
    size_in = model_width * hidden
    weight_in = flat_ffn[:size_in].reshape(model_width, hidden)
    weight_out = flat_ffn[size_in : 2 * size_in].reshape(hidden, model_width)
    offset = 2 * size_in
    bias_in = flat_ffn[offset : offset + hidden]
    small_params = flat_ffn[offset + hidden : offset + hidden + 3 * model_width].reshape(
        3, model_width
    )
    return (weight_in, weight_out, bias_in, small_params)


def pack_rows(pieces, row_count):
    filled = sum((piece.shape[0] for piece in pieces))
    padding = jnp.zeros((row_count * 128 - filled,), jnp.float32)
    return jnp.concatenate(list(pieces) + [padding]).reshape(row_count, 128)


def attend_forward(block_items):
    query_block, key_block, value_block, doc_block = block_items
    scores = jnp.einsum("qhd,khd->hqk", query_block, key_block, preferred_element_type=jnp.float32)
    same_doc = doc_block[:, None] == doc_block[None, :]
    scores = jnp.where(same_doc[None], scores, MASKED_SCORE)
    row_max = jnp.max(scores, axis=-1, keepdims=True)
    exponent = jnp.exp(scores - row_max)
    row_total = jnp.sum(exponent, axis=-1, keepdims=True)
    attn_probs = (exponent / row_total).astype(jnp.bfloat16)
    context = jnp.einsum(
        "hqk,khd->qhd", attn_probs, value_block, preferred_element_type=jnp.float32
    )
    return (context.astype(jnp.bfloat16), (row_max + jnp.log(row_total))[..., 0])


def attend_backward(block_items):
    query_block, key_block, value_block, doc_block, log_total, grad_context = block_items
    scores = jnp.einsum("qhd,khd->hqk", query_block, key_block, preferred_element_type=jnp.float32)
    same_doc = doc_block[:, None] == doc_block[None, :]
    scores = jnp.where(same_doc[None], scores, MASKED_SCORE)
    attn_probs = jnp.exp(scores - log_total[..., None])
    probs_low = attn_probs.astype(jnp.bfloat16)
    grad_probs = jnp.einsum(
        "qhd,khd->hqk", grad_context, value_block, preferred_element_type=jnp.float32
    )
    row_inner = jnp.sum(grad_probs * attn_probs, axis=-1, keepdims=True)
    grad_scores = (attn_probs * (grad_probs - row_inner)).astype(jnp.bfloat16)
    grad_query = jnp.einsum(
        "hqk,khd->qhd", grad_scores, key_block, preferred_element_type=jnp.float32
    ).astype(jnp.bfloat16)
    grad_key = jnp.einsum(
        "hqk,qhd->khd", grad_scores, query_block, preferred_element_type=jnp.float32
    ).astype(jnp.bfloat16)
    grad_value = jnp.einsum(
        "hqk,qhd->khd", probs_low, grad_context, preferred_element_type=jnp.float32
    ).astype(jnp.bfloat16)
    return (grad_query, grad_key, grad_value)


def nesterov(master, moment, average, gradient, step_rate):
    moment_new = 0.5 * moment + gradient
    master_new = master - step_rate * (gradient + 0.5 * moment_new)
    average_new = 0.5 * average + 0.5 * master_new
    return (master_new, moment_new, average_new, master_new.astype(jnp.bfloat16))


def local(
    block_input,
    seg_ids,
    masked,
    out_grad,
    att_master,
    att_moment,
    att_average,
    ffn_master,
    ffn_moment,
    ffn_average,
):
    tok_rows, model_width = block_input.shape
    seq_count, seq_length = seg_ids.shape
    head_count = model_width // HEAD_DIM
    devices = lax.axis_size("fsdp")
    att_rows = att_master.shape[0] * devices
    ffn_rows = ffn_master.shape[0] * devices
    head_shape = (seq_count, seq_length, head_count, HEAD_DIM)
    att_whole = lax.all_gather(att_master.astype(jnp.bfloat16), "fsdp", axis=0, tiled=True)
    att_mats, att_small_low = unpack_attention(att_whole.reshape(-1), model_width)
    att_small = att_small_low.astype(jnp.float32)
    masked_rows = masked.reshape(tok_rows, 1) == 1
    stream_in = jnp.where(masked_rows, att_small[5][None, :], block_input.astype(jnp.float32))
    stream_low = stream_in.astype(jnp.bfloat16)
    projected = jnp.einsum(
        "td,cde->cte", stream_low, att_mats[:3], preferred_element_type=jnp.float32
    )
    queries = ((projected[0] + att_small[0]) * 0.125).astype(jnp.bfloat16).reshape(head_shape)
    key_rows = projected[1].astype(jnp.bfloat16).reshape(head_shape)
    values = (projected[2] + att_small[1]).astype(jnp.bfloat16).reshape(head_shape)
    context, log_total = lax.map(attend_forward, (queries, key_rows, values, seg_ids))
    context_flat = context.reshape(tok_rows, model_width)
    pre_one = (
        stream_in
        + jnp.dot(context_flat, att_mats[3], preferred_element_type=jnp.float32)
        + att_small[2]
    )
    normed_one = layer_norm(pre_one, att_small[3], att_small[4])
    normed_low = normed_one.astype(jnp.bfloat16)
    ffn_whole = lax.all_gather(ffn_master.astype(jnp.bfloat16), "fsdp", axis=0, tiled=True)
    weight_in, weight_out, bias_in_low, ffn_small_low = unpack_ffn(
        ffn_whole.reshape(-1), model_width, FF
    )
    bias_in = bias_in_low.astype(jnp.float32)
    ffn_small = ffn_small_low.astype(jnp.float32)
    hid_pre = jnp.dot(normed_low, weight_in, preferred_element_type=jnp.float32) + bias_in
    hid_act = gelu_exact(hid_pre).astype(jnp.bfloat16)
    pre_two = (
        normed_one + jnp.dot(hid_act, weight_out, preferred_element_type=jnp.float32) + ffn_small[0]
    )
    normed_two, norm_two_pull = jax.vjp(layer_norm, pre_two, ffn_small[1], ffn_small[2])
    block_output = normed_two.astype(jnp.bfloat16)
    ffn_back = lax.all_gather(ffn_master.astype(jnp.bfloat16), "fsdp", axis=0, tiled=True)
    back_in, back_out, bias_unused, small_unused = unpack_ffn(ffn_back.reshape(-1), model_width, FF)
    grad_pre_two, grad_gain_two, grad_shift_two = norm_two_pull(out_grad.astype(jnp.float32))
    grad_branch_two = grad_pre_two.astype(jnp.bfloat16)
    grad_w_out = jnp.einsum(
        "tf,td->fd", hid_act, grad_branch_two, preferred_element_type=jnp.float32
    )
    grad_b_out = jnp.sum(grad_branch_two, axis=0, dtype=jnp.float32)
    grad_act = jnp.einsum(
        "td,fd->tf", grad_branch_two, back_out, preferred_element_type=jnp.float32
    )
    hid_unused, gelu_pull = jax.vjp(gelu_exact, hid_pre)
    grad_hidden = gelu_pull(grad_act)[0].astype(jnp.bfloat16)
    grad_w_in = jnp.einsum("td,tf->df", normed_low, grad_hidden, preferred_element_type=jnp.float32)
    grad_b_in = jnp.sum(grad_hidden, axis=0, dtype=jnp.float32)
    grad_normed_one = grad_pre_two + jnp.einsum(
        "tf,df->td", grad_hidden, back_in, preferred_element_type=jnp.float32
    )
    ffn_flat_grad = pack_rows(
        (
            grad_w_in.reshape(-1),
            grad_w_out.reshape(-1),
            grad_b_in,
            grad_b_out,
            grad_gain_two,
            grad_shift_two,
        ),
        ffn_rows,
    )
    ffn_grad = lax.psum_scatter(ffn_flat_grad, "fsdp", scatter_dimension=0, tiled=True)
    att_back = lax.all_gather(att_master.astype(jnp.bfloat16), "fsdp", axis=0, tiled=True)
    back_mats, small_back = unpack_attention(att_back.reshape(-1), model_width)
    pre_unused, norm_one_pull = jax.vjp(layer_norm, pre_one, att_small[3], att_small[4])
    grad_pre_one, grad_gain_one, grad_shift_one = norm_one_pull(grad_normed_one)
    grad_branch_one = grad_pre_one.astype(jnp.bfloat16)
    grad_w_o = jnp.einsum(
        "td,te->de", context_flat, grad_branch_one, preferred_element_type=jnp.float32
    )
    grad_b_o = jnp.sum(grad_branch_one, axis=0, dtype=jnp.float32)
    grad_context = jnp.einsum(
        "te,de->td", grad_branch_one, back_mats[3], preferred_element_type=jnp.float32
    ).astype(jnp.bfloat16)
    grad_q4, grad_k4, grad_v4 = lax.map(
        attend_backward,
        (queries, key_rows, values, seg_ids, log_total, grad_context.reshape(head_shape)),
    )
    grad_queries = grad_q4.reshape(tok_rows, model_width) * 0.125
    grad_keys = grad_k4.reshape(tok_rows, model_width)
    grad_values = grad_v4.reshape(tok_rows, model_width)
    grad_projected = jnp.stack([grad_queries, grad_keys, grad_values])
    grad_w_qkv = jnp.einsum(
        "td,cte->cde", stream_low, grad_projected, preferred_element_type=jnp.float32
    )
    grad_b_q = jnp.sum(grad_queries, axis=0, dtype=jnp.float32)
    grad_b_v = jnp.sum(grad_values, axis=0, dtype=jnp.float32)
    grad_stream = grad_pre_one + jnp.einsum(
        "cte,cde->td", grad_projected, back_mats[:3], preferred_element_type=jnp.float32
    )
    grad_mask_vector = jnp.sum(jnp.where(masked_rows, grad_stream, 0.0), axis=0)
    input_grad = jnp.where(masked_rows, 0.0, grad_stream)
    att_flat_grad = pack_rows(
        (
            grad_w_qkv.reshape(-1),
            grad_w_o.reshape(-1),
            grad_b_q,
            grad_b_v,
            grad_b_o,
            grad_gain_one,
            grad_shift_one,
            grad_mask_vector,
        ),
        att_rows,
    )
    att_grad = lax.psum_scatter(att_flat_grad, "fsdp", scatter_dimension=0, tiled=True)
    step_rate = 0.05 / math.sqrt(tok_rows * devices)
    att_new = nesterov(att_master, att_moment, att_average, att_grad, step_rate)
    ffn_new = nesterov(ffn_master, ffn_moment, ffn_average, ffn_grad, step_rate)
    return (
        block_output,
        input_grad,
        att_new[0],
        att_new[1],
        att_new[2],
        att_new[3],
        ffn_new[0],
        ffn_new[1],
        ffn_new[2],
        ffn_new[3],
    )


BF = jnp.bfloat16
F32 = jnp.float32
LANES = 128
SLOT = 96
TILE = 256
EXTRA = 16
MIB = 1 << 20
BIG = 58


def params(limit):
    return pltpu.CompilerParams(vmem_limit_bytes=limit * MIB)


def spec_any():
    return pl.BlockSpec(memory_space=pl.ANY)


def spec_vmem():
    return pl.BlockSpec(memory_space=pltpu.VMEM)


def spec_whole(shape):
    return pl.BlockSpec(shape, lambda *ids: (0,) * len(shape))


def dot_nn(left, right):
    return lax.dot_general(left, right, (((1,), (0,)), ((), ())), preferred_element_type=F32)


def dot_nt(left, right):
    return lax.dot_general(left, right, (((1,), (1,)), ((), ())), preferred_element_type=F32)


def dot_tn(left, right):
    return lax.dot_general(left, right, (((0,), (0,)), ((), ())), preferred_element_type=F32)


def slot_of(chunk, me, late=False):
    diff = lax.bitwise_xor(me, chunk)
    far_core = lax.bitwise_and(diff, 1)
    x_bit = lax.bitwise_and(lax.shift_right_logical(diff, 1), 1)
    y_bit = lax.bitwise_and(lax.shift_right_logical(diff, 2), 1)
    z_low = lax.bitwise_and(lax.shift_right_logical(diff, 3), 1)
    z_high = lax.shift_right_logical(diff, 4)
    core = lax.bitwise_xor(lax.bitwise_and(me, 1), far_core)
    third = x_bit + core * (y_bit - x_bit)
    fourth = y_bit + core * (x_bit - y_bit)
    if late:
        return far_core, z_high + 2 * third + 4 * z_low + 8 * fourth
    return far_core, z_high + 2 * z_low + 4 * third + 8 * fourth


def stage_perm(stage):
    if stage == 0:
        return [(i, i ^ 16) for i in range(32)]
    if stage == 1:
        return [(i, i ^ 8) for i in range(32)]
    if stage == 2:
        return [(i, i ^ (4 if i & 1 else 2)) for i in range(32)]
    if stage == 3:
        return [(i, i ^ (2 if i & 1 else 4)) for i in range(32)]
    return [(i, i ^ 1) for i in range(32)]


def exchange(array, stage):
    return lax.ppermute(array, "fsdp", stage_perm(stage))


def widen(held, got):
    return jnp.concatenate([held, got])


def widen_small(held, got):
    low = held.shape[0] - EXTRA
    small = held[low:] + got[low:]
    return jnp.concatenate([held[:low], got[:low], small])


def total_of(arrays, first, last):
    total = arrays[0][first:last].astype(F32)
    for array in arrays[1:]:
        total = total + array[first:last].astype(F32)
    return total


def halve(*arrays):
    rows = arrays[0].shape[0]
    low = total_of(arrays, 0, rows // 2).astype(BF)
    return low, total_of(arrays, rows // 2, rows).astype(BF)


def add_small(values, small):
    return jnp.concatenate([values, small.astype(BF)])


def phase(*values):
    return lax.optimization_barrier(values)


def prep_kernel(last, att_mats, ffn_mats, att_ref, ffn_ref, tail_ref, att_out, small_out, ffn_a, ffn_b, att_buf, ffn_buf):
    me = lax.axis_index("fsdp")
    att_rows = att_ref.shape[0]
    ffn_rows = ffn_ref.shape[0]
    att_buf[0:64, :] = tail_ref[0:64, :]
    att_buf[64 : 64 + att_rows, :] = att_ref[...]
    ffn_buf[0:64, :] = tail_ref[64:128, :]
    ffn_buf[64 : 64 + ffn_rows, :] = ffn_ref[...]
    start = 64 - 2 * me
    for part in range(6):
        cols = slice(part * LANES, (part + 1) * LANES)
        att_out[:, cols] = att_buf[pl.ds(start + part, SLOT, stride=6), :].astype(BF)
    first = me < 16

    @pl.when(first)
    def _():
        for block in range(4):
            out = ffn_a if block < 2 else ffn_b
            rows = slice((block % 2) * 48, (block % 2) * 48 + 48)
            for part in range(6):
                cols = slice(part * LANES, (part + 1) * LANES)
                piece = ffn_buf[pl.ds(start + 6 * block + part, 48, stride=24), :]
                out[rows, cols] = piece.astype(BF)

    @pl.when(jnp.logical_not(first))
    def _():
        for part in range(6):
            cols = slice(part * LANES, (part + 1) * LANES)
            ffn_a[:, cols] = ffn_buf[pl.ds(start + part, SLOT, stride=6), :].astype(BF)
            ffn_b[:, cols] = ffn_buf[pl.ds(start + 6 * SLOT + part, SLOT, stride=6), :].astype(BF)

    small_out[...] = jnp.zeros_like(small_out)

    @pl.when(me == last)
    def _():
        att_at = 64 + att_mats - last * att_rows
        ffn_at = 64 + ffn_mats - last * ffn_rows
        for part in range(6):
            cols = slice(part * LANES, (part + 1) * LANES)
            upper = att_buf[pl.ds(att_at + part, 6, stride=6), :]
            lower = ffn_buf[pl.ds(ffn_at + part, 7, stride=6), :]
            both = jnp.concatenate([upper, lower, jnp.zeros((3, LANES), F32)])
            small_out[:, cols] = both.astype(BF)


def prepare(att_master, ffn_master, tails, devices, width):
    att_mats = 4 * width * width // LANES
    ffn_mats = 2 * width * FF // LANES
    att_rows, ffn_rows = att_master.shape[0], ffn_master.shape[0]
    body = functools.partial(prep_kernel, devices - 1, att_mats, ffn_mats)
    return pl.pallas_call(
        body,
        out_shape=(
            jax.ShapeDtypeStruct((SLOT, width), BF),
            jax.ShapeDtypeStruct((EXTRA, width), BF),
            jax.ShapeDtypeStruct((SLOT, width), BF),
            jax.ShapeDtypeStruct((SLOT, width), BF),
        ),
        in_specs=[spec_vmem()] * 3,
        out_specs=(spec_vmem(),) * 4,
        scratch_shapes=[
            pltpu.VMEM((64 + att_rows + 6, LANES), F32),
            pltpu.VMEM((64 + ffn_rows + 6, LANES), F32),
        ],
        compiler_params=params(16),
        name="prep",
    )(att_master, ffn_master, tails)


def pick(index, refs, use):
    for number in range(len(refs)):

        @pl.when(index == number)
        def _():
            use(refs[number])


def start_copy(quad, far_core, slot, offset, rows, dst, sem):
    at = pl.multiple_of(lax.bitwise_and(slot, 7) * SLOT + offset, 16)

    def copy(ref):
        pltpu.make_async_copy(ref.at[pl.ds(at, rows), :], dst, sem).start()

    pick(2 * far_core + lax.shift_right_logical(slot, 3), quad, copy)


def load_att(quad, dst, sem, first, last):
    me = lax.axis_index("fsdp")

    def body(chunk, carry):
        far_core, slot = slot_of(chunk, me)
        at = pl.multiple_of((chunk - first) * SLOT, 32)
        start_copy(quad, far_core, slot, 0, SLOT, dst.at[pl.ds(at, SLOT), :], sem)
        return carry

    lax.fori_loop(first, last, body, 0)


def load_ffn(quads, w_in, w_out, sem_in, sem_out):
    me = lax.axis_index("fsdp")
    for block in range(4):
        unit = block // 2

        def body_in(chunk, carry):
            far_core, slot = slot_of(chunk, me, unit == 1)
            dst = w_in.at[block, pl.ds(pl.multiple_of(chunk * 48, 16), 48), :]
            start_copy(quads[unit], far_core, slot, (block % 2) * 48, 48, dst, sem_in.at[block])
            return carry

        def body_out(chunk, carry):
            for which in range(2):
                far_core, slot = slot_of(chunk, me, which == 1)
                at = pl.multiple_of((chunk - 16) * 192 + which * SLOT, 32)
                dst = w_out.at[pl.ds(at, SLOT), :]
                start_copy(quads[which], far_core, slot, 0, SLOT, dst, sem_out.at[block])
            return carry

        lax.fori_loop(0, 16, body_in, 0)
        lax.fori_loop(16 + 4 * block, 20 + 4 * block, body_out, 0)


def wait_whole(ref, sem):
    pltpu.make_async_copy(ref, ref, sem).wait()


def head_mask(rows):
    lane = lax.broadcasted_iota(jnp.int32, (rows, LANES), 1)
    return lane < HEAD_DIM


def project_kernel(x_ref, masked_ref, *refs):
    quad = refs[0:4]
    stream_ref, q_ref, k_ref, v_ref, small_ref, weights, smalls, sems, small_sem = refs[4:]
    width = x_ref.shape[1]

    @pl.when(pl.program_id(0) == 0)
    def _():
        for part in range(4):
            src = quad[part].at[pl.ds(8 * SLOT, EXTRA), :]
            pltpu.make_async_copy(src, smalls.at[part], small_sem).start()
        for matrix in range(3):
            rows = weights.at[matrix * width : (matrix + 1) * width]
            load_att(quad, rows, sems.at[matrix], 8 * matrix, 8 * matrix + 8)
        wait_whole(smalls, small_sem)
        total = smalls[0].astype(F32)
        for part in range(1, 4):
            total = total + smalls[part].astype(F32)
        small_ref[...] = total

    small = small_ref[...]
    stream = jnp.where(masked_ref[...] == 1, small[5:6], x_ref[...].astype(F32)).astype(BF)
    stream_ref[...] = stream
    for matrix in range(3):
        rows = slice(matrix * width, (matrix + 1) * width)

        @pl.when(pl.program_id(0) == 0)
        def _():
            wait_whole(weights.at[rows], sems.at[matrix])

        product = dot_nn(stream, weights[rows])
        if matrix == 0:
            q_ref[...] = ((product + small[0:1]) * 0.125).astype(BF)
        elif matrix == 1:
            k_ref[...] = product.astype(BF)
        else:
            v_ref[...] = (product + small[1:2]).astype(BF)


def project(block_input, masked_col, quad):
    tok, width = block_input.shape
    rows = 2 * TILE
    tile = lambda cols: pl.BlockSpec((rows, cols), lambda s: (s, 0))
    bf = jax.ShapeDtypeStruct((tok, width), BF)
    return pl.pallas_call(
        project_kernel,
        grid=(tok // rows,),
        out_shape=(bf, bf, bf, bf, jax.ShapeDtypeStruct((EXTRA, width), F32)),
        in_specs=[tile(width), tile(1)] + [spec_any()] * 4,
        out_specs=(tile(width),) * 4 + (spec_whole((EXTRA, width)),),
        scratch_shapes=[
            pltpu.VMEM((3 * width, width), BF),
            pltpu.VMEM((4, EXTRA, width), BF),
            pltpu.SemaphoreType.DMA((3,)),
            pltpu.SemaphoreType.DMA,
        ],
        compiler_params=params(BIG),
        cost_estimate=pl.CostEstimate(
            flops=6 * tok * width * width, bytes_accessed=16 * MIB, transcendentals=0
        ),
        name="project",
    )(block_input, masked_col, *quad)


def forward_kernel(held, q_ref, k_ref, v_ref, seg_col_ref, seg_row_ref, *refs):
    ctx_ref, lse_ref = refs[held:]
    left = head_mask(q_ref.shape[0])
    same = seg_col_ref[...] == seg_row_ref[0]
    queries = q_ref[...]
    keys = k_ref[...]
    values_t = v_ref[...].T
    outs = []
    for head in range(2):
        keep = left if head == 0 else jnp.logical_not(left)
        own = jnp.where(keep, queries, jnp.zeros_like(queries))
        scores = jnp.where(same, dot_nt(keys, own), MASKED_SCORE)
        top = jnp.max(scores, axis=0, keepdims=True)
        exponent = jnp.exp(scores - top)
        total = jnp.sum(exponent, axis=0, keepdims=True)
        probs = (exponent * (1.0 / total)).astype(BF)
        lse_ref[0, 0, head : head + 1, :] = top + jnp.log(total)
        outs.append(dot_nn(values_t[head * HEAD_DIM : (head + 1) * HEAD_DIM], probs))
    ctx_ref[...] = jnp.concatenate(outs).T.astype(BF)


def sequence_specs(at, seq):
    tile = lambda: pl.BlockSpec((seq, LANES), lambda i: (at, i))
    col = lambda: pl.BlockSpec((seq, 1), lambda i: (at, 0))
    row = lambda: pl.BlockSpec((1, 1, seq), lambda i: (at, 0, 0))
    stat = lambda: pl.BlockSpec((1, 1, 2, seq), lambda i: (at, i, 0, 0))
    return tile, col, row, stat


def attention_forward(at, q, k, v, seg_col, seg_row, held=()):
    tok, width = q.shape
    seq_count, seq = seg_row.shape[0], seg_row.shape[2]
    pairs = width // LANES
    tile, col, row, stat = sequence_specs(at, seq)
    return pl.pallas_call(
        functools.partial(forward_kernel, len(held)),
        grid=(pairs,),
        out_shape=(
            jax.ShapeDtypeStruct((tok, width), BF),
            jax.ShapeDtypeStruct((seq_count, pairs, 2, seq), F32),
        ),
        in_specs=[tile(), tile(), tile(), col(), row()] + [spec_any() for _ in held],
        out_specs=(tile(), stat()),
        input_output_aliases={5 + i: i for i in range(len(held))},
        compiler_params=params(BIG),
        cost_estimate=pl.CostEstimate(
            flops=16 * seq * seq * width,
            bytes_accessed=4 * MIB,
            transcendentals=seq * seq * width // HEAD_DIM,
        ),
        name="attention_forward",
    )(q, k, v, seg_col, seg_row, *held)


def norm_stats(pre_norm):
    center = pre_norm - jnp.mean(pre_norm, axis=-1, keepdims=True)
    scale = lax.rsqrt(jnp.mean(center * center, axis=-1, keepdims=True) + EPSILON)
    return center * scale, scale


def norm_back(grad, gain, normed, scale):
    scaled = grad * gain
    mean_one = jnp.mean(scaled, axis=-1, keepdims=True)
    mean_two = jnp.mean(scaled * normed, axis=-1, keepdims=True)
    return scale * (scaled - mean_one - normed * mean_two)


def column_sum(array):
    return jnp.sum(array, axis=0, keepdims=True)


def gelu_pair(inputs):
    phi_cdf = 0.5 + 0.5 * lax.erf(inputs * math.sqrt(0.5))
    density = jnp.exp(inputs * inputs * -0.5) * (1.0 / math.sqrt(2.0 * math.pi))
    return inputs * phi_cdf, phi_cdf + inputs * density


def ffn_kernel(
    stream_ref,
    ctx_ref,
    grad_ref,
    small_ref,
    *refs,
):
    att_quad, quad_a, quad_b = refs[0:4], refs[4:8], refs[8:12]
    y_ref, x1_ref, hid_ref, dhid_ref, dfb_ref, dpre_ref, dob_ref, dctx_ref, sums_ref = refs[12:21]
    w_in, w_out, w_o, slope, sem_in, sem_out, sem_o = refs[21:]
    width = ctx_ref.shape[1]
    blocks = FF // width
    step = pl.program_id(0)

    @pl.when(step == 0)
    def _():
        load_att(att_quad, w_o, sem_o, 24, 32)
        load_ffn((quad_a, quad_b), w_in, w_out, sem_in, sem_out)
        sums_ref[...] = jnp.zeros_like(sums_ref)

    @pl.when(step == 0)
    def _():
        wait_whole(w_o, sem_o)

    small = small_ref[...]
    pre_one = stream_ref[...].astype(F32) + dot_nn(ctx_ref[...], w_o[...]) + small[2:3]
    normed_one, scale_one = norm_stats(pre_one)
    x_one = normed_one * small[3:4] + small[4:5]
    x_low = x_one.astype(BF)
    x1_ref[...] = x_low

    total = x_one + small[10:11]
    for block in range(blocks):
        cols = slice(block * width, (block + 1) * width)

        @pl.when(step == 0)
        def _():
            wait_whole(w_in.at[block], sem_in.at[block])
            wait_whole(w_out.at[cols, :], sem_out.at[block])

        hidden, gate = gelu_pair(dot_nn(x_low, w_in[block]) + small[6 + block : 7 + block])
        hidden = hidden.astype(BF)
        hid_ref[:, cols] = hidden
        slope[block] = gate
        total = total + dot_nn(hidden, w_out[cols, :])
    normed_two, scale_two = norm_stats(total)
    y_ref[...] = (normed_two * small[11:12] + small[12:13]).astype(BF)
    grad_out = grad_ref[...].astype(F32)
    grad_two = norm_back(grad_out, small[11:12], normed_two, scale_two)
    grad_low = grad_two.astype(BF)
    dfb_ref[...] = grad_low
    sums_ref[10:11] += column_sum(grad_low.astype(F32))
    sums_ref[11:12] += column_sum(grad_out * normed_two)
    sums_ref[12:13] += column_sum(grad_out)
    grad_one = grad_two
    for block in range(blocks):
        cols = slice(block * width, (block + 1) * width)
        dhid = (dot_nt(grad_low, w_out[cols, :]) * slope[block]).astype(BF)
        dhid_ref[:, cols] = dhid
        sums_ref[6 + block : 7 + block] += column_sum(dhid.astype(F32))
        grad_one = grad_one + dot_nt(dhid, w_in[block])
    sums_ref[3:4] += column_sum(grad_one * normed_one)
    sums_ref[4:5] += column_sum(grad_one)
    grad_pre = norm_back(grad_one, small[3:4], normed_one, scale_one)
    dpre_ref[...] = grad_pre
    dob = grad_pre.astype(BF)
    dob_ref[...] = dob
    sums_ref[2:3] += column_sum(dob.astype(F32))
    dctx_ref[...] = dot_nt(dob, w_o[...]).astype(BF)


def feed_forward(stream, ctx, out_grad, small, att_quad, quad_a, quad_b):
    tok, width = ctx.shape
    tile = lambda cols: pl.BlockSpec((TILE, cols), lambda i: (i, 0))
    bf = lambda cols: jax.ShapeDtypeStruct((tok, cols), BF)
    return pl.pallas_call(
        ffn_kernel,
        grid=(tok // TILE,),
        out_shape=(
            bf(width),
            bf(width),
            bf(FF),
            bf(FF),
            bf(width),
            jax.ShapeDtypeStruct((tok, width), F32),
            bf(width),
            bf(width),
            jax.ShapeDtypeStruct((EXTRA, width), F32),
        ),
        in_specs=[tile(width)] * 3 + [spec_whole((EXTRA, width))] + [spec_any()] * 12,
        out_specs=(
            tile(width),
            tile(width),
            tile(FF),
            tile(FF),
            tile(width),
            tile(width),
            tile(width),
            tile(width),
            spec_whole((EXTRA, width)),
        ),
        scratch_shapes=[
            pltpu.VMEM((FF // width, width, width), BF),
            pltpu.VMEM((FF, width), BF),
            pltpu.VMEM((width, width), BF),
            pltpu.VMEM((FF // width, TILE, width), F32),
            pltpu.SemaphoreType.DMA((FF // width,)),
            pltpu.SemaphoreType.DMA((FF // width,)),
            pltpu.SemaphoreType.DMA,
        ],
        compiler_params=params(BIG),
        cost_estimate=pl.CostEstimate(
            flops=8 * tok * width * FF, bytes_accessed=40 * MIB, transcendentals=2 * tok * FF
        ),
        name="feed_forward",
    )(stream, ctx, out_grad, small, *att_quad, *quad_a, *quad_b)


def send_slot(parts, far_core, slot, offset, src, sem):
    at = pl.multiple_of(lax.bitwise_and(slot, 7) * SLOT + offset, 16)

    def copy(ref):
        pltpu.make_async_copy(src, ref.at[pl.ds(at, src.shape[0]), :], sem).start()

    pick(2 * far_core + lax.shift_right_logical(slot, 3), parts, copy)


def part_shapes(width, small):
    rows = [8 * SLOT, 8 * SLOT, 8 * SLOT, 8 * SLOT + (EXTRA if small else 0)]
    return tuple(jax.ShapeDtypeStruct((count, width), BF) for count in rows)


def wait_reuse(stage, sems, buf, step):
    @pl.when(step >= 2)
    def _():
        wait_whole(stage.at[buf], sems.at[buf])


def wait_last(stage, sems, step, steps):
    @pl.when(step == steps - 1)
    def _():
        for buf in range(2):
            wait_whole(stage.at[buf], sems.at[buf])


def send_in_blocks(parts, me, late, part, stage, buf, sem):
    for chunk in range(16):
        far_core, slot = slot_of(chunk, me, late)
        src = stage.at[buf, chunk * 48 : (chunk + 1) * 48]
        send_slot(parts, far_core, slot, part * 48, src, sem)


def ffn_grad_kernel(x_ref, hid_ref, dhid_ref, dfb_ref, sums_ref, *refs):
    parts_a, parts_b = refs[0:4], refs[4:8]
    stage, small_stage, sems, small_sem = refs[8:]
    me = lax.axis_index("fsdp")
    step = pl.program_id(0)
    buf = lax.rem(step, 2)
    small_rows = parts_b[3].at[pl.ds(8 * SLOT, EXTRA), :]

    @pl.when(step == 0)
    def _():
        small_stage[...] = sums_ref[...].astype(BF)
        pltpu.make_async_copy(small_stage, small_rows, small_sem).start()

    wait_reuse(stage, sems, buf, step)

    @pl.when(step < 4)
    def _():
        stage[buf] = dot_tn(hid_ref[...], dfb_ref[...]).astype(BF)
        for piece in range(8):
            late = piece % 2 == 1
            far_core, slot = slot_of(16 + 4 * step + piece // 2, me, late)
            src = stage.at[buf, piece * SLOT : (piece + 1) * SLOT]
            send_slot(parts_b if late else parts_a, far_core, slot, 0, src, sems.at[buf])

    @pl.when(step >= 4)
    def _():
        stage[buf] = dot_tn(x_ref[...], dhid_ref[...]).astype(BF)
        send_in_blocks(parts_b, me, True, step - 4, stage, buf, sems.at[buf])

    @pl.when(step == 5)
    def _():
        wait_whole(small_stage, small_sem)

    wait_last(stage, sems, step, 6)


def ffn_grads(x_low, hidden, dhid, dfb, sums):
    tok, width = x_low.shape
    out = pl.pallas_call(
        ffn_grad_kernel,
        grid=(6,),
        out_shape=part_shapes(width, False) + part_shapes(width, True),
        in_specs=[
            spec_whole((tok, width)),
            pl.BlockSpec((tok, width), lambda i: (0, jnp.minimum(i, 3))),
            pl.BlockSpec((tok, width), lambda i: (0, jnp.maximum(i - 2, 2))),
            spec_whole((tok, width)),
            spec_whole((EXTRA, width)),
        ],
        out_specs=(spec_any(),) * 8,
        scratch_shapes=[
            pltpu.VMEM((2, width, width), BF),
            pltpu.VMEM((EXTRA, width), BF),
            pltpu.SemaphoreType.DMA((2,)),
            pltpu.SemaphoreType.DMA,
        ],
        compiler_params=params(BIG),
        cost_estimate=pl.CostEstimate(
            flops=3 * tok * width * FF, bytes_accessed=24 * MIB, transcendentals=0
        ),
        name="ffn_grads",
    )(x_low, hidden, dhid, dfb, sums)
    return out[0:4], out[4:8]


def ffn_rest_kernel(x_ref, dhid_ref, *refs):
    parts = refs[4:8]
    stage, sems = refs[8:]
    me = lax.axis_index("fsdp")
    step = pl.program_id(0)
    stage[step] = dot_tn(x_ref[...], dhid_ref[...]).astype(BF)
    send_in_blocks(parts, me, False, step, stage, step, sems.at[step])
    wait_last(stage, sems, step, 2)


def ffn_rest(x_low, dhid, parts):
    tok, width = x_low.shape
    return pl.pallas_call(
        ffn_rest_kernel,
        grid=(2,),
        out_shape=part_shapes(width, False),
        in_specs=[spec_whole((tok, width)), pl.BlockSpec((tok, width), lambda i: (0, i))]
        + [spec_any()] * 4,
        out_specs=(spec_any(),) * 4,
        input_output_aliases={2 + i: i for i in range(4)},
        scratch_shapes=[pltpu.VMEM((2, width, width), BF), pltpu.SemaphoreType.DMA((2,))],
        compiler_params=params(BIG),
        cost_estimate=pl.CostEstimate(
            flops=tok * width * FF, bytes_accessed=8 * MIB, transcendentals=0
        ),
        name="ffn_rest",
    )(x_low, dhid, *parts)


def backward_kernel(held, q_ref, k_ref, v_ref, dctx_ref, lse_ref, seg_col_ref, seg_row_ref, *refs):
    dq_ref, dk_ref, dv_ref = refs[held:]
    left = head_mask(q_ref.shape[0])
    same = seg_col_ref[...] == seg_row_ref[0]
    queries = q_ref[...]
    keys = k_ref[...]
    values = v_ref[...]
    grads = dctx_ref[...]
    keys_t = keys.T
    grad_q = []
    grad_k = None
    grad_v = None
    for head in range(2):
        keep = left if head == 0 else jnp.logical_not(left)
        own = jnp.where(keep, queries, jnp.zeros_like(queries))
        own_grad = jnp.where(keep, grads, jnp.zeros_like(grads))
        log_total = lse_ref[0, 0, head : head + 1, :]
        scores = jnp.where(same, dot_nt(keys, own), MASKED_SCORE)
        probs = jnp.exp(scores - log_total)
        grad_probs = dot_nt(values, own_grad)
        inner = jnp.sum(grad_probs * probs, axis=0, keepdims=True)
        grad_scores = (probs * (grad_probs - inner)).astype(BF)
        part_v = dot_nn(probs.astype(BF), own_grad)
        part_k = dot_nn(grad_scores, own)
        grad_v = part_v if head == 0 else grad_v + part_v
        grad_k = part_k if head == 0 else grad_k + part_k
        grad_q.append(dot_nn(keys_t[head * HEAD_DIM : (head + 1) * HEAD_DIM], grad_scores))
    dq_ref[...] = (jnp.concatenate(grad_q).T.astype(BF) * 0.125).astype(BF)
    dk_ref[...] = grad_k.astype(BF)
    dv_ref[...] = grad_v.astype(BF)


def attention_backward(at, q, k, v, dctx, lse, seg_col, seg_row, held=()):
    tok, width = q.shape
    seq = seg_row.shape[2]
    tile, col, row, stat = sequence_specs(at, seq)
    return pl.pallas_call(
        functools.partial(backward_kernel, len(held)),
        grid=(width // LANES,),
        out_shape=(jax.ShapeDtypeStruct((tok, width), BF),) * 3,
        in_specs=[tile(), tile(), tile(), tile(), stat(), col(), row()]
        + [spec_any() for _ in held],
        out_specs=(tile(), tile(), tile()),
        input_output_aliases={7 + i: i for i in range(len(held))},
        compiler_params=params(BIG),
        cost_estimate=pl.CostEstimate(
            flops=40 * seq * seq * width,
            bytes_accessed=6 * MIB,
            transcendentals=seq * seq * width // HEAD_DIM,
        ),
        name="attention_backward",
    )(q, k, v, dctx, lse, seg_col, seg_row, *held)


def input_grad_kernel(dq_ref, dk_ref, dv_ref, dpre_ref, masked_ref, *refs):
    quad = refs[0:4]
    dx_ref, small_ref, weights, sems = refs[4:]
    width = dq_ref.shape[1]
    step = pl.program_id(0)

    @pl.when(step == 0)
    def _():
        for matrix in range(3):
            rows = weights.at[matrix * width : (matrix + 1) * width]
            load_att(quad, rows, sems.at[matrix], 8 * matrix, 8 * matrix + 8)
        small_ref[...] = jnp.zeros_like(small_ref)

    grad = dpre_ref[...]
    for matrix in range(3):
        rows = slice(matrix * width, (matrix + 1) * width)

        @pl.when(step == 0)
        def _():
            wait_whole(weights.at[rows], sems.at[matrix])

        grad = grad + dot_nt((dq_ref, dk_ref, dv_ref)[matrix][...], weights[rows])
    chosen = masked_ref[...] == 1
    dx_ref[...] = jnp.where(chosen, 0.0, grad)
    small_ref[0:1] += column_sum(dq_ref[...].astype(F32))
    small_ref[1:2] += column_sum(dv_ref[...].astype(F32))
    small_ref[5:6] += column_sum(jnp.where(chosen, grad, 0.0))


def input_grads(dq, dk, dv, dpre, masked_col, quad):
    tok, width = dq.shape
    rows = TILE
    tile = lambda cols: pl.BlockSpec((rows, cols), lambda i: (i, 0))
    whole = spec_whole((EXTRA, width))
    return pl.pallas_call(
        input_grad_kernel,
        grid=(tok // rows,),
        out_shape=(
            jax.ShapeDtypeStruct((tok, width), F32),
            jax.ShapeDtypeStruct((EXTRA, width), F32),
        ),
        in_specs=[tile(width)] * 4 + [tile(1)] + [spec_any()] * 4,
        out_specs=(tile(width), whole),
        scratch_shapes=[pltpu.VMEM((3 * width, width), BF), pltpu.SemaphoreType.DMA((3,))],
        compiler_params=params(BIG),
        cost_estimate=pl.CostEstimate(
            flops=6 * tok * width * width, bytes_accessed=16 * MIB, transcendentals=0
        ),
        name="input_grads",
    )(dq, dk, dv, dpre, masked_col, *quad)


def att_grad_kernel(*refs):
    sources, parts = refs[0:6], refs[6:10]
    held, stage, load_sems, sems = refs[10:]
    me = lax.axis_index("fsdp")
    step = pl.program_id(0)
    buf = lax.rem(step, 2)

    @pl.when(step == 0)
    def _():
        for number in range(6):
            pltpu.make_async_copy(sources[number], held.at[number], load_sems.at[number]).start()

    wait_reuse(stage, sems, buf, step)
    for matrix in range(4):

        @pl.when(step == matrix)
        def _():
            for number in ((0, 1), (2, 3), (4,), (5,))[matrix]:
                wait_whole(held.at[number], load_sems.at[number])
            left = 0 if matrix == 0 else 2
            right = 1 if matrix == 0 else 2 + matrix
            stage[buf] = dot_tn(held[left], held[right]).astype(BF)

    first = lax.rem(step + 3, 4) * 8
    for piece in range(8):
        far_core, slot = slot_of(first + piece, me)
        src = stage.at[buf, piece * SLOT : (piece + 1) * SLOT]
        send_slot(parts, far_core, slot, 0, src, sems.at[buf])
    wait_last(stage, sems, step, 4)


def att_grads(ctx, dob, stream, dq, dk, dv):
    tok, width = stream.shape
    return pl.pallas_call(
        att_grad_kernel,
        grid=(4,),
        out_shape=part_shapes(width, False),
        in_specs=[spec_any()] * 6,
        out_specs=(spec_any(),) * 4,
        scratch_shapes=[
            pltpu.VMEM((6, tok, width), BF),
            pltpu.VMEM((2, width, width), BF),
            pltpu.SemaphoreType.DMA((6,)),
            pltpu.SemaphoreType.DMA((2,)),
        ],
        compiler_params=params(BIG),
        cost_estimate=pl.CostEstimate(
            flops=8 * tok * width * width, bytes_accessed=16 * MIB, transcendentals=0
        ),
        name="att_grads",
    )(ctx, dob, stream, dq, dk, dv)


def flat_att_kernel(grad_ref, out_ref):
    for part in range(6):
        out_ref[pl.ds(part, SLOT, stride=6), :] = grad_ref[:, part * LANES : (part + 1) * LANES]


def flat_ffn_kernel(a_ref, b_ref, out_ref):
    first = lax.axis_index("fsdp") < 16

    @pl.when(first)
    def _():
        for block in range(4):
            source = a_ref if block < 2 else b_ref
            rows = slice((block % 2) * 48, (block % 2) * 48 + 48)
            for part in range(6):
                cols = slice(part * LANES, (part + 1) * LANES)
                out_ref[pl.ds(6 * block + part, 48, stride=24), :] = source[rows, cols]

    @pl.when(jnp.logical_not(first))
    def _():
        for part in range(6):
            cols = slice(part * LANES, (part + 1) * LANES)
            out_ref[pl.ds(part, SLOT, stride=6), :] = a_ref[:, cols]
            out_ref[pl.ds(6 * SLOT + part, SLOT, stride=6), :] = b_ref[:, cols]


def flatten(kernel, rows, *pieces):
    return pl.pallas_call(
        kernel,
        out_shape=jax.ShapeDtypeStruct((rows, LANES), F32),
        in_specs=[spec_vmem()] * len(pieces),
        out_specs=spec_vmem(),
        compiler_params=params(16),
        name="flatten",
    )(*pieces)


def update_kernel(last, small_at, rate, flat_ref, head_ref, small_ref, w_ref, m_ref, a_ref, w_out, m_out, a_out, low_out, buf):
    me = lax.axis_index("fsdp")
    aligned = flat_ref.shape[0]
    own = w_ref.shape[0]
    count = small_at[1]
    buf[0:aligned, :] = flat_ref[...]
    buf[aligned : aligned + 64, :] = head_ref[...]

    @pl.when(me == last)
    def _():
        buf[aligned : aligned + 64, :] = jnp.zeros((64, LANES), F32)
        for part in range(6):
            cols = slice(part * LANES, (part + 1) * LANES)
            buf[pl.ds(aligned + part, count, stride=6), :] = small_ref[
                small_at[0] : small_at[0] + count, cols
            ]

    grad = buf[pl.ds(2 * me, own), :]
    moment = 0.5 * m_ref[...] + grad
    master = w_ref[...] - rate * (grad + 0.5 * moment)
    m_out[...] = moment
    w_out[...] = master
    a_out[...] = 0.5 * a_ref[...] + 0.5 * master
    low_out[...] = master.astype(BF)


def update(flat, head, small, small_at, rate, devices, master, moment, average):
    own = master.shape[0]
    f32 = jax.ShapeDtypeStruct((own, LANES), F32)
    body = functools.partial(update_kernel, devices - 1, small_at, rate)
    return pl.pallas_call(
        body,
        out_shape=(f32, f32, f32, jax.ShapeDtypeStruct((own, LANES), BF)),
        in_specs=[spec_vmem()] * 6,
        out_specs=(spec_vmem(),) * 4,
        scratch_shapes=[pltpu.VMEM((flat.shape[0] + 64, LANES), F32)],
        compiler_params=params(16),
        name="update",
    )(flat, head, small, master, moment, average)


def local_exchange(
    block_input,
    seg_ids,
    masked,
    out_grad,
    att_master,
    att_moment,
    att_average,
    ffn_master,
    ffn_moment,
    ffn_average,
):
    tok, width = block_input.shape
    seq_count, seq = seg_ids.shape
    devices = lax.axis_size("fsdp")
    up = [(i, i + 1) for i in range(devices - 1)]
    down = [(i + 1, i) for i in range(devices - 1)]
    tails = lax.ppermute(jnp.concatenate([att_master[-64:], ffn_master[-64:]]), "fsdp", up)
    masked_col = masked.reshape(tok, 1)
    seg_col = seg_ids.reshape(tok, 1)
    seg_row = seg_ids.reshape(seq_count, 1, seq)
    att_chunk, small_chunk, chunk_a, chunk_b = prepare(att_master, ffn_master, tails, devices, width)
    att = jnp.concatenate([att_chunk, small_chunk])
    got, masked_col, seg_col, seg_row = phase(exchange(att, 0), masked_col, seg_col, seg_row)
    att = widen_small(att, got)
    got = exchange(att, 1)
    att, unit_a = phase(widen_small(att, got), chunk_a)
    got, got_a = phase(exchange(att, 2), exchange(unit_a, 0))
    att, unit_a, unit_b = phase(widen_small(att, got), widen(unit_a, got_a), chunk_b)
    att_next, att_far, got_a, got_b = phase(
        exchange(att, 3), exchange(att, 4), exchange(unit_a, 1), exchange(unit_b, 0)
    )
    unit_a, unit_b, att_next = phase(widen(unit_a, got_a), widen(unit_b, got_b), att_next)
    att_last, got_b, block_input = phase(exchange(att_next, 4), exchange(unit_b, 2), block_input)
    att = (att, att_next, att_far, att_last)
    unit_a, unit_b, block_input = phase(unit_a, widen(unit_b, got_b), block_input)
    got_b = exchange(unit_b, 1)
    stream, q, k, v, small = project(block_input, masked_col, att)
    got_a, q = phase(exchange(unit_a, 2), q)
    unit_a, q = phase(widen(unit_a, got_a), q)
    held = attention_forward(0, q, k, v, seg_col, seg_row)
    a_next, a_far, got_b, held = phase(exchange(unit_a, 3), exchange(unit_a, 4), got_b, held)
    unit_b, a_next, held = phase(widen(unit_b, got_b), a_next, held)
    ctx, lse = attention_forward(1, q, k, v, seg_col, seg_row, held)
    b_next, b_far, a_last, ctx = phase(
        exchange(unit_b, 3), exchange(unit_b, 4), exchange(a_next, 4), ctx
    )
    b_last = exchange(b_next, 4)
    block_output, x_low, hidden, dhid, dfb, dpre, dob, dctx, sums = feed_forward(
        stream,
        ctx,
        out_grad,
        small,
        att,
        (unit_a, a_next, a_far, a_last),
        (unit_b, b_next, b_far, b_last),
    )
    part_a, part_b = ffn_grads(x_low, hidden, dhid, dfb, sums)
    part_b, dhid = phase(part_b, dhid)
    part_a = ffn_rest(x_low, dhid, part_a)
    high_b, low_b, part_a = phase(exchange(part_b[3], 4), exchange(part_b[2], 4), part_a)
    small_sum = sums + high_b[8 * SLOT :].astype(F32)
    high_b = add_small(total_of((part_b[1], high_b), 0, 8 * SLOT).astype(BF), small_sum)
    high_b, part_a, dctx = phase(high_b, part_a, dctx)
    held = attention_backward(0, q, k, v, dctx, lse, seg_col, seg_row)
    got_b, high_a, low_a, held = phase(
        exchange(high_b, 3), exchange(part_a[3], 4), exchange(part_a[2], 4), held
    )
    high_a = total_of((part_a[1], high_a), 0, 8 * SLOT).astype(BF)
    small_sum = small_sum + got_b[8 * SLOT :].astype(F32)
    kept_b, sent_b = halve(part_b[0], low_b, got_b[: 8 * SLOT])
    high_a, sent_b, held = phase(high_a, add_small(sent_b, small_sum), held)
    dq, dk, dv = attention_backward(1, q, k, v, dctx, lse, seg_col, seg_row, held)
    got_a, got_b, dq = phase(exchange(high_a, 3), exchange(sent_b, 1), dq)
    kept_a, sent_a = halve(part_a[0], low_a, got_a)
    small_sum = small_sum + got_b[4 * SLOT :].astype(F32)
    kept_b, sent_b = halve(kept_b, got_b[: 4 * SLOT])
    sent_a, sent_b, dq = phase(sent_a, add_small(sent_b, small_sum), dq)
    part = att_grads(ctx, dob, stream, dq, dk, dv)
    got_a, got_b, part = phase(exchange(sent_a, 2), exchange(sent_b, 2), part)
    kept_a, sent_a = halve(kept_a, got_a)
    small_sum = small_sum + got_b[2 * SLOT :].astype(F32)
    kept_b, sent_b = halve(kept_b, got_b[: 2 * SLOT])
    sent_a, sent_b, part = phase(sent_a, add_small(sent_b, small_sum), part)
    got_b = exchange(sent_b, 0)
    high = exchange(part[3], 4)
    high = total_of((part[1], high), 0, 8 * SLOT).astype(BF)
    high, sent_a, dq = phase(high, sent_a, dq)
    input_grad, late = input_grads(dq, dk, dv, dpre, masked_col, att)
    got, low, got_a, got_b, late = phase(
        exchange(high, 3), exchange(part[2], 4), exchange(sent_a, 1), got_b, late
    )
    kept, sent = halve(part[0], low, got)
    kept_a, sent_a = halve(kept_a, got_a)
    sent, sent_a, late = phase(sent, sent_a, late)
    got, got_a, got_late = phase(exchange(sent, 2), exchange(sent_a, 0), exchange(late.astype(BF), 4))
    kept, sent = halve(kept, got)
    late = late + got_late.astype(F32)
    sent, late, got_a = phase(sent, late, got_a)
    got = exchange(sent, 1)
    late = late + exchange(late.astype(BF), 2).astype(F32)
    late = late + exchange(late.astype(BF), 3).astype(F32)
    small_sum = small_sum + got_b[SLOT:].astype(F32)
    grad_a = total_of((kept_a, got_a), 0, SLOT)
    grad_b = total_of((kept_b, got_b), 0, SLOT)
    ffn_flat = flatten(flat_ffn_kernel, 12 * SLOT, grad_a, grad_b)
    kept, sent = halve(kept, got)
    sent, late, ffn_flat, small_sum = phase(sent, late, ffn_flat, small_sum)
    got = exchange(sent, 0)
    late = late + exchange(late.astype(BF), 1).astype(F32)
    ffn_head = lax.ppermute(ffn_flat[:64], "fsdp", down)
    got, late, ffn_head = phase(got, late, ffn_head)
    grad_att = total_of((kept, got), 0, SLOT)
    att_flat = flatten(flat_att_kernel, 6 * SLOT, grad_att)
    att_head = lax.ppermute(att_flat[:64], "fsdp", down)
    late = late + exchange(late.astype(BF), 0).astype(F32)
    rate = 0.05 / math.sqrt(tok * devices)
    ffn_new = update(
        ffn_flat, ffn_head, small_sum, (6, 7), rate, devices, ffn_master, ffn_moment, ffn_average
    )
    att_head, late, ffn_new = phase(att_head, late, ffn_new)
    small_total = small_sum + late
    att_new = update(
        att_flat, att_head, small_total, (0, 6), rate, devices, att_master, att_moment, att_average
    )
    return (block_output, input_grad) + tuple(att_new) + tuple(ffn_new)


def chunked(mesh):
    return mesh.shape["fsdp"] == 32


def solution(mesh):
    in_specs = (
        P("fsdp", None),
        P("fsdp", None),
        P("fsdp", None),
        P("fsdp", None),
        P("fsdp", None),
        P("fsdp", None),
        P("fsdp", None),
        P("fsdp", None),
        P("fsdp", None),
        P("fsdp", None),
    )
    out_specs = (
        P("fsdp", None),
        P("fsdp", None),
        P("fsdp", None),
        P("fsdp", None),
        P("fsdp", None),
        P("fsdp", None),
        P("fsdp", None),
        P("fsdp", None),
        P("fsdp", None),
        P("fsdp", None),
    )
    body = local_exchange if chunked(mesh) else local
    return jax.shard_map(body, mesh=mesh, in_specs=in_specs, out_specs=out_specs, check_vma=False)
```

```python
import functools
import math

import jax
import jax.numpy as jnp
from jax import lax
from jax.experimental import pallas as pl
from jax.experimental.pallas import tpu as pltpu
from jax.sharding import PartitionSpec as P

HEAD_DIM = 64
FF = 3072


EPSILON = 1e-05
MASKED_SCORE = -1e30


def layer_norm(pre_norm, gain, shift):
    center = pre_norm - jnp.mean(pre_norm, axis=-1, keepdims=True)
    spread = jnp.mean(center * center, axis=-1, keepdims=True)
    return center * lax.rsqrt(spread + EPSILON) * gain + shift


def gelu_exact(inputs):
    return jax.nn.gelu(inputs, approximate=False)


def unpack_attention(flat_att, model_width):
    square = model_width * model_width
    att_mats = flat_att[: 4 * square].reshape(4, model_width, model_width)
    small_params = flat_att[4 * square : 4 * square + 6 * model_width].reshape(6, model_width)
    return (att_mats, small_params)


def unpack_ffn(flat_ffn, model_width, hidden):
    size_in = model_width * hidden
    weight_in = flat_ffn[:size_in].reshape(model_width, hidden)
    weight_out = flat_ffn[size_in : 2 * size_in].reshape(hidden, model_width)
    offset = 2 * size_in
    bias_in = flat_ffn[offset : offset + hidden]
    small_params = flat_ffn[offset + hidden : offset + hidden + 3 * model_width].reshape(
        3, model_width
    )
    return (weight_in, weight_out, bias_in, small_params)


def pack_rows(pieces, row_count):
    filled = sum((piece.shape[0] for piece in pieces))
    padding = jnp.zeros((row_count * 128 - filled,), jnp.float32)
    return jnp.concatenate(list(pieces) + [padding]).reshape(row_count, 128)


def attend_forward(block_items):
    query_block, key_block, value_block, doc_block = block_items
    scores = jnp.einsum("qhd,khd->hqk", query_block, key_block, preferred_element_type=jnp.float32)
    same_doc = doc_block[:, None] == doc_block[None, :]
    scores = jnp.where(same_doc[None], scores, MASKED_SCORE)
    row_max = jnp.max(scores, axis=-1, keepdims=True)
    exponent = jnp.exp(scores - row_max)
    row_total = jnp.sum(exponent, axis=-1, keepdims=True)
    attn_probs = (exponent / row_total).astype(jnp.bfloat16)
    context = jnp.einsum(
        "hqk,khd->qhd", attn_probs, value_block, preferred_element_type=jnp.float32
    )
    return (context.astype(jnp.bfloat16), (row_max + jnp.log(row_total))[..., 0])


def attend_backward(block_items):
    query_block, key_block, value_block, doc_block, log_total, grad_context = block_items
    scores = jnp.einsum("qhd,khd->hqk", query_block, key_block, preferred_element_type=jnp.float32)
    same_doc = doc_block[:, None] == doc_block[None, :]
    scores = jnp.where(same_doc[None], scores, MASKED_SCORE)
    attn_probs = jnp.exp(scores - log_total[..., None])
    probs_low = attn_probs.astype(jnp.bfloat16)
    grad_probs = jnp.einsum(
        "qhd,khd->hqk", grad_context, value_block, preferred_element_type=jnp.float32
    )
    row_inner = jnp.sum(grad_probs * attn_probs, axis=-1, keepdims=True)
    grad_scores = (attn_probs * (grad_probs - row_inner)).astype(jnp.bfloat16)
    grad_query = jnp.einsum(
        "hqk,khd->qhd", grad_scores, key_block, preferred_element_type=jnp.float32
    ).astype(jnp.bfloat16)
    grad_key = jnp.einsum(
        "hqk,qhd->khd", grad_scores, query_block, preferred_element_type=jnp.float32
    ).astype(jnp.bfloat16)
    grad_value = jnp.einsum(
        "hqk,qhd->khd", probs_low, grad_context, preferred_element_type=jnp.float32
    ).astype(jnp.bfloat16)
    return (grad_query, grad_key, grad_value)


def nesterov(master, moment, average, gradient, step_rate):
    moment_new = 0.5 * moment + gradient
    master_new = master - step_rate * (gradient + 0.5 * moment_new)
    average_new = 0.5 * average + 0.5 * master_new
    return (master_new, moment_new, average_new, master_new.astype(jnp.bfloat16))


def local(
    block_input,
    seg_ids,
    masked,
    out_grad,
    att_master,
    att_moment,
    att_average,
    ffn_master,
    ffn_moment,
    ffn_average,
):
    tok_rows, model_width = block_input.shape
    seq_count, seq_length = seg_ids.shape
    head_count = model_width // HEAD_DIM
    devices = lax.axis_size("fsdp")
    att_rows = att_master.shape[0] * devices
    ffn_rows = ffn_master.shape[0] * devices
    head_shape = (seq_count, seq_length, head_count, HEAD_DIM)
    att_whole = lax.all_gather(att_master.astype(jnp.bfloat16), "fsdp", axis=0, tiled=True)
    att_mats, att_small_low = unpack_attention(att_whole.reshape(-1), model_width)
    att_small = att_small_low.astype(jnp.float32)
    masked_rows = masked.reshape(tok_rows, 1) == 1
    stream_in = jnp.where(masked_rows, att_small[5][None, :], block_input.astype(jnp.float32))
    stream_low = stream_in.astype(jnp.bfloat16)
    projected = jnp.einsum(
        "td,cde->cte", stream_low, att_mats[:3], preferred_element_type=jnp.float32
    )
    queries = ((projected[0] + att_small[0]) * 0.125).astype(jnp.bfloat16).reshape(head_shape)
    key_rows = projected[1].astype(jnp.bfloat16).reshape(head_shape)
    values = (projected[2] + att_small[1]).astype(jnp.bfloat16).reshape(head_shape)
    context, log_total = lax.map(attend_forward, (queries, key_rows, values, seg_ids))
    context_flat = context.reshape(tok_rows, model_width)
    pre_one = (
        stream_in
        + jnp.dot(context_flat, att_mats[3], preferred_element_type=jnp.float32)
        + att_small[2]
    )
    normed_one = layer_norm(pre_one, att_small[3], att_small[4])
    normed_low = normed_one.astype(jnp.bfloat16)
    ffn_whole = lax.all_gather(ffn_master.astype(jnp.bfloat16), "fsdp", axis=0, tiled=True)
    weight_in, weight_out, bias_in_low, ffn_small_low = unpack_ffn(
        ffn_whole.reshape(-1), model_width, FF
    )
    bias_in = bias_in_low.astype(jnp.float32)
    ffn_small = ffn_small_low.astype(jnp.float32)
    hid_pre = jnp.dot(normed_low, weight_in, preferred_element_type=jnp.float32) + bias_in
    hid_act = gelu_exact(hid_pre).astype(jnp.bfloat16)
    pre_two = (
        normed_one + jnp.dot(hid_act, weight_out, preferred_element_type=jnp.float32) + ffn_small[0]
    )
    normed_two, norm_two_pull = jax.vjp(layer_norm, pre_two, ffn_small[1], ffn_small[2])
    block_output = normed_two.astype(jnp.bfloat16)
    ffn_back = lax.all_gather(ffn_master.astype(jnp.bfloat16), "fsdp", axis=0, tiled=True)
    back_in, back_out, bias_unused, small_unused = unpack_ffn(ffn_back.reshape(-1), model_width, FF)
    grad_pre_two, grad_gain_two, grad_shift_two = norm_two_pull(out_grad.astype(jnp.float32))
    grad_branch_two = grad_pre_two.astype(jnp.bfloat16)
    grad_w_out = jnp.einsum(
        "tf,td->fd", hid_act, grad_branch_two, preferred_element_type=jnp.float32
    )
    grad_b_out = jnp.sum(grad_branch_two, axis=0, dtype=jnp.float32)
    grad_act = jnp.einsum(
        "td,fd->tf", grad_branch_two, back_out, preferred_element_type=jnp.float32
    )
    hid_unused, gelu_pull = jax.vjp(gelu_exact, hid_pre)
    grad_hidden = gelu_pull(grad_act)[0].astype(jnp.bfloat16)
    grad_w_in = jnp.einsum("td,tf->df", normed_low, grad_hidden, preferred_element_type=jnp.float32)
    grad_b_in = jnp.sum(grad_hidden, axis=0, dtype=jnp.float32)
    grad_normed_one = grad_pre_two + jnp.einsum(
        "tf,df->td", grad_hidden, back_in, preferred_element_type=jnp.float32
    )
    ffn_flat_grad = pack_rows(
        (
            grad_w_in.reshape(-1),
            grad_w_out.reshape(-1),
            grad_b_in,
            grad_b_out,
            grad_gain_two,
            grad_shift_two,
        ),
        ffn_rows,
    )
    ffn_grad = lax.psum_scatter(ffn_flat_grad, "fsdp", scatter_dimension=0, tiled=True)
    att_back = lax.all_gather(att_master.astype(jnp.bfloat16), "fsdp", axis=0, tiled=True)
    back_mats, small_back = unpack_attention(att_back.reshape(-1), model_width)
    pre_unused, norm_one_pull = jax.vjp(layer_norm, pre_one, att_small[3], att_small[4])
    grad_pre_one, grad_gain_one, grad_shift_one = norm_one_pull(grad_normed_one)
    grad_branch_one = grad_pre_one.astype(jnp.bfloat16)
    grad_w_o = jnp.einsum(
        "td,te->de", context_flat, grad_branch_one, preferred_element_type=jnp.float32
    )
    grad_b_o = jnp.sum(grad_branch_one, axis=0, dtype=jnp.float32)
    grad_context = jnp.einsum(
        "te,de->td", grad_branch_one, back_mats[3], preferred_element_type=jnp.float32
    ).astype(jnp.bfloat16)
    grad_q4, grad_k4, grad_v4 = lax.map(
        attend_backward,
        (queries, key_rows, values, seg_ids, log_total, grad_context.reshape(head_shape)),
    )
    grad_queries = grad_q4.reshape(tok_rows, model_width) * 0.125
    grad_keys = grad_k4.reshape(tok_rows, model_width)
    grad_values = grad_v4.reshape(tok_rows, model_width)
    grad_projected = jnp.stack([grad_queries, grad_keys, grad_values])
    grad_w_qkv = jnp.einsum(
        "td,cte->cde", stream_low, grad_projected, preferred_element_type=jnp.float32
    )
    grad_b_q = jnp.sum(grad_queries, axis=0, dtype=jnp.float32)
    grad_b_v = jnp.sum(grad_values, axis=0, dtype=jnp.float32)
    grad_stream = grad_pre_one + jnp.einsum(
        "cte,cde->td", grad_projected, back_mats[:3], preferred_element_type=jnp.float32
    )
    grad_mask_vector = jnp.sum(jnp.where(masked_rows, grad_stream, 0.0), axis=0)
    input_grad = jnp.where(masked_rows, 0.0, grad_stream)
    att_flat_grad = pack_rows(
        (
            grad_w_qkv.reshape(-1),
            grad_w_o.reshape(-1),
            grad_b_q,
            grad_b_v,
            grad_b_o,
            grad_gain_one,
            grad_shift_one,
            grad_mask_vector,
        ),
        att_rows,
    )
    att_grad = lax.psum_scatter(att_flat_grad, "fsdp", scatter_dimension=0, tiled=True)
    step_rate = 0.05 / math.sqrt(tok_rows * devices)
    att_new = nesterov(att_master, att_moment, att_average, att_grad, step_rate)
    ffn_new = nesterov(ffn_master, ffn_moment, ffn_average, ffn_grad, step_rate)
    return (
        block_output,
        input_grad,
        att_new[0],
        att_new[1],
        att_new[2],
        att_new[3],
        ffn_new[0],
        ffn_new[1],
        ffn_new[2],
        ffn_new[3],
    )


BF = jnp.bfloat16
F32 = jnp.float32
LANES = 128
SLOT = 96
TILE = 256
FFN_TILE = 512
FFN_SPLIT = 2
PAIRS = 2
EXTRA = 16
MIB = 1 << 20
BIG = 58


def params(limit):
    return pltpu.CompilerParams(vmem_limit_bytes=limit * MIB)


def spec_any():
    return pl.BlockSpec(memory_space=pl.ANY)


def spec_vmem():
    return pl.BlockSpec(memory_space=pltpu.VMEM)


def spec_whole(shape):
    return pl.BlockSpec(shape, lambda *ids: (0,) * len(shape))


def dot_nn(left, right):
    return lax.dot_general(left, right, (((1,), (0,)), ((), ())), preferred_element_type=F32)


def dot_nt(left, right):
    return lax.dot_general(left, right, (((1,), (1,)), ((), ())), preferred_element_type=F32)


def dot_tn(left, right):
    return lax.dot_general(left, right, (((0,), (0,)), ((), ())), preferred_element_type=F32)


def slot_of(chunk, me, late=False):
    diff = lax.bitwise_xor(me, chunk)
    far_core = lax.bitwise_and(diff, 1)
    x_bit = lax.bitwise_and(lax.shift_right_logical(diff, 1), 1)
    y_bit = lax.bitwise_and(lax.shift_right_logical(diff, 2), 1)
    z_low = lax.bitwise_and(lax.shift_right_logical(diff, 3), 1)
    z_high = lax.shift_right_logical(diff, 4)
    core = lax.bitwise_xor(lax.bitwise_and(me, 1), far_core)
    third = x_bit + core * (y_bit - x_bit)
    fourth = y_bit + core * (x_bit - y_bit)
    if late:
        return far_core, z_high + 2 * third + 4 * z_low + 8 * fourth
    return far_core, z_high + 2 * z_low + 4 * third + 8 * fourth


def bit(value, place):
    return lax.bitwise_and(lax.shift_right_logical(value, place), 1)


def chunk_of(part, slot, me, late=False):
    third, z_low = (bit(slot, 1), bit(slot, 2)) if late else (bit(slot, 2), bit(slot, 1))
    far_core, fourth = part >> 1, part & 1
    rest = far_core + 8 * z_low + 16 * bit(slot, 0)
    first_core = rest + 2 * third + 4 * fourth
    other_core = rest + 4 * third + 2 * fourth
    core = lax.bitwise_xor(bit(me, 0), far_core)
    return lax.bitwise_xor(me, first_core + core * (other_core - first_core))


def stage_perm(stage):
    if stage == 0:
        return [(i, i ^ 16) for i in range(32)]
    if stage == 1:
        return [(i, i ^ 8) for i in range(32)]
    if stage == 2:
        return [(i, i ^ (4 if i & 1 else 2)) for i in range(32)]
    if stage == 3:
        return [(i, i ^ (2 if i & 1 else 4)) for i in range(32)]
    return [(i, i ^ 1) for i in range(32)]


def exchange(array, stage):
    return lax.ppermute(array, "fsdp", stage_perm(stage))


def widen(held, got):
    return jnp.concatenate([held, got])


def widen_small(held, got):
    low = held.shape[0] - EXTRA
    small = held[low:] + got[low:]
    return jnp.concatenate([held[:low], got[:low], small])


def total_of(arrays, first, last):
    total = arrays[0][first:last].astype(F32)
    for array in arrays[1:]:
        total = total + array[first:last].astype(F32)
    return total


def halve(*arrays):
    rows = arrays[0].shape[0]
    low = total_of(arrays, 0, rows // 2).astype(BF)
    return low, total_of(arrays, rows // 2, rows).astype(BF)


def add_small(values, small):
    return jnp.concatenate([values, small.astype(BF)])


def phase(*values):
    return lax.optimization_barrier(values)


def tail_kernel(att_ref, ffn_ref, out_ref, buf, sems):
    refs = (att_ref, ffn_ref)
    starts = [(ref.shape[0] - 64) // 8 * 8 for ref in refs]
    copies = []
    for number in range(2):
        rows = refs[number].shape[0] - starts[number]
        src = refs[number].at[starts[number] :, :]
        copies.append(pltpu.make_async_copy(src, buf.at[number, 0:rows, :], sems.at[number]))
        copies[number].start()
    for number in range(2):
        rows = refs[number].shape[0] - starts[number]
        copies[number].wait()
        out_ref[number * 64 : number * 64 + 64, :] = buf[number, rows - 64 : rows, :]


def row_tails(att_master, ffn_master):
    return pl.pallas_call(
        tail_kernel,
        out_shape=jax.ShapeDtypeStruct((128, LANES), F32),
        in_specs=[spec_any()] * 2,
        out_specs=spec_vmem(),
        scratch_shapes=[pltpu.VMEM((2, 72, LANES), F32), pltpu.SemaphoreType.DMA((2,))],
        compiler_params=params(BIG),
        name="row_tails",
    )(att_master, ffn_master)


def prep_kernel(last, att_mats, ffn_mats, att_ref, ffn_ref, tail_ref, *refs):
    att_out, ffn_a, ffn_b, att_buf, ffn_buf = refs
    me = lax.axis_index("fsdp")
    att_rows = att_ref.shape[0]
    ffn_rows = ffn_ref.shape[0]
    att_buf[0:64, :] = tail_ref[0:64, :]
    att_buf[64 : 64 + att_rows, :] = att_ref[...]
    ffn_buf[0:64, :] = tail_ref[64:128, :]
    ffn_buf[64 : 64 + ffn_rows, :] = ffn_ref[...]
    start = 64 - 2 * me
    for part in range(6):
        cols = slice(part * LANES, (part + 1) * LANES)
        att_out[0:SLOT, cols] = att_buf[pl.ds(start + part, SLOT, stride=6), :].astype(BF)
    att_out[SLOT:, :] = jnp.zeros((EXTRA, att_out.shape[1]), BF)
    first = me < 16

    @pl.when(first)
    def _():
        for block in range(4):
            out = ffn_a if block < 2 else ffn_b
            rows = slice((block % 2) * 48, (block % 2) * 48 + 48)
            for part in range(6):
                cols = slice(part * LANES, (part + 1) * LANES)
                piece = ffn_buf[pl.ds(start + 6 * block + part, 48, stride=24), :]
                out[rows, cols] = piece.astype(BF)

    @pl.when(jnp.logical_not(first))
    def _():
        for part in range(6):
            cols = slice(part * LANES, (part + 1) * LANES)
            ffn_a[:, cols] = ffn_buf[pl.ds(start + part, SLOT, stride=6), :].astype(BF)
            ffn_b[:, cols] = ffn_buf[pl.ds(start + 6 * SLOT + part, SLOT, stride=6), :].astype(BF)

    @pl.when(me == last)
    def _():
        att_at = 64 + att_mats - last * att_rows
        ffn_at = 64 + ffn_mats - last * ffn_rows
        for part in range(6):
            cols = slice(part * LANES, (part + 1) * LANES)
            upper = att_buf[pl.ds(att_at + part, 6, stride=6), :]
            lower = ffn_buf[pl.ds(ffn_at + part, 7, stride=6), :]
            both = jnp.concatenate([upper, lower, jnp.zeros((3, LANES), F32)])
            att_out[SLOT:, cols] = both.astype(BF)


def prepare(att_master, ffn_master, tails, devices, width):
    att_mats = 4 * width * width // LANES
    ffn_mats = 2 * width * FF // LANES
    att_rows, ffn_rows = att_master.shape[0], ffn_master.shape[0]
    body = functools.partial(prep_kernel, devices - 1, att_mats, ffn_mats)
    return pl.pallas_call(
        body,
        out_shape=(
            jax.ShapeDtypeStruct((SLOT + EXTRA, width), BF),
            jax.ShapeDtypeStruct((SLOT, width), BF),
            jax.ShapeDtypeStruct((SLOT, width), BF),
        ),
        in_specs=[spec_vmem()] * 3,
        out_specs=(spec_vmem(),) * 3,
        scratch_shapes=[
            pltpu.VMEM((64 + att_rows + 6, LANES), F32),
            pltpu.VMEM((64 + ffn_rows + 6, LANES), F32),
        ],
        compiler_params=params(16),
        name="prep",
    )(att_master, ffn_master, tails)


def pick(index, refs, use):
    for number in range(len(refs)):

        @pl.when(index == number)
        def _():
            use(refs[number])


def each_slot(body):
    def step(slot, carry):
        for part in range(4):
            body(part, slot)
        return carry

    lax.fori_loop(0, 8, step, 0)


def load_projections(quad, dst, sems):
    me = lax.axis_index("fsdp")

    def body(part, slot):
        chunk = chunk_of(part, slot, me)

        @pl.when(chunk < 24)
        def _():
            at = pl.multiple_of(chunk * SLOT, 32)
            src = quad[part].at[pl.ds(pl.multiple_of(slot * SLOT, 32), SLOT), :]
            sem = sems.at[lax.shift_right_logical(chunk, 3)]
            pltpu.make_async_copy(src, dst.at[pl.ds(at, SLOT), :], sem).start()

    each_slot(body)


def load_output(quad, dst, sem):
    me = lax.axis_index("fsdp")
    planes = (1 - bit(me, 4)) + 2 * (1 - bit(me, 3))

    def step(third, carry):
        slot = planes + 4 * third
        for part in range(4):
            at = pl.multiple_of((chunk_of(part, slot, me) - 24) * SLOT, 32)
            src = quad[part].at[pl.ds(pl.multiple_of(slot * SLOT, 32), SLOT), :]
            pltpu.make_async_copy(src, dst.at[pl.ds(at, SLOT), :], sem).start()
        return carry

    lax.fori_loop(0, 2, step, 0)


def load_ffn(quads, w_in, w_out, sem_in, sem_out):
    me = lax.axis_index("fsdp")
    for unit in range(2):

        def body(part, slot):
            chunk = chunk_of(part, slot, me, unit == 1)
            src = quads[unit][part].at[slot]

            @pl.when(chunk < 16)
            def _():
                at = pl.multiple_of(chunk * 48, 16)
                dst = w_in.at[2 * unit : 2 * unit + 2, pl.ds(at, 48), :]
                pltpu.make_async_copy(src, dst, sem_in.at[unit]).start()

            @pl.when(chunk >= 16)
            def _():
                dst = w_out.at[2 * (chunk - 16) + unit]
                pltpu.make_async_copy(src, dst, sem_out).start()

        each_slot(body)


def wait_whole(ref, sem):
    pltpu.make_async_copy(ref, ref, sem).wait()


def as_column(row):
    return jnp.broadcast_to(row.astype(F32), (8, row.shape[1])).T[:, 0:1]


def head_mask(rows):
    lane = lax.broadcasted_iota(jnp.int32, (rows, LANES), 1)
    return lane < HEAD_DIM


def project_kernel(x_ref, masked_ref, *refs):
    quad = refs[0:4]
    stream_ref, q_ref, k_ref, v_ref, small_ref, weights, smalls, sems, small_sem = refs[4:]
    width = x_ref.shape[1]

    @pl.when(pl.program_id(0) == 0)
    def _():
        for part in range(4):
            src = quad[part].at[pl.ds(8 * SLOT, EXTRA), :]
            pltpu.make_async_copy(src, smalls.at[part], small_sem).start()
        load_projections(quad, weights, sems)
        wait_whole(smalls, small_sem)
        total = smalls[0].astype(F32)
        for part in range(1, 4):
            total = total + smalls[part].astype(F32)
        small_ref[...] = total

    small = small_ref[...]
    stream = jnp.where(as_column(masked_ref[0]) == 1.0, small[5:6], x_ref[...].astype(F32)).astype(BF)
    stream_ref[...] = stream
    for matrix in range(3):
        rows = slice(matrix * width, (matrix + 1) * width)

        @pl.when(pl.program_id(0) == 0)
        def _():
            wait_whole(weights.at[rows], sems.at[matrix])

        product = dot_nn(stream, weights[rows])
        if matrix == 0:
            q_ref[...] = ((product + small[0:1]) * 0.125).astype(BF)
        elif matrix == 1:
            k_ref[...] = product.astype(BF)
        else:
            v_ref[...] = (product + small[1:2]).astype(BF)


def project(block_input, masked_row, quad):
    tok, width = block_input.shape
    rows = masked_row.shape[2]
    tile = lambda cols: pl.BlockSpec((rows, cols), lambda s: (s, 0))
    bf = jax.ShapeDtypeStruct((tok, width), BF)
    return pl.pallas_call(
        project_kernel,
        grid=(tok // rows,),
        out_shape=(bf, bf, bf, bf, jax.ShapeDtypeStruct((EXTRA, width), F32)),
        in_specs=[tile(width), pl.BlockSpec((1, 1, rows), lambda s: (s, 0, 0))] + [spec_any()] * 4,
        out_specs=(tile(width),) * 4 + (spec_whole((EXTRA, width)),),
        scratch_shapes=[
            pltpu.VMEM((3 * width, width), BF),
            pltpu.VMEM((4, EXTRA, width), BF),
            pltpu.SemaphoreType.DMA((3,)),
            pltpu.SemaphoreType.DMA,
        ],
        compiler_params=params(BIG),
        cost_estimate=pl.CostEstimate(
            flops=6 * tok * width * width, bytes_accessed=16 * MIB, transcendentals=0
        ),
        name="project",
    )(block_input, masked_row, *quad)


def forward_kernel(held, q_ref, k_ref, v_ref, seg_row_ref, *refs):
    ctx_ref, lse_ref = refs[held:]
    left = head_mask(q_ref.shape[0])
    same = as_column(seg_row_ref[0]) == seg_row_ref[0].astype(F32)
    for pair in range(PAIRS):
        cols = slice(pair * LANES, (pair + 1) * LANES)
        queries = q_ref[:, cols]
        keys = k_ref[:, cols]
        values_t = v_ref[:, cols].T
        outs = []
        for head in range(2):
            keep = left if head == 0 else jnp.logical_not(left)
            own = jnp.where(keep, queries, jnp.zeros_like(queries))
            scores = jnp.where(same, dot_nt(keys, own), MASKED_SCORE)
            top = jnp.max(scores, axis=0, keepdims=True)
            exponent = jnp.exp(scores - top)
            total = jnp.sum(exponent, axis=0, keepdims=True)
            probs = (exponent * (1.0 / total)).astype(BF)
            lse_ref[0, pair, head : head + 1, :] = top + jnp.log(total)
            outs.append(dot_nn(values_t[head * HEAD_DIM : (head + 1) * HEAD_DIM], probs))
        ctx_ref[:, cols] = jnp.concatenate(outs).T.astype(BF)


def sequence_specs(at, seq):
    tile = lambda: pl.BlockSpec((seq, PAIRS * LANES), lambda i: (at, i))
    row = lambda: pl.BlockSpec((1, 1, seq), lambda i: (at, 0, 0))
    stat = lambda: pl.BlockSpec((1, PAIRS, 2, seq), lambda i: (at, i, 0, 0))
    return tile, row, stat


def attention_forward(at, q, k, v, seg_row, held=()):
    tok, width = q.shape
    seq_count, seq = seg_row.shape[0], seg_row.shape[2]
    pairs = width // LANES
    tile, row, stat = sequence_specs(at, seq)
    return pl.pallas_call(
        functools.partial(forward_kernel, len(held)),
        grid=(pairs // PAIRS,),
        out_shape=(
            jax.ShapeDtypeStruct((tok, width), BF),
            jax.ShapeDtypeStruct((seq_count, pairs, 2, seq), F32),
        ),
        in_specs=[tile(), tile(), tile(), row()] + [spec_any() for _ in held],
        out_specs=(tile(), stat()),
        input_output_aliases={4 + i: i for i in range(len(held))},
        compiler_params=params(BIG),
        cost_estimate=pl.CostEstimate(
            flops=16 * seq * seq * width,
            bytes_accessed=4 * MIB,
            transcendentals=seq * seq * width // HEAD_DIM,
        ),
        name="attention_forward",
    )(q, k, v, seg_row, *held)


def norm_stats(pre_norm):
    center = pre_norm - jnp.mean(pre_norm, axis=-1, keepdims=True)
    scale = lax.rsqrt(jnp.mean(center * center, axis=-1, keepdims=True) + EPSILON)
    return center * scale, scale


def norm_back(grad, gain, normed, scale):
    scaled = grad * gain
    mean_one = jnp.mean(scaled, axis=-1, keepdims=True)
    mean_two = jnp.mean(scaled * normed, axis=-1, keepdims=True)
    return scale * (scaled - mean_one - normed * mean_two)


def column_sum(array):
    return jnp.sum(array, axis=0, keepdims=True)


def gelu_pair(inputs):
    phi_cdf = 0.5 + 0.5 * lax.erf(inputs * math.sqrt(0.5))
    density = jnp.exp(inputs * inputs * -0.5) * (1.0 / math.sqrt(2.0 * math.pi))
    return inputs * phi_cdf, phi_cdf + inputs * density


def ffn_kernel(
    stream_ref,
    ctx_ref,
    grad_ref,
    small_ref,
    *refs,
):
    att_quad, quad_a, quad_b = refs[0:4], refs[4:8], refs[8:12]
    y_ref, x1_ref, hid_ref, dhid_ref, dfb_ref, dob_ref, dctx_ref, sums_ref = refs[12:20]
    w_in, w_out, w_o, slope, sem_in, sem_out, sem_o = refs[20:]
    width = ctx_ref.shape[1]
    step = pl.program_id(0)

    @pl.when(step == 0)
    def _():
        load_output(att_quad, w_o, sem_o)
        load_ffn((quad_a, quad_b), w_in, w_out, sem_in, sem_out)
        sums_ref[...] = jnp.zeros_like(sums_ref)
        wait_whole(w_o, sem_o)

    def block_cols(block):
        return slice(block * width, (block + 1) * width)

    def out_rows(block):
        return w_out[8 * block : 8 * block + 8].reshape(width, width)

    @pl.when(step == 0)
    def _():
        wait_whole(w_in.at[0:2], sem_in.at[0])
        wait_whole(w_in.at[2:4], sem_in.at[1])
        wait_whole(w_out, sem_out)

    small = small_ref[...]
    halves = range(FFN_SPLIT)
    size = FFN_TILE // FFN_SPLIT
    rows = [slice(part * size, (part + 1) * size) for part in halves]
    state = [{} for part in halves]

    def first_norm(part):
        own = state[part]
        pre_one = stream_ref[rows[part]].astype(F32) + dot_nn(ctx_ref[rows[part]], w_o[...])
        normed, own["scale"] = norm_stats(pre_one + small[2:3])
        own["normed"] = normed
        x_one = normed * small[3:4] + small[4:5]
        own["x"] = x_one.astype(BF)
        x1_ref[rows[part]] = own["x"]
        own["total"] = x_one + small[10:11]

    def forward(part, block):
        own = state[part]
        product = dot_nn(own["x"], w_in[block])
        hidden, gate = gelu_pair(product + small[6 + block : 7 + block])
        hidden = hidden.astype(BF)
        hid_ref[rows[part], block_cols(block)] = hidden
        slope[block, rows[part]] = gate
        own["total"] = own["total"] + dot_nn(hidden, out_rows(block))

    def second_norm(part):
        own = state[part]
        normed, scale = norm_stats(own["total"])
        y_ref[rows[part]] = (normed * small[11:12] + small[12:13]).astype(BF)
        grad_out = grad_ref[rows[part]].astype(F32)
        grad_two = norm_back(grad_out, small[11:12], normed, scale)
        own["low"] = grad_two.astype(BF)
        own["grad"] = grad_two
        dfb_ref[rows[part]] = own["low"]
        sums_ref[10:11] += column_sum(own["low"].astype(F32))
        sums_ref[11:12] += column_sum(grad_out * normed)
        sums_ref[12:13] += column_sum(grad_out)

    def backward(part, block):
        own = state[part]
        product = dot_nt(own["low"], out_rows(block))
        dhid = (product * slope[block, rows[part]]).astype(BF)
        dhid_ref[rows[part], block_cols(block)] = dhid
        sums_ref[6 + block : 7 + block] += column_sum(dhid.astype(F32))
        own["grad"] = own["grad"] + dot_nt(dhid, w_in[block])

    def last_norm(part):
        own = state[part]
        grad_one = own["grad"]
        sums_ref[3:4] += column_sum(grad_one * own["normed"])
        sums_ref[4:5] += column_sum(grad_one)
        dob = norm_back(grad_one, small[3:4], own["normed"], own["scale"]).astype(BF)
        dob_ref[rows[part]] = dob
        sums_ref[2:3] += column_sum(dob.astype(F32))
        dctx_ref[rows[part]] = dot_nt(dob, w_o[...]).astype(BF)

    for part in halves:
        first_norm(part)
    for block in range(FF // width):
        for part in halves:
            forward(part, block)
    for part in halves:
        second_norm(part)
    for block in range(FF // width):
        for part in halves:
            backward(part, block)
    for part in halves:
        last_norm(part)


def feed_forward(stream, ctx, out_grad, small, att_quad, quad_a, quad_b):
    tok, width = ctx.shape
    slots = (8, 2, 48, width)
    quad_a = [array.reshape(slots) for array in quad_a]
    quad_b = [array.reshape(slots) for array in quad_b]
    tile = lambda cols: pl.BlockSpec((FFN_TILE, cols), lambda i: (i, 0))
    bf = lambda cols: jax.ShapeDtypeStruct((tok, cols), BF)
    return pl.pallas_call(
        ffn_kernel,
        grid=(tok // FFN_TILE,),
        out_shape=(
            bf(width),
            bf(width),
            bf(FF),
            bf(FF),
            bf(width),
            bf(width),
            bf(width),
            jax.ShapeDtypeStruct((EXTRA, width), F32),
        ),
        in_specs=[tile(width)] * 3 + [spec_whole((EXTRA, width))] + [spec_any()] * 12,
        out_specs=(
            tile(width),
            tile(width),
            tile(FF),
            tile(FF),
            tile(width),
            tile(width),
            tile(width),
            spec_whole((EXTRA, width)),
        ),
        scratch_shapes=[
            pltpu.VMEM((FF // width, width, width), BF),
            pltpu.VMEM((FF // SLOT, 2, 48, width), BF),
            pltpu.VMEM((width, width), BF),
            pltpu.VMEM((FF // width, FFN_TILE, width), F32),
            pltpu.SemaphoreType.DMA((2,)),
            pltpu.SemaphoreType.DMA,
            pltpu.SemaphoreType.DMA,
        ],
        compiler_params=params(BIG),
        cost_estimate=pl.CostEstimate(
            flops=8 * tok * width * FF, bytes_accessed=40 * MIB, transcendentals=2 * tok * FF
        ),
        name="feed_forward",
    )(stream, ctx, out_grad, small, *att_quad, *quad_a, *quad_b)


def send_slot(parts, far_core, slot, offset, src, sem):
    at = pl.multiple_of(lax.bitwise_and(slot, 7) * SLOT + offset, 16)

    def copy(ref):
        pltpu.make_async_copy(src, ref.at[pl.ds(at, src.shape[0]), :], sem).start()

    pick(2 * far_core + lax.shift_right_logical(slot, 3), parts, copy)


def part_shapes(width, small):
    rows = [8 * SLOT, 8 * SLOT, 8 * SLOT, 8 * SLOT + (EXTRA if small else 0)]
    return tuple(jax.ShapeDtypeStruct((count, width), BF) for count in rows)


def wait_reuse(stage, sems, buf, step):
    @pl.when(step >= 2)
    def _():
        wait_whole(stage.at[buf], sems.at[buf])


def wait_last(stage, sems, step, steps):
    @pl.when(step == steps - 1)
    def _():
        for buf in range(2):
            wait_whole(stage.at[buf], sems.at[buf])


def send_in_blocks(parts, me, late, part, stage, buf, sem):
    def body(chunk, carry):
        far_core, slot = slot_of(chunk, me, late)
        src = stage.at[buf, pl.ds(pl.multiple_of(chunk * 48, 16), 48)]
        send_slot(parts, far_core, slot, part * 48, src, sem)
        return carry

    lax.fori_loop(0, 16, body, 0)


def ffn_grad_kernel(x_ref, hid_ref, dhid_ref, dfb_ref, sums_ref, *refs):
    parts_a, parts_b = refs[0:4], refs[4:8]
    whole, blocks, stage, small_stage, whole_sem, block_sem, sems, small_sem = refs[8:]
    width = x_ref.shape[1]
    me = lax.axis_index("fsdp")
    step = pl.program_id(0)
    buf = lax.rem(step, 2)
    small_rows = parts_b[3].at[pl.ds(8 * SLOT, EXTRA), :]

    def fetch(index):
        into, sem = blocks.at[lax.rem(index, 2)], block_sem.at[lax.rem(index, 2)]

        def start(ref, block):
            at = pl.multiple_of(block * width, LANES)
            pltpu.make_async_copy(ref.at[:, pl.ds(at, width)], into, sem).start()

        @pl.when(index < 4)
        def _():
            start(hid_ref, index)

        @pl.when(index >= 4)
        def _():
            start(dhid_ref, index - 2)

    @pl.when(step == 0)
    def _():
        pltpu.make_async_copy(dfb_ref, whole.at[0], whole_sem.at[0]).start()
        fetch(step)
        pltpu.make_async_copy(x_ref, whole.at[1], whole_sem.at[1]).start()
        small_stage[...] = sums_ref[...].astype(BF)
        pltpu.make_async_copy(small_stage, small_rows, small_sem).start()
        wait_whole(whole.at[0], whole_sem.at[0])

    @pl.when(step < 5)
    def _():
        fetch(step + 1)

    @pl.when(step == 4)
    def _():
        wait_whole(whole.at[1], whole_sem.at[1])

    wait_whole(blocks.at[buf], block_sem.at[buf])
    wait_reuse(stage, sems, buf, step)

    @pl.when(step < 4)
    def _():
        stage[buf] = dot_tn(blocks[buf], whole[0]).astype(BF)

        def body(chunk, carry):
            for unit in range(2):
                far_core, slot = slot_of(16 + 4 * step + chunk, me, unit == 1)
                at = pl.multiple_of((2 * chunk + unit) * SLOT, 32)
                src = stage.at[buf, pl.ds(at, SLOT)]
                send_slot((parts_a, parts_b)[unit], far_core, slot, 0, src, sems.at[buf])
            return carry

        lax.fori_loop(0, 4, body, 0)

    @pl.when(step >= 4)
    def _():
        stage[buf] = dot_tn(whole[1], blocks[buf]).astype(BF)
        send_in_blocks(parts_b, me, True, step - 4, stage, buf, sems.at[buf])

    @pl.when(step == 5)
    def _():
        wait_whole(small_stage, small_sem)

    wait_last(stage, sems, step, 6)


def ffn_grads(x_low, hidden, dhid, dfb, sums):
    tok, width = x_low.shape
    out = pl.pallas_call(
        ffn_grad_kernel,
        grid=(6,),
        out_shape=part_shapes(width, False) + part_shapes(width, True),
        in_specs=[spec_any()] * 4 + [spec_whole((EXTRA, width))],
        out_specs=(spec_any(),) * 8,
        scratch_shapes=[
            pltpu.VMEM((2, tok, width), BF),
            pltpu.VMEM((2, tok, width), BF),
            pltpu.VMEM((2, width, width), BF),
            pltpu.VMEM((EXTRA, width), BF),
            pltpu.SemaphoreType.DMA((2,)),
            pltpu.SemaphoreType.DMA((2,)),
            pltpu.SemaphoreType.DMA((2,)),
            pltpu.SemaphoreType.DMA,
        ],
        compiler_params=params(BIG),
        cost_estimate=pl.CostEstimate(
            flops=3 * tok * width * FF, bytes_accessed=24 * MIB, transcendentals=0
        ),
        name="ffn_grads",
    )(x_low, hidden, dhid, dfb, sums)
    return out[0:4], out[4:8]


def ffn_rest_kernel(x_ref, dhid_ref, *refs):
    parts = refs[4:8]
    stage, sems = refs[8:]
    me = lax.axis_index("fsdp")
    step = pl.program_id(0)
    stage[step] = dot_tn(x_ref[...], dhid_ref[...]).astype(BF)
    send_in_blocks(parts, me, False, step, stage, step, sems.at[step])
    wait_last(stage, sems, step, 2)


def ffn_rest(x_low, dhid, parts):
    tok, width = x_low.shape
    return pl.pallas_call(
        ffn_rest_kernel,
        grid=(2,),
        out_shape=part_shapes(width, False),
        in_specs=[spec_whole((tok, width)), pl.BlockSpec((tok, width), lambda i: (0, i))]
        + [spec_any()] * 4,
        out_specs=(spec_any(),) * 4,
        input_output_aliases={2 + i: i for i in range(4)},
        scratch_shapes=[pltpu.VMEM((2, width, width), BF), pltpu.SemaphoreType.DMA((2,))],
        compiler_params=params(BIG),
        cost_estimate=pl.CostEstimate(
            flops=tok * width * FF, bytes_accessed=8 * MIB, transcendentals=0
        ),
        name="ffn_rest",
    )(x_low, dhid, *parts)


def backward_kernel(held, q_ref, k_ref, v_ref, dctx_ref, lse_ref, seg_row_ref, *refs):
    dq_ref, dk_ref, dv_ref = refs[held:]
    left = head_mask(q_ref.shape[0])
    same = as_column(seg_row_ref[0]) == seg_row_ref[0].astype(F32)
    heads = 2 * PAIRS
    held_a, held_b, held_c = {}, {}, {}

    def pair_cols(head):
        return slice(head // 2 * LANES, (head // 2 + 1) * LANES)

    def products(head):
        cols = pair_cols(head)
        keep = left if head % 2 == 0 else jnp.logical_not(left)
        own = jnp.where(keep, q_ref[:, cols], jnp.zeros((keep.shape), BF))
        own_grad = jnp.where(keep, dctx_ref[:, cols], jnp.zeros((keep.shape), BF))
        scores = dot_nt(k_ref[:, cols], own)
        held_a[head] = (own, own_grad, scores, dot_nt(v_ref[:, cols], own_grad))

    def softmax_back(head):
        own, own_grad, scores, grad_probs = held_a.pop(head)
        scores = jnp.where(same, scores, MASKED_SCORE)
        probs = jnp.exp(scores - lse_ref[0, head // 2, head % 2 : head % 2 + 1, :])
        inner = jnp.sum(grad_probs * probs, axis=0, keepdims=True)
        grad_scores = (probs * (grad_probs - inner)).astype(BF)
        held_b[head] = (own, own_grad, probs.astype(BF), grad_scores)

    def outputs(head):
        own, own_grad, probs, grad_scores = held_b.pop(head)
        cols = pair_cols(head)
        keys_t = k_ref[:, cols].T[(head % 2) * HEAD_DIM : (head % 2 + 1) * HEAD_DIM]
        grad_q = dot_nn(keys_t, grad_scores)
        grad_k = dot_nn(grad_scores, own)
        grad_v = dot_nn(probs, own_grad)
        if head % 2 == 0:
            held_c[0] = (grad_q, grad_k, grad_v)
            return
        first_q, first_k, first_v = held_c.pop(0)
        both_q = jnp.concatenate([first_q, grad_q]).T
        dq_ref[:, cols] = (both_q.astype(BF) * 0.125).astype(BF)
        dk_ref[:, cols] = (first_k + grad_k).astype(BF)
        dv_ref[:, cols] = (first_v + grad_v).astype(BF)

    for tick in range(heads + 2):
        if tick < heads:
            products(tick)
        if 0 <= tick - 1 < heads:
            softmax_back(tick - 1)
        if tick >= 2:
            outputs(tick - 2)


def attention_backward(at, q, k, v, dctx, lse, seg_row, held=()):
    tok, width = q.shape
    seq = seg_row.shape[2]
    tile, row, stat = sequence_specs(at, seq)
    return pl.pallas_call(
        functools.partial(backward_kernel, len(held)),
        grid=(width // LANES // PAIRS,),
        out_shape=(jax.ShapeDtypeStruct((tok, width), BF),) * 3,
        in_specs=[tile(), tile(), tile(), tile(), stat(), row()]
        + [spec_any() for _ in held],
        out_specs=(tile(), tile(), tile()),
        input_output_aliases={6 + i: i for i in range(len(held))},
        compiler_params=params(BIG),
        cost_estimate=pl.CostEstimate(
            flops=40 * seq * seq * width,
            bytes_accessed=6 * MIB,
            transcendentals=seq * seq * width // HEAD_DIM,
        ),
        name="attention_backward",
    )(q, k, v, dctx, lse, seg_row, *held)


def input_grad_kernel(dq_ref, dk_ref, dv_ref, dob_ref, masked_ref, *refs):
    quad = refs[0:4]
    dx_ref, small_ref, weights, sems = refs[4:]
    width = dq_ref.shape[1]
    step = pl.program_id(0)

    @pl.when(step == 0)
    def _():
        load_projections(quad, weights, sems)
        small_ref[...] = jnp.zeros_like(small_ref)

    grad = dob_ref[...].astype(F32)
    for matrix in range(3):
        rows = slice(matrix * width, (matrix + 1) * width)

        @pl.when(step == 0)
        def _():
            wait_whole(weights.at[rows], sems.at[matrix])

        grad = grad + dot_nt((dq_ref, dk_ref, dv_ref)[matrix][...], weights[rows])
    chosen = as_column(masked_ref[0]) == 1.0
    dx_ref[...] = jnp.where(chosen, 0.0, grad)
    small_ref[0:1] += column_sum(dq_ref[...].astype(F32))
    small_ref[1:2] += column_sum(dv_ref[...].astype(F32))
    small_ref[5:6] += column_sum(jnp.where(chosen, grad, 0.0))


def input_grads(dq, dk, dv, dob, masked_row, quad):
    tok, width = dq.shape
    rows = masked_row.shape[2]
    tile = lambda cols: pl.BlockSpec((rows, cols), lambda i: (i, 0))
    whole = spec_whole((EXTRA, width))
    return pl.pallas_call(
        input_grad_kernel,
        grid=(tok // rows,),
        out_shape=(
            jax.ShapeDtypeStruct((tok, width), F32),
            jax.ShapeDtypeStruct((EXTRA, width), F32),
        ),
        in_specs=[tile(width)] * 4
        + [pl.BlockSpec((1, 1, rows), lambda i: (i, 0, 0))]
        + [spec_any()] * 4,
        out_specs=(tile(width), whole),
        scratch_shapes=[pltpu.VMEM((3 * width, width), BF), pltpu.SemaphoreType.DMA((3,))],
        compiler_params=params(BIG),
        cost_estimate=pl.CostEstimate(
            flops=6 * tok * width * width, bytes_accessed=16 * MIB, transcendentals=0
        ),
        name="input_grads",
    )(dq, dk, dv, dob, masked_row, *quad)


def att_grad_kernel(*refs):
    sources, parts = refs[0:6], refs[6:10]
    held, stage, load_sems, sems = refs[10:]
    me = lax.axis_index("fsdp")
    step = pl.program_id(0)
    buf = lax.rem(step, 2)

    @pl.when(step == 0)
    def _():
        for number in range(6):
            pltpu.make_async_copy(sources[number], held.at[number], load_sems.at[number]).start()

    wait_reuse(stage, sems, buf, step)
    for matrix in range(4):

        @pl.when(step == matrix)
        def _():
            for number in ((0, 1), (2, 3), (4,), (5,))[matrix]:
                wait_whole(held.at[number], load_sems.at[number])
            left = 0 if matrix == 0 else 2
            right = 1 if matrix == 0 else 2 + matrix
            stage[buf] = dot_tn(held[left], held[right]).astype(BF)

    first = lax.rem(step + 3, 4) * 8

    def body(piece, carry):
        far_core, slot = slot_of(first + piece, me)
        src = stage.at[buf, pl.ds(pl.multiple_of(piece * SLOT, 32), SLOT)]
        send_slot(parts, far_core, slot, 0, src, sems.at[buf])
        return carry

    lax.fori_loop(0, 8, body, 0)
    wait_last(stage, sems, step, 4)


def att_grads(ctx, dob, stream, dq, dk, dv):
    tok, width = stream.shape
    return pl.pallas_call(
        att_grad_kernel,
        grid=(4,),
        out_shape=part_shapes(width, False),
        in_specs=[spec_any()] * 6,
        out_specs=(spec_any(),) * 4,
        scratch_shapes=[
            pltpu.VMEM((6, tok, width), BF),
            pltpu.VMEM((2, width, width), BF),
            pltpu.SemaphoreType.DMA((6,)),
            pltpu.SemaphoreType.DMA((2,)),
        ],
        compiler_params=params(BIG),
        cost_estimate=pl.CostEstimate(
            flops=8 * tok * width * width, bytes_accessed=16 * MIB, transcendentals=0
        ),
        name="att_grads",
    )(ctx, dob, stream, dq, dk, dv)


def flat_ffn_kernel(a_ref, b_ref, out_ref):
    first = lax.axis_index("fsdp") < 16

    @pl.when(first)
    def _():
        for block in range(4):
            source = a_ref if block < 2 else b_ref
            rows = slice((block % 2) * 48, (block % 2) * 48 + 48)
            for part in range(6):
                cols = slice(part * LANES, (part + 1) * LANES)
                out_ref[pl.ds(6 * block + part, 48, stride=24), :] = source[rows, cols]

    @pl.when(jnp.logical_not(first))
    def _():
        for part in range(6):
            cols = slice(part * LANES, (part + 1) * LANES)
            out_ref[pl.ds(part, SLOT, stride=6), :] = a_ref[:, cols]
            out_ref[pl.ds(6 * SLOT + part, SLOT, stride=6), :] = b_ref[:, cols]


def flatten_ffn(grad_a, grad_b):
    return pl.pallas_call(
        flat_ffn_kernel,
        out_shape=jax.ShapeDtypeStruct((12 * SLOT, LANES), F32),
        in_specs=[spec_vmem()] * 2,
        out_specs=spec_vmem(),
        compiler_params=params(16),
        name="flatten_ffn",
    )(grad_a, grad_b)


def flat_att_kernel(kept_ref, got_ref, ffn_ref, late_ref, out_ref, head_ref):
    for part in range(6):
        cols = slice(part * LANES, (part + 1) * LANES)
        total = kept_ref[:, cols].astype(F32) + got_ref[0:SLOT, cols].astype(F32)
        out_ref[pl.ds(part, SLOT, stride=6), :] = total
    head_ref[0:64, :] = out_ref[0:64, :]
    head_ref[64:128, :] = ffn_ref[0:64, :]

    @pl.when(lax.axis_index("fsdp") == 0)
    def _():
        for part in range(6):
            cols = slice(part * LANES, (part + 1) * LANES)
            head_ref[pl.ds(part, 6, stride=6), :] = late_ref[0:6, cols]


def flatten_att(kept, got, ffn_flat, late):
    return pl.pallas_call(
        flat_att_kernel,
        out_shape=(
            jax.ShapeDtypeStruct((6 * SLOT, LANES), F32),
            jax.ShapeDtypeStruct((128, LANES), F32),
        ),
        in_specs=[spec_vmem()] * 4,
        out_specs=(spec_vmem(),) * 2,
        compiler_params=params(16),
        name="flatten_att",
    )(kept, got, ffn_flat, late)


def update_kernel(last, rate, *refs):
    inputs, outputs, bufs = refs[0:10], refs[10:18], refs[18:20]
    me = lax.axis_index("fsdp")
    head_ref, small_ref = inputs[2], inputs[3]
    for unit in range(2):
        flat_ref = inputs[unit]
        w_ref, m_ref, a_ref = inputs[4 + 3 * unit : 7 + 3 * unit]
        w_out, m_out, a_out, low_out = outputs[4 * unit : 4 * unit + 4]
        buf = bufs[unit]
        aligned = flat_ref.shape[0]
        first, count = ((0, 6), (6, 7))[unit]
        buf[0:aligned, :] = flat_ref[...]
        buf[aligned : aligned + 64, :] = head_ref[unit * 64 : unit * 64 + 64, :]

        @pl.when(me == last)
        def _():
            buf[aligned : aligned + 64, :] = jnp.zeros((64, LANES), F32)
            for part in range(6):
                cols = slice(part * LANES, (part + 1) * LANES)
                small = small_ref[first : first + count, cols]
                if unit == 0:
                    small = small + head_ref[pl.ds(part, count, stride=6), :]
                buf[pl.ds(aligned + part, count, stride=6), :] = small

        grad = buf[pl.ds(2 * me, w_ref.shape[0]), :]
        moment = 0.5 * m_ref[...] + grad
        master = w_ref[...] - rate * (grad + 0.5 * moment)
        m_out[...] = moment
        w_out[...] = master
        a_out[...] = 0.5 * a_ref[...] + 0.5 * master
        low_out[...] = master.astype(BF)


def update(flats, head, small, rate, devices, att, ffn):
    shapes = []
    for arrays in (att, ffn):
        f32 = jax.ShapeDtypeStruct(arrays[0].shape, F32)
        shapes += [f32, f32, f32, jax.ShapeDtypeStruct(arrays[0].shape, BF)]
    out = pl.pallas_call(
        functools.partial(update_kernel, devices - 1, rate),
        out_shape=tuple(shapes),
        in_specs=[spec_vmem()] * 10,
        out_specs=(spec_vmem(),) * 8,
        scratch_shapes=[pltpu.VMEM((flat.shape[0] + 64, LANES), F32) for flat in flats],
        compiler_params=params(16),
        name="update",
    )(*flats, head, small, *att, *ffn)
    return out


def local_exchange(
    block_input,
    seg_ids,
    masked,
    out_grad,
    att_master,
    att_moment,
    att_average,
    ffn_master,
    ffn_moment,
    ffn_average,
):
    tok, width = block_input.shape
    seq_count, seq = seg_ids.shape
    devices = lax.axis_size("fsdp")
    up = [(i, i + 1) for i in range(devices - 1)]
    down = [(i + 1, i) for i in range(devices - 1)]
    tails = lax.ppermute(row_tails(att_master, ffn_master), "fsdp", up)
    masked_row = masked.reshape(seq_count, 1, seq)
    seg_row = seg_ids.reshape(seq_count, 1, seq)
    att, chunk_a, chunk_b = prepare(att_master, ffn_master, tails, devices, width)
    got, masked_row, seg_row = phase(exchange(att, 0), masked_row, seg_row)
    att = widen_small(att, got)
    got = exchange(att, 1)
    att, unit_a = phase(widen_small(att, got), chunk_a)
    got, got_a = phase(exchange(att, 2), exchange(unit_a, 0))
    att, unit_a, unit_b = phase(widen_small(att, got), widen(unit_a, got_a), chunk_b)
    att_next, att_far, got_a, got_b = phase(
        exchange(att, 3), exchange(att, 4), exchange(unit_a, 1), exchange(unit_b, 0)
    )
    unit_a, unit_b, att_next = phase(widen(unit_a, got_a), widen(unit_b, got_b), att_next)
    att_last, got_b, block_input = phase(exchange(att_next, 4), exchange(unit_b, 2), block_input)
    att = (att, att_next, att_far, att_last)
    unit_a, unit_b, block_input = phase(unit_a, widen(unit_b, got_b), block_input)
    got_b = exchange(unit_b, 1)
    stream, q, k, v, small = project(block_input, masked_row, att)
    got_a, q = phase(exchange(unit_a, 2), q)
    unit_a, q = phase(widen(unit_a, got_a), q)
    held = attention_forward(0, q, k, v, seg_row)
    a_next, a_far, got_b, held = phase(exchange(unit_a, 3), exchange(unit_a, 4), got_b, held)
    unit_b, a_next, held = phase(widen(unit_b, got_b), a_next, held)
    ctx, lse = attention_forward(1, q, k, v, seg_row, held)
    b_next, b_far, a_last, ctx = phase(
        exchange(unit_b, 3), exchange(unit_b, 4), exchange(a_next, 4), ctx
    )
    b_last = exchange(b_next, 4)
    block_output, x_low, hidden, dhid, dfb, dob, dctx, sums = feed_forward(
        stream,
        ctx,
        out_grad,
        small,
        att,
        (unit_a, a_next, a_far, a_last),
        (unit_b, b_next, b_far, b_last),
    )
    part_a, part_b = ffn_grads(x_low, hidden, dhid, dfb, sums)
    part_b, dhid = phase(part_b, dhid)
    part_a = ffn_rest(x_low, dhid, part_a)
    high_b, low_b, part_a = phase(exchange(part_b[3], 4), exchange(part_b[2], 4), part_a)
    small_sum = sums + high_b[8 * SLOT :].astype(F32)
    high_b = add_small(total_of((part_b[1], high_b), 0, 8 * SLOT).astype(BF), small_sum)
    high_b, part_a, dctx = phase(high_b, part_a, dctx)
    held = attention_backward(0, q, k, v, dctx, lse, seg_row)
    got_b, high_a, low_a, held = phase(
        exchange(high_b, 3), exchange(part_a[3], 4), exchange(part_a[2], 4), held
    )
    high_a = total_of((part_a[1], high_a), 0, 8 * SLOT).astype(BF)
    small_sum = small_sum + got_b[8 * SLOT :].astype(F32)
    kept_b, sent_b = halve(part_b[0], low_b, got_b[: 8 * SLOT])
    high_a, sent_b, held = phase(high_a, add_small(sent_b, small_sum), held)
    dq, dk, dv = attention_backward(1, q, k, v, dctx, lse, seg_row, held)
    got_a, got_b, dq = phase(exchange(high_a, 3), exchange(sent_b, 1), dq)
    kept_a, sent_a = halve(part_a[0], low_a, got_a)
    small_sum = small_sum + got_b[4 * SLOT :].astype(F32)
    kept_b, sent_b = halve(kept_b, got_b[: 4 * SLOT])
    sent_a, sent_b, dq = phase(sent_a, add_small(sent_b, small_sum), dq)
    part = att_grads(ctx, dob, stream, dq, dk, dv)
    got_a, got_b, part = phase(exchange(sent_a, 2), exchange(sent_b, 2), part)
    kept_a, sent_a = halve(kept_a, got_a)
    small_sum = small_sum + got_b[2 * SLOT :].astype(F32)
    kept_b, sent_b = halve(kept_b, got_b[: 2 * SLOT])
    sent_a, sent_b, part = phase(sent_a, add_small(sent_b, small_sum), part)
    got_b = exchange(sent_b, 0)
    high = exchange(part[3], 4)
    high = total_of((part[1], high), 0, 8 * SLOT).astype(BF)
    high, sent_a, dq = phase(high, sent_a, dq)
    input_grad, late = input_grads(dq, dk, dv, dob, masked_row, att)
    got, low, got_a, got_b, late = phase(
        exchange(high, 3), exchange(part[2], 4), exchange(sent_a, 1), got_b, late
    )
    kept, sent = halve(part[0], low, got)
    kept_a, sent_a = halve(kept_a, got_a)
    sent, sent_a, late = phase(sent, sent_a, late)
    got, got_a = phase(exchange(add_small(sent, late), 2), exchange(sent_a, 0))
    late = late + got[4 * SLOT :].astype(F32)
    kept, sent = halve(kept, got[: 4 * SLOT])
    sent, late, got_a, got_b = phase(sent, late, got_a, got_b)
    got = exchange(sent, 1)
    late = late + exchange(late.astype(BF), 3).astype(F32)
    late = late + exchange(late.astype(BF), 4).astype(F32)
    kept, sent = halve(kept, got)
    sent, got_a, got_b = phase(add_small(sent, late), got_a, got_b)
    got = exchange(sent, 0)
    small_sum = small_sum + got_b[SLOT:].astype(F32)
    grad_a = total_of((kept_a, got_a), 0, SLOT)
    grad_b = total_of((kept_b, got_b), 0, SLOT)
    ffn_flat = flatten_ffn(grad_a, grad_b)
    got, ffn_flat, small_sum = phase(got, ffn_flat, small_sum)
    late = late + got[SLOT:].astype(F32)
    att_flat, heads = flatten_att(kept, got, ffn_flat, late)
    heads = lax.ppermute(heads, "fsdp", down + [(0, devices - 1)])
    rate = 0.05 / math.sqrt(tok * devices)
    new = update(
        (att_flat, ffn_flat),
        heads,
        small_sum + late,
        rate,
        devices,
        (att_master, att_moment, att_average),
        (ffn_master, ffn_moment, ffn_average),
    )
    return (block_output, input_grad) + tuple(new)


def chunked(mesh):
    return mesh.shape["fsdp"] == 32


def solution(mesh):
    in_specs = (
        P("fsdp", None),
        P("fsdp", None),
        P("fsdp", None),
        P("fsdp", None),
        P("fsdp", None),
        P("fsdp", None),
        P("fsdp", None),
        P("fsdp", None),
        P("fsdp", None),
        P("fsdp", None),
    )
    out_specs = (
        P("fsdp", None),
        P("fsdp", None),
        P("fsdp", None),
        P("fsdp", None),
        P("fsdp", None),
        P("fsdp", None),
        P("fsdp", None),
        P("fsdp", None),
        P("fsdp", None),
        P("fsdp", None),
    )
    body = local_exchange if chunked(mesh) else local
    return jax.shard_map(body, mesh=mesh, in_specs=in_specs, out_specs=out_specs, check_vma=False)
```

```python
import functools
import math

import jax
import jax.numpy as jnp
from jax import lax
from jax.experimental import pallas as pl
from jax.experimental.pallas import tpu as pltpu
from jax.sharding import PartitionSpec as P

HEAD_DIM = 64
FF = 3072


EPSILON = 1e-05
MASKED_SCORE = -1e30


def layer_norm(pre_norm, gain, shift):
    center = pre_norm - jnp.mean(pre_norm, axis=-1, keepdims=True)
    spread = jnp.mean(center * center, axis=-1, keepdims=True)
    return center * lax.rsqrt(spread + EPSILON) * gain + shift


def gelu_exact(inputs):
    return jax.nn.gelu(inputs, approximate=False)


def unpack_attention(flat_att, model_width):
    square = model_width * model_width
    att_mats = flat_att[: 4 * square].reshape(4, model_width, model_width)
    small_params = flat_att[4 * square : 4 * square + 6 * model_width].reshape(6, model_width)
    return (att_mats, small_params)


def unpack_ffn(flat_ffn, model_width, hidden):
    size_in = model_width * hidden
    weight_in = flat_ffn[:size_in].reshape(model_width, hidden)
    weight_out = flat_ffn[size_in : 2 * size_in].reshape(hidden, model_width)
    offset = 2 * size_in
    bias_in = flat_ffn[offset : offset + hidden]
    small_params = flat_ffn[offset + hidden : offset + hidden + 3 * model_width].reshape(
        3, model_width
    )
    return (weight_in, weight_out, bias_in, small_params)


def pack_rows(pieces, row_count):
    filled = sum((piece.shape[0] for piece in pieces))
    padding = jnp.zeros((row_count * 128 - filled,), jnp.float32)
    return jnp.concatenate(list(pieces) + [padding]).reshape(row_count, 128)


def attend_forward(block_items):
    query_block, key_block, value_block, doc_block = block_items
    scores = jnp.einsum("qhd,khd->hqk", query_block, key_block, preferred_element_type=jnp.float32)
    same_doc = doc_block[:, None] == doc_block[None, :]
    scores = jnp.where(same_doc[None], scores, MASKED_SCORE)
    row_max = jnp.max(scores, axis=-1, keepdims=True)
    exponent = jnp.exp(scores - row_max)
    row_total = jnp.sum(exponent, axis=-1, keepdims=True)
    attn_probs = (exponent / row_total).astype(jnp.bfloat16)
    context = jnp.einsum(
        "hqk,khd->qhd", attn_probs, value_block, preferred_element_type=jnp.float32
    )
    return (context.astype(jnp.bfloat16), (row_max + jnp.log(row_total))[..., 0])


def attend_backward(block_items):
    query_block, key_block, value_block, doc_block, log_total, grad_context = block_items
    scores = jnp.einsum("qhd,khd->hqk", query_block, key_block, preferred_element_type=jnp.float32)
    same_doc = doc_block[:, None] == doc_block[None, :]
    scores = jnp.where(same_doc[None], scores, MASKED_SCORE)
    attn_probs = jnp.exp(scores - log_total[..., None])
    probs_low = attn_probs.astype(jnp.bfloat16)
    grad_probs = jnp.einsum(
        "qhd,khd->hqk", grad_context, value_block, preferred_element_type=jnp.float32
    )
    row_inner = jnp.sum(grad_probs * attn_probs, axis=-1, keepdims=True)
    grad_scores = (attn_probs * (grad_probs - row_inner)).astype(jnp.bfloat16)
    grad_query = jnp.einsum(
        "hqk,khd->qhd", grad_scores, key_block, preferred_element_type=jnp.float32
    ).astype(jnp.bfloat16)
    grad_key = jnp.einsum(
        "hqk,qhd->khd", grad_scores, query_block, preferred_element_type=jnp.float32
    ).astype(jnp.bfloat16)
    grad_value = jnp.einsum(
        "hqk,qhd->khd", probs_low, grad_context, preferred_element_type=jnp.float32
    ).astype(jnp.bfloat16)
    return (grad_query, grad_key, grad_value)


def nesterov(master, moment, average, gradient, step_rate):
    moment_new = 0.5 * moment + gradient
    master_new = master - step_rate * (gradient + 0.5 * moment_new)
    average_new = 0.5 * average + 0.5 * master_new
    return (master_new, moment_new, average_new, master_new.astype(jnp.bfloat16))


def local(
    block_input,
    seg_ids,
    masked,
    out_grad,
    att_master,
    att_moment,
    att_average,
    ffn_master,
    ffn_moment,
    ffn_average,
):
    tok_rows, model_width = block_input.shape
    seq_count, seq_length = seg_ids.shape
    head_count = model_width // HEAD_DIM
    devices = lax.axis_size("fsdp")
    att_rows = att_master.shape[0] * devices
    ffn_rows = ffn_master.shape[0] * devices
    head_shape = (seq_count, seq_length, head_count, HEAD_DIM)
    att_whole = lax.all_gather(att_master.astype(jnp.bfloat16), "fsdp", axis=0, tiled=True)
    att_mats, att_small_low = unpack_attention(att_whole.reshape(-1), model_width)
    att_small = att_small_low.astype(jnp.float32)
    masked_rows = masked.reshape(tok_rows, 1) == 1
    stream_in = jnp.where(masked_rows, att_small[5][None, :], block_input.astype(jnp.float32))
    stream_low = stream_in.astype(jnp.bfloat16)
    projected = jnp.einsum(
        "td,cde->cte", stream_low, att_mats[:3], preferred_element_type=jnp.float32
    )
    queries = ((projected[0] + att_small[0]) * 0.125).astype(jnp.bfloat16).reshape(head_shape)
    key_rows = projected[1].astype(jnp.bfloat16).reshape(head_shape)
    values = (projected[2] + att_small[1]).astype(jnp.bfloat16).reshape(head_shape)
    context, log_total = lax.map(attend_forward, (queries, key_rows, values, seg_ids))
    context_flat = context.reshape(tok_rows, model_width)
    pre_one = (
        stream_in
        + jnp.dot(context_flat, att_mats[3], preferred_element_type=jnp.float32)
        + att_small[2]
    )
    normed_one = layer_norm(pre_one, att_small[3], att_small[4])
    normed_low = normed_one.astype(jnp.bfloat16)
    ffn_whole = lax.all_gather(ffn_master.astype(jnp.bfloat16), "fsdp", axis=0, tiled=True)
    weight_in, weight_out, bias_in_low, ffn_small_low = unpack_ffn(
        ffn_whole.reshape(-1), model_width, FF
    )
    bias_in = bias_in_low.astype(jnp.float32)
    ffn_small = ffn_small_low.astype(jnp.float32)
    hid_pre = jnp.dot(normed_low, weight_in, preferred_element_type=jnp.float32) + bias_in
    hid_act = gelu_exact(hid_pre).astype(jnp.bfloat16)
    pre_two = (
        normed_one + jnp.dot(hid_act, weight_out, preferred_element_type=jnp.float32) + ffn_small[0]
    )
    normed_two, norm_two_pull = jax.vjp(layer_norm, pre_two, ffn_small[1], ffn_small[2])
    block_output = normed_two.astype(jnp.bfloat16)
    ffn_back = lax.all_gather(ffn_master.astype(jnp.bfloat16), "fsdp", axis=0, tiled=True)
    back_in, back_out, bias_unused, small_unused = unpack_ffn(ffn_back.reshape(-1), model_width, FF)
    grad_pre_two, grad_gain_two, grad_shift_two = norm_two_pull(out_grad.astype(jnp.float32))
    grad_branch_two = grad_pre_two.astype(jnp.bfloat16)
    grad_w_out = jnp.einsum(
        "tf,td->fd", hid_act, grad_branch_two, preferred_element_type=jnp.float32
    )
    grad_b_out = jnp.sum(grad_branch_two, axis=0, dtype=jnp.float32)
    grad_act = jnp.einsum(
        "td,fd->tf", grad_branch_two, back_out, preferred_element_type=jnp.float32
    )
    hid_unused, gelu_pull = jax.vjp(gelu_exact, hid_pre)
    grad_hidden = gelu_pull(grad_act)[0].astype(jnp.bfloat16)
    grad_w_in = jnp.einsum("td,tf->df", normed_low, grad_hidden, preferred_element_type=jnp.float32)
    grad_b_in = jnp.sum(grad_hidden, axis=0, dtype=jnp.float32)
    grad_normed_one = grad_pre_two + jnp.einsum(
        "tf,df->td", grad_hidden, back_in, preferred_element_type=jnp.float32
    )
    ffn_flat_grad = pack_rows(
        (
            grad_w_in.reshape(-1),
            grad_w_out.reshape(-1),
            grad_b_in,
            grad_b_out,
            grad_gain_two,
            grad_shift_two,
        ),
        ffn_rows,
    )
    ffn_grad = lax.psum_scatter(ffn_flat_grad, "fsdp", scatter_dimension=0, tiled=True)
    att_back = lax.all_gather(att_master.astype(jnp.bfloat16), "fsdp", axis=0, tiled=True)
    back_mats, small_back = unpack_attention(att_back.reshape(-1), model_width)
    pre_unused, norm_one_pull = jax.vjp(layer_norm, pre_one, att_small[3], att_small[4])
    grad_pre_one, grad_gain_one, grad_shift_one = norm_one_pull(grad_normed_one)
    grad_branch_one = grad_pre_one.astype(jnp.bfloat16)
    grad_w_o = jnp.einsum(
        "td,te->de", context_flat, grad_branch_one, preferred_element_type=jnp.float32
    )
    grad_b_o = jnp.sum(grad_branch_one, axis=0, dtype=jnp.float32)
    grad_context = jnp.einsum(
        "te,de->td", grad_branch_one, back_mats[3], preferred_element_type=jnp.float32
    ).astype(jnp.bfloat16)
    grad_q4, grad_k4, grad_v4 = lax.map(
        attend_backward,
        (queries, key_rows, values, seg_ids, log_total, grad_context.reshape(head_shape)),
    )
    grad_queries = grad_q4.reshape(tok_rows, model_width) * 0.125
    grad_keys = grad_k4.reshape(tok_rows, model_width)
    grad_values = grad_v4.reshape(tok_rows, model_width)
    grad_projected = jnp.stack([grad_queries, grad_keys, grad_values])
    grad_w_qkv = jnp.einsum(
        "td,cte->cde", stream_low, grad_projected, preferred_element_type=jnp.float32
    )
    grad_b_q = jnp.sum(grad_queries, axis=0, dtype=jnp.float32)
    grad_b_v = jnp.sum(grad_values, axis=0, dtype=jnp.float32)
    grad_stream = grad_pre_one + jnp.einsum(
        "cte,cde->td", grad_projected, back_mats[:3], preferred_element_type=jnp.float32
    )
    grad_mask_vector = jnp.sum(jnp.where(masked_rows, grad_stream, 0.0), axis=0)
    input_grad = jnp.where(masked_rows, 0.0, grad_stream)
    att_flat_grad = pack_rows(
        (
            grad_w_qkv.reshape(-1),
            grad_w_o.reshape(-1),
            grad_b_q,
            grad_b_v,
            grad_b_o,
            grad_gain_one,
            grad_shift_one,
            grad_mask_vector,
        ),
        att_rows,
    )
    att_grad = lax.psum_scatter(att_flat_grad, "fsdp", scatter_dimension=0, tiled=True)
    step_rate = 0.05 / math.sqrt(tok_rows * devices)
    att_new = nesterov(att_master, att_moment, att_average, att_grad, step_rate)
    ffn_new = nesterov(ffn_master, ffn_moment, ffn_average, ffn_grad, step_rate)
    return (
        block_output,
        input_grad,
        att_new[0],
        att_new[1],
        att_new[2],
        att_new[3],
        ffn_new[0],
        ffn_new[1],
        ffn_new[2],
        ffn_new[3],
    )


BF = jnp.bfloat16
F32 = jnp.float32
LANES = 128
SLOT = 96
TILE = 256
FFN_TILE = 512
FFN_SPLIT = 2
FWD_PAIRS = 1
BWD_PAIRS = 2
EXTRA = 16
MIB = 1 << 20
BIG = 58


def params(limit):
    return pltpu.CompilerParams(vmem_limit_bytes=limit * MIB)


def spec_any():
    return pl.BlockSpec(memory_space=pl.ANY)


def spec_vmem():
    return pl.BlockSpec(memory_space=pltpu.VMEM)


def spec_whole(shape):
    return pl.BlockSpec(shape, lambda *ids: (0,) * len(shape))


def dot_nn(left, right):
    return lax.dot_general(left, right, (((1,), (0,)), ((), ())), preferred_element_type=F32)


def dot_nt(left, right):
    return lax.dot_general(left, right, (((1,), (1,)), ((), ())), preferred_element_type=F32)


def dot_tn(left, right):
    return lax.dot_general(left, right, (((0,), (0,)), ((), ())), preferred_element_type=F32)


def slot_of(chunk, me, late=False):
    diff = lax.bitwise_xor(me, chunk)
    far_core = lax.bitwise_and(diff, 1)
    x_bit = lax.bitwise_and(lax.shift_right_logical(diff, 1), 1)
    y_bit = lax.bitwise_and(lax.shift_right_logical(diff, 2), 1)
    z_low = lax.bitwise_and(lax.shift_right_logical(diff, 3), 1)
    z_high = lax.shift_right_logical(diff, 4)
    core = lax.bitwise_xor(lax.bitwise_and(me, 1), far_core)
    third = x_bit + core * (y_bit - x_bit)
    fourth = y_bit + core * (x_bit - y_bit)
    if late:
        return far_core, z_high + 2 * third + 4 * z_low + 8 * fourth
    return far_core, z_high + 2 * z_low + 4 * third + 8 * fourth


def bit(value, place):
    return lax.bitwise_and(lax.shift_right_logical(value, place), 1)


def chunk_of(part, slot, me, late=False):
    third, z_low = (bit(slot, 1), bit(slot, 2)) if late else (bit(slot, 2), bit(slot, 1))
    far_core, fourth = part >> 1, part & 1
    rest = far_core + 8 * z_low + 16 * bit(slot, 0)
    first_core = rest + 2 * third + 4 * fourth
    other_core = rest + 4 * third + 2 * fourth
    core = lax.bitwise_xor(bit(me, 0), far_core)
    return lax.bitwise_xor(me, first_core + core * (other_core - first_core))


def stage_perm(stage):
    if stage == 0:
        return [(i, i ^ 16) for i in range(32)]
    if stage == 1:
        return [(i, i ^ 8) for i in range(32)]
    if stage == 2:
        return [(i, i ^ (4 if i & 1 else 2)) for i in range(32)]
    if stage == 3:
        return [(i, i ^ (2 if i & 1 else 4)) for i in range(32)]
    return [(i, i ^ 1) for i in range(32)]


def exchange(array, stage):
    return lax.ppermute(array, "fsdp", stage_perm(stage))


def widen(held, got):
    return jnp.concatenate([held, got])


def widen_small(held, got):
    low = held.shape[0] - EXTRA
    small = held[low:] + got[low:]
    return jnp.concatenate([held[:low], got[:low], small])


def total_of(arrays, first, last):
    total = arrays[0][first:last].astype(F32)
    for array in arrays[1:]:
        total = total + array[first:last].astype(F32)
    return total


def halve(*arrays):
    rows = arrays[0].shape[0]
    low = total_of(arrays, 0, rows // 2).astype(BF)
    return low, total_of(arrays, rows // 2, rows).astype(BF)


def add_small(values, small):
    return jnp.concatenate([values, small.astype(BF)])


def phase(*values):
    return lax.optimization_barrier(values)


def tail_kernel(att_ref, ffn_ref, out_ref, buf, sems):
    refs = (att_ref, ffn_ref)
    starts = [(ref.shape[0] - 64) // 8 * 8 for ref in refs]
    copies = []
    for number in range(2):
        rows = refs[number].shape[0] - starts[number]
        src = refs[number].at[starts[number] :, :]
        copies.append(pltpu.make_async_copy(src, buf.at[number, 0:rows, :], sems.at[number]))
        copies[number].start()
    for number in range(2):
        rows = refs[number].shape[0] - starts[number]
        copies[number].wait()
        out_ref[number * 64 : number * 64 + 64, :] = buf[number, rows - 64 : rows, :]


def row_tails(att_master, ffn_master):
    return pl.pallas_call(
        tail_kernel,
        out_shape=jax.ShapeDtypeStruct((128, LANES), F32),
        in_specs=[spec_any()] * 2,
        out_specs=spec_vmem(),
        scratch_shapes=[pltpu.VMEM((2, 72, LANES), F32), pltpu.SemaphoreType.DMA((2,))],
        compiler_params=params(BIG),
        name="row_tails",
    )(att_master, ffn_master)


def prep_kernel(last, att_mats, ffn_mats, att_ref, ffn_ref, tail_ref, *refs):
    att_out, ffn_a, ffn_b, att_buf, ffn_buf = refs
    me = lax.axis_index("fsdp")
    att_rows = att_ref.shape[0]
    ffn_rows = ffn_ref.shape[0]
    att_buf[0:64, :] = tail_ref[0:64, :]
    att_buf[64 : 64 + att_rows, :] = att_ref[...]
    ffn_buf[0:64, :] = tail_ref[64:128, :]
    ffn_buf[64 : 64 + ffn_rows, :] = ffn_ref[...]
    start = 64 - 2 * me
    for part in range(6):
        cols = slice(part * LANES, (part + 1) * LANES)
        att_out[0:SLOT, cols] = att_buf[pl.ds(start + part, SLOT, stride=6), :].astype(BF)
    att_out[SLOT:, :] = jnp.zeros((EXTRA, att_out.shape[1]), BF)
    first = me < 16

    @pl.when(first)
    def _():
        for block in range(4):
            out = ffn_a if block < 2 else ffn_b
            rows = slice((block % 2) * 48, (block % 2) * 48 + 48)
            for part in range(6):
                cols = slice(part * LANES, (part + 1) * LANES)
                piece = ffn_buf[pl.ds(start + 6 * block + part, 48, stride=24), :]
                out[rows, cols] = piece.astype(BF)

    @pl.when(jnp.logical_not(first))
    def _():
        for part in range(6):
            cols = slice(part * LANES, (part + 1) * LANES)
            ffn_a[:, cols] = ffn_buf[pl.ds(start + part, SLOT, stride=6), :].astype(BF)
            ffn_b[:, cols] = ffn_buf[pl.ds(start + 6 * SLOT + part, SLOT, stride=6), :].astype(BF)

    @pl.when(me == last)
    def _():
        att_at = 64 + att_mats - last * att_rows
        ffn_at = 64 + ffn_mats - last * ffn_rows
        for part in range(6):
            cols = slice(part * LANES, (part + 1) * LANES)
            upper = att_buf[pl.ds(att_at + part, 6, stride=6), :]
            lower = ffn_buf[pl.ds(ffn_at + part, 7, stride=6), :]
            both = jnp.concatenate([upper, lower, jnp.zeros((3, LANES), F32)])
            att_out[SLOT:, cols] = both.astype(BF)


def prepare(att_master, ffn_master, tails, devices, width):
    att_mats = 4 * width * width // LANES
    ffn_mats = 2 * width * FF // LANES
    att_rows, ffn_rows = att_master.shape[0], ffn_master.shape[0]
    body = functools.partial(prep_kernel, devices - 1, att_mats, ffn_mats)
    return pl.pallas_call(
        body,
        out_shape=(
            jax.ShapeDtypeStruct((SLOT + EXTRA, width), BF),
            jax.ShapeDtypeStruct((SLOT, width), BF),
            jax.ShapeDtypeStruct((SLOT, width), BF),
        ),
        in_specs=[spec_vmem()] * 3,
        out_specs=(spec_vmem(),) * 3,
        scratch_shapes=[
            pltpu.VMEM((64 + att_rows + 6, LANES), F32),
            pltpu.VMEM((64 + ffn_rows + 6, LANES), F32),
        ],
        compiler_params=params(16),
        name="prep",
    )(att_master, ffn_master, tails)


def pick(index, refs, use):
    for number in range(len(refs)):

        @pl.when(index == number)
        def _():
            use(refs[number])


def each_slot(body):
    def step(slot, carry):
        for part in range(4):
            body(part, slot)
        return carry

    lax.fori_loop(0, 8, step, 0)


def load_projections(quad, dst, sems):
    me = lax.axis_index("fsdp")

    def body(part, slot):
        chunk = chunk_of(part, slot, me)

        @pl.when(chunk < 24)
        def _():
            at = pl.multiple_of(chunk * SLOT, 32)
            src = quad[part].at[pl.ds(pl.multiple_of(slot * SLOT, 32), SLOT), :]
            sem = sems.at[lax.shift_right_logical(chunk, 3)]
            pltpu.make_async_copy(src, dst.at[pl.ds(at, SLOT), :], sem).start()

    each_slot(body)


def load_output(quad, dst, sem):
    me = lax.axis_index("fsdp")
    planes = (1 - bit(me, 4)) + 2 * (1 - bit(me, 3))

    def step(third, carry):
        slot = planes + 4 * third
        for part in range(4):
            at = pl.multiple_of((chunk_of(part, slot, me) - 24) * SLOT, 32)
            src = quad[part].at[pl.ds(pl.multiple_of(slot * SLOT, 32), SLOT), :]
            pltpu.make_async_copy(src, dst.at[pl.ds(at, SLOT), :], sem).start()
        return carry

    lax.fori_loop(0, 2, step, 0)


def load_ffn(quads, w_in, w_out, sem_in, sem_out):
    me = lax.axis_index("fsdp")
    for unit in range(2):

        def body(part, slot):
            chunk = chunk_of(part, slot, me, unit == 1)
            src = quads[unit][part].at[slot]

            @pl.when(chunk < 16)
            def _():
                at = pl.multiple_of(chunk * 48, 16)
                dst = w_in.at[2 * unit : 2 * unit + 2, pl.ds(at, 48), :]
                pltpu.make_async_copy(src, dst, sem_in.at[unit]).start()

            @pl.when(chunk >= 16)
            def _():
                dst = w_out.at[2 * (chunk - 16) + unit]
                pltpu.make_async_copy(src, dst, sem_out).start()

        each_slot(body)


def wait_whole(ref, sem):
    pltpu.make_async_copy(ref, ref, sem).wait()


def as_column(row):
    return jnp.broadcast_to(row.astype(F32), (8, row.shape[1])).T[:, 0:1]


def head_mask(rows):
    lane = lax.broadcasted_iota(jnp.int32, (rows, LANES), 1)
    return lane < HEAD_DIM


def project_kernel(x_ref, masked_ref, *refs):
    quad = refs[0:4]
    stream_ref, qkv_ref, small_ref, weights, smalls, sems, small_sem = refs[4:]
    width = x_ref.shape[1]

    @pl.when(pl.program_id(0) == 0)
    def _():
        for part in range(4):
            src = quad[part].at[pl.ds(8 * SLOT, EXTRA), :]
            pltpu.make_async_copy(src, smalls.at[part], small_sem).start()
        load_projections(quad, weights, sems)
        wait_whole(smalls, small_sem)
        total = smalls[0].astype(F32)
        for part in range(1, 4):
            total = total + smalls[part].astype(F32)
        small_ref[...] = total

    small = small_ref[...]
    stream = jnp.where(as_column(masked_ref[0]) == 1.0, small[5:6], x_ref[...].astype(F32)).astype(BF)
    stream_ref[...] = stream

    def body(matrix, carry):
        rows = pl.ds(pl.multiple_of(matrix * width, width), width)

        @pl.when(pl.program_id(0) == 0)
        def _():
            wait_whole(weights.at[rows], sems.at[matrix])

        odd = lax.rem(matrix, 2)
        bias = small_ref[pl.ds(lax.div(matrix, 2), 1), :] * (1.0 - odd.astype(F32))
        scale = jnp.where(matrix == 0, 0.125, 1.0)
        product = dot_nn(stream_ref[...], weights[rows])
        qkv_ref[matrix] = ((product + bias) * scale).astype(BF)
        return carry

    lax.fori_loop(0, 3, body, 0)


def project(block_input, masked_row, quad):
    tok, width = block_input.shape
    rows = masked_row.shape[2]
    tile = lambda cols: pl.BlockSpec((rows, cols), lambda s: (s, 0))
    bf = jax.ShapeDtypeStruct((tok, width), BF)
    return pl.pallas_call(
        project_kernel,
        grid=(tok // rows,),
        out_shape=(
            bf,
            jax.ShapeDtypeStruct((3, tok, width), BF),
            jax.ShapeDtypeStruct((EXTRA, width), F32),
        ),
        in_specs=[tile(width), pl.BlockSpec((1, 1, rows), lambda s: (s, 0, 0))] + [spec_any()] * 4,
        out_specs=(
            tile(width),
            pl.BlockSpec((3, rows, width), lambda s: (0, s, 0)),
            spec_whole((EXTRA, width)),
        ),
        scratch_shapes=[
            pltpu.VMEM((3 * width, width), BF),
            pltpu.VMEM((4, EXTRA, width), BF),
            pltpu.SemaphoreType.DMA((3,)),
            pltpu.SemaphoreType.DMA,
        ],
        compiler_params=params(BIG),
        cost_estimate=pl.CostEstimate(
            flops=6 * tok * width * width, bytes_accessed=16 * MIB, transcendentals=0
        ),
        name="project",
    )(block_input, masked_row, *quad)


def forward_kernel(held, q_ref, k_ref, v_ref, seg_row_ref, *refs):
    ctx_ref, lse_ref = refs[held:]
    left = head_mask(q_ref.shape[0])
    same = as_column(seg_row_ref[0]) == seg_row_ref[0].astype(F32)
    for pair in range(FWD_PAIRS):
        cols = slice(pair * LANES, (pair + 1) * LANES)
        queries = q_ref[:, cols]
        keys = k_ref[:, cols]
        values_t = v_ref[:, cols].T
        outs = []
        for head in range(2):
            keep = left if head == 0 else jnp.logical_not(left)
            own = jnp.where(keep, queries, jnp.zeros_like(queries))
            scores = jnp.where(same, dot_nt(keys, own), MASKED_SCORE)
            top = jnp.max(scores, axis=0, keepdims=True)
            exponent = jnp.exp(scores - top)
            total = jnp.sum(exponent, axis=0, keepdims=True)
            probs = (exponent * (1.0 / total)).astype(BF)
            lse_ref[0, pair, head : head + 1, :] = top + jnp.log(total)
            outs.append(dot_nn(values_t[head * HEAD_DIM : (head + 1) * HEAD_DIM], probs))
        ctx_ref[:, cols] = jnp.concatenate(outs).T.astype(BF)


def sequence_specs(at, seq, pairs):
    tile = lambda: pl.BlockSpec((seq, pairs * LANES), lambda i: (at, i))
    row = lambda: pl.BlockSpec((1, 1, seq), lambda i: (at, 0, 0))
    part = lambda which: pl.BlockSpec((None, seq, pairs * LANES), lambda i: (which, at, i))
    stat = lambda: pl.BlockSpec((1, pairs, 2, seq), lambda i: (at, i, 0, 0))
    return tile, row, stat, [part(0), part(1), part(2)]


def attention_forward(at, qkv, seg_row, held=()):
    tok, width = qkv.shape[1:]
    seq_count, seq = seg_row.shape[0], seg_row.shape[2]
    pairs = width // LANES
    tile, row, stat, parts = sequence_specs(at, seq, FWD_PAIRS)
    return pl.pallas_call(
        functools.partial(forward_kernel, len(held)),
        grid=(pairs // FWD_PAIRS,),
        out_shape=(
            jax.ShapeDtypeStruct((tok, width), BF),
            jax.ShapeDtypeStruct((seq_count, pairs, 2, seq), F32),
        ),
        in_specs=parts + [row()] + [spec_any() for _ in held],
        out_specs=(tile(), stat()),
        input_output_aliases={4 + i: i for i in range(len(held))},
        compiler_params=params(BIG),
        cost_estimate=pl.CostEstimate(
            flops=16 * seq * seq * width,
            bytes_accessed=4 * MIB,
            transcendentals=seq * seq * width // HEAD_DIM,
        ),
        name="attention_forward",
    )(qkv, qkv, qkv, seg_row, *held)


def norm_stats(pre_norm):
    center = pre_norm - jnp.mean(pre_norm, axis=-1, keepdims=True)
    scale = lax.rsqrt(jnp.mean(center * center, axis=-1, keepdims=True) + EPSILON)
    return center * scale, scale


def norm_back(grad, gain, normed, scale):
    scaled = grad * gain
    mean_one = jnp.mean(scaled, axis=-1, keepdims=True)
    mean_two = jnp.mean(scaled * normed, axis=-1, keepdims=True)
    return scale * (scaled - mean_one - normed * mean_two)


def column_sum(array):
    return jnp.sum(array, axis=0, keepdims=True)


def gelu_pair(inputs):
    phi_cdf = 0.5 + 0.5 * lax.erf(inputs * math.sqrt(0.5))
    density = jnp.exp(inputs * inputs * -0.5) * (1.0 / math.sqrt(2.0 * math.pi))
    return inputs * phi_cdf, phi_cdf + inputs * density


def ffn_kernel(
    stream_ref,
    ctx_ref,
    grad_ref,
    small_ref,
    *refs,
):
    att_quad, quad_a, quad_b = refs[0:4], refs[4:8], refs[8:12]
    y_ref, x1_ref, hid_ref, dhid_ref, dfb_ref, dob_ref, dctx_ref, sums_ref = refs[12:20]
    w_in, w_out, w_o, slope, sem_in, sem_out, sem_o = refs[20:]
    width = ctx_ref.shape[1]
    step = pl.program_id(0)

    @pl.when(step == 0)
    def _():
        load_output(att_quad, w_o, sem_o)
        load_ffn((quad_a, quad_b), w_in, w_out, sem_in, sem_out)
        sums_ref[...] = jnp.zeros_like(sums_ref)
        wait_whole(w_o, sem_o)

    def block_cols(block):
        return slice(block * width, (block + 1) * width)

    def out_rows(block):
        return w_out[8 * block : 8 * block + 8].reshape(width, width)

    @pl.when(step == 0)
    def _():
        wait_whole(w_in.at[0:2], sem_in.at[0])
        wait_whole(w_in.at[2:4], sem_in.at[1])
        wait_whole(w_out, sem_out)

    small = small_ref[...]
    halves = range(FFN_SPLIT)
    size = FFN_TILE // FFN_SPLIT
    rows = [slice(part * size, (part + 1) * size) for part in halves]
    state = [{} for part in halves]

    def first_norm(part):
        own = state[part]
        pre_one = stream_ref[rows[part]].astype(F32) + dot_nn(ctx_ref[rows[part]], w_o[...])
        normed, own["scale"] = norm_stats(pre_one + small[2:3])
        own["normed"] = normed
        x_one = normed * small[3:4] + small[4:5]
        own["x"] = x_one.astype(BF)
        x1_ref[rows[part]] = own["x"]
        own["total"] = x_one + small[10:11]

    def forward(part, block):
        own = state[part]
        product = dot_nn(own["x"], w_in[block])
        hidden, gate = gelu_pair(product + small[6 + block : 7 + block])
        hidden = hidden.astype(BF)
        hid_ref[rows[part], block_cols(block)] = hidden
        slope[block, rows[part]] = gate
        own["total"] = own["total"] + dot_nn(hidden, out_rows(block))

    def second_norm(part):
        own = state[part]
        normed, scale = norm_stats(own["total"])
        y_ref[rows[part]] = (normed * small[11:12] + small[12:13]).astype(BF)
        grad_out = grad_ref[rows[part]].astype(F32)
        grad_two = norm_back(grad_out, small[11:12], normed, scale)
        own["low"] = grad_two.astype(BF)
        own["grad"] = grad_two
        dfb_ref[rows[part]] = own["low"]
        sums_ref[10:11] += column_sum(own["low"].astype(F32))
        sums_ref[11:12] += column_sum(grad_out * normed)
        sums_ref[12:13] += column_sum(grad_out)

    def backward(part, block):
        own = state[part]
        product = dot_nt(own["low"], out_rows(block))
        dhid = (product * slope[block, rows[part]]).astype(BF)
        dhid_ref[rows[part], block_cols(block)] = dhid
        sums_ref[6 + block : 7 + block] += column_sum(dhid.astype(F32))
        own["grad"] = own["grad"] + dot_nt(dhid, w_in[block])

    def last_norm(part):
        own = state[part]
        grad_one = own["grad"]
        sums_ref[3:4] += column_sum(grad_one * own["normed"])
        sums_ref[4:5] += column_sum(grad_one)
        dob = norm_back(grad_one, small[3:4], own["normed"], own["scale"]).astype(BF)
        dob_ref[rows[part]] = dob
        sums_ref[2:3] += column_sum(dob.astype(F32))
        dctx_ref[rows[part]] = dot_nt(dob, w_o[...]).astype(BF)

    for part in halves:
        first_norm(part)
    for block in range(FF // width):
        for part in halves:
            forward(part, block)
    for part in halves:
        second_norm(part)
    for block in range(FF // width):
        for part in halves:
            backward(part, block)
    for part in halves:
        last_norm(part)


def feed_forward(stream, ctx, out_grad, small, att_quad, quad_a, quad_b):
    tok, width = ctx.shape
    slots = (8, 2, 48, width)
    quad_a = [array.reshape(slots) for array in quad_a]
    quad_b = [array.reshape(slots) for array in quad_b]
    tile = lambda cols: pl.BlockSpec((FFN_TILE, cols), lambda i: (i, 0))
    bf = lambda cols: jax.ShapeDtypeStruct((tok, cols), BF)
    return pl.pallas_call(
        ffn_kernel,
        grid=(tok // FFN_TILE,),
        out_shape=(
            bf(width),
            bf(width),
            bf(FF),
            bf(FF),
            bf(width),
            bf(width),
            bf(width),
            jax.ShapeDtypeStruct((EXTRA, width), F32),
        ),
        in_specs=[tile(width)] * 3 + [spec_whole((EXTRA, width))] + [spec_any()] * 12,
        out_specs=(
            tile(width),
            tile(width),
            tile(FF),
            tile(FF),
            tile(width),
            tile(width),
            tile(width),
            spec_whole((EXTRA, width)),
        ),
        scratch_shapes=[
            pltpu.VMEM((FF // width, width, width), BF),
            pltpu.VMEM((FF // SLOT, 2, 48, width), BF),
            pltpu.VMEM((width, width), BF),
            pltpu.VMEM((FF // width, FFN_TILE, width), F32),
            pltpu.SemaphoreType.DMA((2,)),
            pltpu.SemaphoreType.DMA,
            pltpu.SemaphoreType.DMA,
        ],
        compiler_params=params(BIG),
        cost_estimate=pl.CostEstimate(
            flops=8 * tok * width * FF, bytes_accessed=40 * MIB, transcendentals=2 * tok * FF
        ),
        name="feed_forward",
    )(stream, ctx, out_grad, small, *att_quad, *quad_a, *quad_b)


def send_slot(parts, far_core, slot, offset, src, sem):
    at = pl.multiple_of(lax.bitwise_and(slot, 7) * SLOT + offset, 16)

    def copy(ref):
        pltpu.make_async_copy(src, ref.at[pl.ds(at, src.shape[0]), :], sem).start()

    pick(2 * far_core + lax.shift_right_logical(slot, 3), parts, copy)


def part_shapes(width, small):
    rows = [8 * SLOT, 8 * SLOT, 8 * SLOT, 8 * SLOT + (EXTRA if small else 0)]
    return tuple(jax.ShapeDtypeStruct((count, width), BF) for count in rows)


def wait_reuse(stage, sems, buf, step):
    @pl.when(step >= 2)
    def _():
        wait_whole(stage.at[buf], sems.at[buf])


def wait_last(stage, sems, step, steps):
    @pl.when(step == steps - 1)
    def _():
        for buf in range(2):
            wait_whole(stage.at[buf], sems.at[buf])


def send_in_blocks(parts, me, late, part, stage, buf, sem):
    def body(chunk, carry):
        far_core, slot = slot_of(chunk, me, late)
        src = stage.at[buf, pl.ds(pl.multiple_of(chunk * 48, 16), 48)]
        send_slot(parts, far_core, slot, part * 48, src, sem)
        return carry

    lax.fori_loop(0, 16, body, 0)


def ffn_grad_kernel(x_ref, hid_ref, dhid_ref, dfb_ref, sums_ref, *refs):
    parts_a, parts_b = refs[0:4], refs[4:8]
    held, stage, small_stage, held_sem, sems, small_sem = refs[8:]
    width = x_ref.shape[1]
    me = lax.axis_index("fsdp")
    step = pl.program_id(0)
    buf = lax.rem(step, 2)
    small_rows = parts_b[3].at[pl.ds(8 * SLOT, EXTRA), :]

    def fetch(index):
        into, sem = held.at[2 + lax.rem(index, 2)], held_sem.at[2 + lax.rem(index, 2)]

        def start(ref, block):
            at = pl.multiple_of(block * width, LANES)
            pltpu.make_async_copy(ref.at[:, pl.ds(at, width)], into, sem).start()

        @pl.when(index < 4)
        def _():
            start(hid_ref, index)

        @pl.when(index >= 4)
        def _():
            start(dhid_ref, index - 2)

    @pl.when(step == 0)
    def _():
        pltpu.make_async_copy(dfb_ref, held.at[0], held_sem.at[0]).start()
        fetch(step)
        pltpu.make_async_copy(x_ref, held.at[1], held_sem.at[1]).start()
        small_stage[...] = sums_ref[...].astype(BF)
        pltpu.make_async_copy(small_stage, small_rows, small_sem).start()
        wait_whole(held.at[0], held_sem.at[0])

    @pl.when(step < 5)
    def _():
        fetch(step + 1)

    @pl.when(step == 4)
    def _():
        wait_whole(held.at[1], held_sem.at[1])

    wait_whole(held.at[2 + buf], held_sem.at[2 + buf])
    wait_reuse(stage, sems, buf, step)
    second = lax.div(step, 4)
    left = (2 + buf) * (1 - second) + second
    stage[buf] = dot_tn(held[left], held[(2 + buf) * second]).astype(BF)

    @pl.when(step < 4)
    def _():

        def body(chunk, carry):
            for unit in range(2):
                far_core, slot = slot_of(16 + 4 * step + chunk, me, unit == 1)
                at = pl.multiple_of((2 * chunk + unit) * SLOT, 32)
                src = stage.at[buf, pl.ds(at, SLOT)]
                send_slot((parts_a, parts_b)[unit], far_core, slot, 0, src, sems.at[buf])
            return carry

        lax.fori_loop(0, 4, body, 0)

    @pl.when(step >= 4)
    def _():
        send_in_blocks(parts_b, me, True, step - 4, stage, buf, sems.at[buf])

    @pl.when(step == 5)
    def _():
        wait_whole(small_stage, small_sem)

    wait_last(stage, sems, step, 6)


def ffn_grads(x_low, hidden, dhid, dfb, sums):
    tok, width = x_low.shape
    out = pl.pallas_call(
        ffn_grad_kernel,
        grid=(6,),
        out_shape=part_shapes(width, False) + part_shapes(width, True),
        in_specs=[spec_any()] * 4 + [spec_whole((EXTRA, width))],
        out_specs=(spec_any(),) * 8,
        scratch_shapes=[
            pltpu.VMEM((4, tok, width), BF),
            pltpu.VMEM((2, width, width), BF),
            pltpu.VMEM((EXTRA, width), BF),
            pltpu.SemaphoreType.DMA((4,)),
            pltpu.SemaphoreType.DMA((2,)),
            pltpu.SemaphoreType.DMA,
        ],
        compiler_params=params(BIG),
        cost_estimate=pl.CostEstimate(
            flops=3 * tok * width * FF, bytes_accessed=24 * MIB, transcendentals=0
        ),
        name="ffn_grads",
    )(x_low, hidden, dhid, dfb, sums)
    return out[0:4], out[4:8]


def ffn_rest_kernel(x_ref, dhid_ref, *refs):
    parts = refs[4:8]
    stage, sems = refs[8:]
    me = lax.axis_index("fsdp")
    step = pl.program_id(0)
    stage[step] = dot_tn(x_ref[...], dhid_ref[...]).astype(BF)
    send_in_blocks(parts, me, False, step, stage, step, sems.at[step])
    wait_last(stage, sems, step, 2)


def ffn_rest(x_low, dhid, parts):
    tok, width = x_low.shape
    return pl.pallas_call(
        ffn_rest_kernel,
        grid=(2,),
        out_shape=part_shapes(width, False),
        in_specs=[spec_whole((tok, width)), pl.BlockSpec((tok, width), lambda i: (0, i))]
        + [spec_any()] * 4,
        out_specs=(spec_any(),) * 4,
        input_output_aliases={2 + i: i for i in range(4)},
        scratch_shapes=[pltpu.VMEM((2, width, width), BF), pltpu.SemaphoreType.DMA((2,))],
        compiler_params=params(BIG),
        cost_estimate=pl.CostEstimate(
            flops=tok * width * FF, bytes_accessed=8 * MIB, transcendentals=0
        ),
        name="ffn_rest",
    )(x_low, dhid, *parts)


def backward_kernel(held, q_ref, k_ref, v_ref, dctx_ref, lse_ref, seg_row_ref, *refs):
    dq_ref, dk_ref, dv_ref = refs[held:]
    left = head_mask(q_ref.shape[0])
    same = as_column(seg_row_ref[0]) == seg_row_ref[0].astype(F32)
    heads = 2 * BWD_PAIRS
    held_a, held_b, held_c = {}, {}, {}

    def pair_cols(head):
        return slice(head // 2 * LANES, (head // 2 + 1) * LANES)

    def products(head):
        cols = pair_cols(head)
        keep = left if head % 2 == 0 else jnp.logical_not(left)
        own = jnp.where(keep, q_ref[:, cols], jnp.zeros((keep.shape), BF))
        own_grad = jnp.where(keep, dctx_ref[:, cols], jnp.zeros((keep.shape), BF))
        scores = dot_nt(k_ref[:, cols], own)
        held_a[head] = (own, own_grad, scores, dot_nt(v_ref[:, cols], own_grad))

    def softmax_back(head):
        own, own_grad, scores, grad_probs = held_a.pop(head)
        scores = jnp.where(same, scores, MASKED_SCORE)
        probs = jnp.exp(scores - lse_ref[0, head // 2, head % 2 : head % 2 + 1, :])
        inner = jnp.sum(grad_probs * probs, axis=0, keepdims=True)
        grad_scores = (probs * (grad_probs - inner)).astype(BF)
        held_b[head] = (own, own_grad, probs.astype(BF), grad_scores)

    def outputs(head):
        own, own_grad, probs, grad_scores = held_b.pop(head)
        cols = pair_cols(head)
        keys_t = k_ref[:, cols].T[(head % 2) * HEAD_DIM : (head % 2 + 1) * HEAD_DIM]
        grad_q = dot_nn(keys_t, grad_scores)
        grad_k = dot_nn(grad_scores, own)
        grad_v = dot_nn(probs, own_grad)
        if head % 2 == 0:
            held_c[0] = (grad_q, grad_k, grad_v)
            return
        first_q, first_k, first_v = held_c.pop(0)
        both_q = jnp.concatenate([first_q, grad_q]).T
        dq_ref[:, cols] = (both_q.astype(BF) * 0.125).astype(BF)
        dk_ref[:, cols] = (first_k + grad_k).astype(BF)
        dv_ref[:, cols] = (first_v + grad_v).astype(BF)

    for tick in range(heads + 2):
        if tick < heads:
            products(tick)
        if 0 <= tick - 1 < heads:
            softmax_back(tick - 1)
        if tick >= 2:
            outputs(tick - 2)


def attention_backward(at, qkv, dctx, lse, seg_row, held=()):
    tok, width = qkv.shape[1:]
    seq = seg_row.shape[2]
    tile, row, stat, parts = sequence_specs(at, seq, BWD_PAIRS)
    return pl.pallas_call(
        functools.partial(backward_kernel, len(held)),
        grid=(width // LANES // BWD_PAIRS,),
        out_shape=(jax.ShapeDtypeStruct((tok, width), BF),) * 3,
        in_specs=parts + [tile(), stat(), row()]
        + [spec_any() for _ in held],
        out_specs=(tile(), tile(), tile()),
        input_output_aliases={6 + i: i for i in range(len(held))},
        compiler_params=params(BIG),
        cost_estimate=pl.CostEstimate(
            flops=40 * seq * seq * width,
            bytes_accessed=6 * MIB,
            transcendentals=seq * seq * width // HEAD_DIM,
        ),
        name="attention_backward",
    )(qkv, qkv, qkv, dctx, lse, seg_row, *held)


def input_grad_kernel(dq_ref, dk_ref, dv_ref, dob_ref, masked_ref, *refs):
    quad = refs[0:4]
    dx_ref, small_ref, weights, sems = refs[4:]
    width = dq_ref.shape[1]
    step = pl.program_id(0)

    @pl.when(step == 0)
    def _():
        load_projections(quad, weights, sems)
        small_ref[...] = jnp.zeros_like(small_ref)

    grad = dob_ref[...].astype(F32)
    for matrix in range(3):
        rows = slice(matrix * width, (matrix + 1) * width)

        @pl.when(step == 0)
        def _():
            wait_whole(weights.at[rows], sems.at[matrix])

        grad = grad + dot_nt((dq_ref, dk_ref, dv_ref)[matrix][...], weights[rows])
    chosen = as_column(masked_ref[0]) == 1.0
    dx_ref[...] = jnp.where(chosen, 0.0, grad)
    small_ref[0:1] += column_sum(dq_ref[...].astype(F32))
    small_ref[1:2] += column_sum(dv_ref[...].astype(F32))
    small_ref[5:6] += column_sum(jnp.where(chosen, grad, 0.0))


def input_grads(dq, dk, dv, dob, masked_row, quad):
    tok, width = dq.shape
    rows = TILE
    per = masked_row.shape[2] // rows
    tile = lambda cols: pl.BlockSpec((rows, cols), lambda i: (i, 0))
    whole = spec_whole((EXTRA, width))
    return pl.pallas_call(
        input_grad_kernel,
        grid=(tok // rows,),
        out_shape=(
            jax.ShapeDtypeStruct((tok, width), F32),
            jax.ShapeDtypeStruct((EXTRA, width), F32),
        ),
        in_specs=[tile(width)] * 4
        + [pl.BlockSpec((1, 1, rows), lambda i: (i // per, 0, i % per))]
        + [spec_any()] * 4,
        out_specs=(tile(width), whole),
        scratch_shapes=[pltpu.VMEM((3 * width, width), BF), pltpu.SemaphoreType.DMA((3,))],
        compiler_params=params(BIG),
        cost_estimate=pl.CostEstimate(
            flops=6 * tok * width * width, bytes_accessed=16 * MIB, transcendentals=0
        ),
        name="input_grads",
    )(dq, dk, dv, dob, masked_row, *quad)


def att_grad_kernel(*refs):
    sources, parts = refs[0:6], refs[6:10]
    held, stage, load_sems, sems = refs[10:]
    me = lax.axis_index("fsdp")
    step = pl.program_id(0)
    buf = lax.rem(step, 2)

    @pl.when(step == 0)
    def _():
        for number in range(6):
            pltpu.make_async_copy(sources[number], held.at[number], load_sems.at[number]).start()

    wait_reuse(stage, sems, buf, step)
    for matrix in range(4):

        @pl.when(step == matrix)
        def _():
            for number in ((0, 1), (2, 3), (4,), (5,))[matrix]:
                wait_whole(held.at[number], load_sems.at[number])

    left = 2 * jnp.minimum(step, 1)
    stage[buf] = dot_tn(held[left], held[left + jnp.maximum(step, 1)]).astype(BF)
    first = lax.rem(step + 3, 4) * 8

    def body(piece, carry):
        far_core, slot = slot_of(first + piece, me)
        src = stage.at[buf, pl.ds(pl.multiple_of(piece * SLOT, 32), SLOT)]
        send_slot(parts, far_core, slot, 0, src, sems.at[buf])
        return carry

    lax.fori_loop(0, 8, body, 0)
    wait_last(stage, sems, step, 4)


def att_grads(ctx, dob, stream, dq, dk, dv):
    tok, width = stream.shape
    return pl.pallas_call(
        att_grad_kernel,
        grid=(4,),
        out_shape=part_shapes(width, False),
        in_specs=[spec_any()] * 6,
        out_specs=(spec_any(),) * 4,
        scratch_shapes=[
            pltpu.VMEM((6, tok, width), BF),
            pltpu.VMEM((2, width, width), BF),
            pltpu.SemaphoreType.DMA((6,)),
            pltpu.SemaphoreType.DMA((2,)),
        ],
        compiler_params=params(BIG),
        cost_estimate=pl.CostEstimate(
            flops=8 * tok * width * width, bytes_accessed=16 * MIB, transcendentals=0
        ),
        name="att_grads",
    )(ctx, dob, stream, dq, dk, dv)


def flat_ffn_kernel(a_ref, b_ref, out_ref):
    first = lax.axis_index("fsdp") < 16

    @pl.when(first)
    def _():
        for block in range(4):
            source = a_ref if block < 2 else b_ref
            rows = slice((block % 2) * 48, (block % 2) * 48 + 48)
            for part in range(6):
                cols = slice(part * LANES, (part + 1) * LANES)
                out_ref[pl.ds(6 * block + part, 48, stride=24), :] = source[rows, cols]

    @pl.when(jnp.logical_not(first))
    def _():
        for part in range(6):
            cols = slice(part * LANES, (part + 1) * LANES)
            out_ref[pl.ds(part, SLOT, stride=6), :] = a_ref[:, cols]
            out_ref[pl.ds(6 * SLOT + part, SLOT, stride=6), :] = b_ref[:, cols]


def flatten_ffn(grad_a, grad_b):
    return pl.pallas_call(
        flat_ffn_kernel,
        out_shape=jax.ShapeDtypeStruct((12 * SLOT, LANES), F32),
        in_specs=[spec_vmem()] * 2,
        out_specs=spec_vmem(),
        compiler_params=params(16),
        name="flatten_ffn",
    )(grad_a, grad_b)


def flat_att_kernel(kept_ref, got_ref, ffn_ref, late_ref, out_ref, head_ref):
    for part in range(6):
        cols = slice(part * LANES, (part + 1) * LANES)
        total = kept_ref[:, cols].astype(F32) + got_ref[0:SLOT, cols].astype(F32)
        out_ref[pl.ds(part, SLOT, stride=6), :] = total
    head_ref[0:64, :] = out_ref[0:64, :]
    head_ref[64:128, :] = ffn_ref[0:64, :]

    @pl.when(lax.axis_index("fsdp") == 0)
    def _():
        for part in range(6):
            cols = slice(part * LANES, (part + 1) * LANES)
            head_ref[pl.ds(part, 6, stride=6), :] = late_ref[0:6, cols]


def flatten_att(kept, got, ffn_flat, late):
    return pl.pallas_call(
        flat_att_kernel,
        out_shape=(
            jax.ShapeDtypeStruct((6 * SLOT, LANES), F32),
            jax.ShapeDtypeStruct((128, LANES), F32),
        ),
        in_specs=[spec_vmem()] * 4,
        out_specs=(spec_vmem(),) * 2,
        compiler_params=params(16),
        name="flatten_att",
    )(kept, got, ffn_flat, late)


def update_kernel(last, rate, *refs):
    inputs, outputs, bufs = refs[0:10], refs[10:18], refs[18:20]
    me = lax.axis_index("fsdp")
    head_ref, small_ref = inputs[2], inputs[3]
    for unit in range(2):
        flat_ref = inputs[unit]
        w_ref, m_ref, a_ref = inputs[4 + 3 * unit : 7 + 3 * unit]
        w_out, m_out, a_out, low_out = outputs[4 * unit : 4 * unit + 4]
        buf = bufs[unit]
        aligned = flat_ref.shape[0]
        first, count = ((0, 6), (6, 7))[unit]
        buf[0:aligned, :] = flat_ref[...]
        buf[aligned : aligned + 64, :] = head_ref[unit * 64 : unit * 64 + 64, :]

        @pl.when(me == last)
        def _():
            buf[aligned : aligned + 64, :] = jnp.zeros((64, LANES), F32)
            for part in range(6):
                cols = slice(part * LANES, (part + 1) * LANES)
                small = small_ref[first : first + count, cols]
                if unit == 0:
                    small = small + head_ref[pl.ds(part, count, stride=6), :]
                buf[pl.ds(aligned + part, count, stride=6), :] = small

        grad = buf[pl.ds(2 * me, w_ref.shape[0]), :]
        moment = 0.5 * m_ref[...] + grad
        master = w_ref[...] - rate * (grad + 0.5 * moment)
        m_out[...] = moment
        w_out[...] = master
        a_out[...] = 0.5 * a_ref[...] + 0.5 * master
        low_out[...] = master.astype(BF)


def update(flats, head, small, rate, devices, att, ffn):
    shapes = []
    for arrays in (att, ffn):
        f32 = jax.ShapeDtypeStruct(arrays[0].shape, F32)
        shapes += [f32, f32, f32, jax.ShapeDtypeStruct(arrays[0].shape, BF)]
    out = pl.pallas_call(
        functools.partial(update_kernel, devices - 1, rate),
        out_shape=tuple(shapes),
        in_specs=[spec_vmem()] * 10,
        out_specs=(spec_vmem(),) * 8,
        scratch_shapes=[pltpu.VMEM((flat.shape[0] + 64, LANES), F32) for flat in flats],
        compiler_params=params(16),
        name="update",
    )(*flats, head, small, *att, *ffn)
    return out


def local_exchange(
    block_input,
    seg_ids,
    masked,
    out_grad,
    att_master,
    att_moment,
    att_average,
    ffn_master,
    ffn_moment,
    ffn_average,
):
    tok, width = block_input.shape
    seq_count, seq = seg_ids.shape
    devices = lax.axis_size("fsdp")
    up = [(i, i + 1) for i in range(devices - 1)]
    down = [(i + 1, i) for i in range(devices - 1)]
    tails = lax.ppermute(row_tails(att_master, ffn_master), "fsdp", up)
    masked_row = masked.reshape(seq_count, 1, seq)
    seg_row = seg_ids.reshape(seq_count, 1, seq)
    att, chunk_a, chunk_b = prepare(att_master, ffn_master, tails, devices, width)
    got, masked_row, seg_row = phase(exchange(att, 0), masked_row, seg_row)
    att = widen_small(att, got)
    got = exchange(att, 1)
    att, unit_a = phase(widen_small(att, got), chunk_a)
    got, got_a = phase(exchange(att, 2), exchange(unit_a, 0))
    att, unit_a, unit_b = phase(widen_small(att, got), widen(unit_a, got_a), chunk_b)
    att_next, att_far, got_a, got_b = phase(
        exchange(att, 3), exchange(att, 4), exchange(unit_a, 1), exchange(unit_b, 0)
    )
    unit_a, unit_b, att_next = phase(widen(unit_a, got_a), widen(unit_b, got_b), att_next)
    att_last, got_b, block_input = phase(exchange(att_next, 4), exchange(unit_b, 2), block_input)
    att = (att, att_next, att_far, att_last)
    unit_a, unit_b, block_input = phase(unit_a, widen(unit_b, got_b), block_input)
    got_b = exchange(unit_b, 1)
    stream, qkv, small = project(block_input, masked_row, att)
    got_a, qkv = phase(exchange(unit_a, 2), qkv)
    unit_a, qkv = phase(widen(unit_a, got_a), qkv)
    held = attention_forward(0, qkv, seg_row)
    a_next, a_far, got_b, held = phase(exchange(unit_a, 3), exchange(unit_a, 4), got_b, held)
    unit_b, a_next, held = phase(widen(unit_b, got_b), a_next, held)
    ctx, lse = attention_forward(1, qkv, seg_row, held)
    b_next, b_far, a_last, ctx = phase(
        exchange(unit_b, 3), exchange(unit_b, 4), exchange(a_next, 4), ctx
    )
    b_last = exchange(b_next, 4)
    block_output, x_low, hidden, dhid, dfb, dob, dctx, sums = feed_forward(
        stream,
        ctx,
        out_grad,
        small,
        att,
        (unit_a, a_next, a_far, a_last),
        (unit_b, b_next, b_far, b_last),
    )
    part_a, part_b = ffn_grads(x_low, hidden, dhid, dfb, sums)
    part_b, dhid = phase(part_b, dhid)
    part_a = ffn_rest(x_low, dhid, part_a)
    high_b, low_b, part_a = phase(exchange(part_b[3], 4), exchange(part_b[2], 4), part_a)
    small_sum = sums + high_b[8 * SLOT :].astype(F32)
    high_b = add_small(total_of((part_b[1], high_b), 0, 8 * SLOT).astype(BF), small_sum)
    high_b, part_a, dctx = phase(high_b, part_a, dctx)
    held = attention_backward(0, qkv, dctx, lse, seg_row)
    got_b, high_a, low_a, held = phase(
        exchange(high_b, 3), exchange(part_a[3], 4), exchange(part_a[2], 4), held
    )
    high_a = total_of((part_a[1], high_a), 0, 8 * SLOT).astype(BF)
    small_sum = small_sum + got_b[8 * SLOT :].astype(F32)
    kept_b, sent_b = halve(part_b[0], low_b, got_b[: 8 * SLOT])
    high_a, sent_b, held = phase(high_a, add_small(sent_b, small_sum), held)
    dq, dk, dv = attention_backward(1, qkv, dctx, lse, seg_row, held)
    got_a, got_b, dq = phase(exchange(high_a, 3), exchange(sent_b, 1), dq)
    kept_a, sent_a = halve(part_a[0], low_a, got_a)
    small_sum = small_sum + got_b[4 * SLOT :].astype(F32)
    kept_b, sent_b = halve(kept_b, got_b[: 4 * SLOT])
    sent_a, sent_b, dq = phase(sent_a, add_small(sent_b, small_sum), dq)
    part = att_grads(ctx, dob, stream, dq, dk, dv)
    got_a, got_b, part = phase(exchange(sent_a, 2), exchange(sent_b, 2), part)
    kept_a, sent_a = halve(kept_a, got_a)
    small_sum = small_sum + got_b[2 * SLOT :].astype(F32)
    kept_b, sent_b = halve(kept_b, got_b[: 2 * SLOT])
    sent_a, sent_b, part = phase(sent_a, add_small(sent_b, small_sum), part)
    got_b = exchange(sent_b, 0)
    high = exchange(part[3], 4)
    high = total_of((part[1], high), 0, 8 * SLOT).astype(BF)
    high, sent_a, dq = phase(high, sent_a, dq)
    input_grad, late = input_grads(dq, dk, dv, dob, masked_row, att)
    got, low, got_a, got_b, late = phase(
        exchange(high, 3), exchange(part[2], 4), exchange(sent_a, 1), got_b, late
    )
    kept, sent = halve(part[0], low, got)
    kept_a, sent_a = halve(kept_a, got_a)
    sent, sent_a, late = phase(sent, sent_a, late)
    got, got_a = phase(exchange(add_small(sent, late), 2), exchange(sent_a, 0))
    late = late + got[4 * SLOT :].astype(F32)
    kept, sent = halve(kept, got[: 4 * SLOT])
    sent, late, got_a, got_b = phase(sent, late, got_a, got_b)
    got = exchange(sent, 1)
    late = late + exchange(late.astype(BF), 3).astype(F32)
    late = late + exchange(late.astype(BF), 4).astype(F32)
    kept, sent = halve(kept, got)
    sent, got_a, got_b = phase(add_small(sent, late), got_a, got_b)
    got = exchange(sent, 0)
    small_sum = small_sum + got_b[SLOT:].astype(F32)
    grad_a = total_of((kept_a, got_a), 0, SLOT)
    grad_b = total_of((kept_b, got_b), 0, SLOT)
    ffn_flat = flatten_ffn(grad_a, grad_b)
    got, ffn_flat, small_sum = phase(got, ffn_flat, small_sum)
    late = late + got[SLOT:].astype(F32)
    att_flat, heads = flatten_att(kept, got, ffn_flat, late)
    heads = lax.ppermute(heads, "fsdp", down + [(0, devices - 1)])
    rate = 0.05 / math.sqrt(tok * devices)
    new = update(
        (att_flat, ffn_flat),
        heads,
        small_sum + late,
        rate,
        devices,
        (att_master, att_moment, att_average),
        (ffn_master, ffn_moment, ffn_average),
    )
    return (block_output, input_grad) + tuple(new)


def chunked(mesh):
    return mesh.shape["fsdp"] == 32


def solution(mesh):
    in_specs = (
        P("fsdp", None),
        P("fsdp", None),
        P("fsdp", None),
        P("fsdp", None),
        P("fsdp", None),
        P("fsdp", None),
        P("fsdp", None),
        P("fsdp", None),
        P("fsdp", None),
        P("fsdp", None),
    )
    out_specs = (
        P("fsdp", None),
        P("fsdp", None),
        P("fsdp", None),
        P("fsdp", None),
        P("fsdp", None),
        P("fsdp", None),
        P("fsdp", None),
        P("fsdp", None),
        P("fsdp", None),
        P("fsdp", None),
    )
    body = local_exchange if chunked(mesh) else local
    return jax.shard_map(body, mesh=mesh, in_specs=in_specs, out_specs=out_specs, check_vma=False)
```

```python
import functools
import math

import jax
import jax.numpy as jnp
from jax import lax
from jax.experimental import pallas as pl
from jax.experimental.pallas import tpu as pltpu
from jax.sharding import PartitionSpec as P

HEAD_DIM = 64
FF = 3072


EPSILON = 1e-05
MASKED_SCORE = -1e30


def layer_norm(pre_norm, gain, shift):
    center = pre_norm - jnp.mean(pre_norm, axis=-1, keepdims=True)
    spread = jnp.mean(center * center, axis=-1, keepdims=True)
    return center * lax.rsqrt(spread + EPSILON) * gain + shift


def gelu_exact(inputs):
    return jax.nn.gelu(inputs, approximate=False)


def unpack_attention(flat_att, model_width):
    square = model_width * model_width
    att_mats = flat_att[: 4 * square].reshape(4, model_width, model_width)
    small_params = flat_att[4 * square : 4 * square + 6 * model_width].reshape(6, model_width)
    return (att_mats, small_params)


def unpack_ffn(flat_ffn, model_width, hidden):
    size_in = model_width * hidden
    weight_in = flat_ffn[:size_in].reshape(model_width, hidden)
    weight_out = flat_ffn[size_in : 2 * size_in].reshape(hidden, model_width)
    offset = 2 * size_in
    bias_in = flat_ffn[offset : offset + hidden]
    small_params = flat_ffn[offset + hidden : offset + hidden + 3 * model_width].reshape(
        3, model_width
    )
    return (weight_in, weight_out, bias_in, small_params)


def pack_rows(pieces, row_count):
    filled = sum((piece.shape[0] for piece in pieces))
    padding = jnp.zeros((row_count * 128 - filled,), jnp.float32)
    return jnp.concatenate(list(pieces) + [padding]).reshape(row_count, 128)


def attend_forward(block_items):
    query_block, key_block, value_block, doc_block = block_items
    scores = jnp.einsum("qhd,khd->hqk", query_block, key_block, preferred_element_type=jnp.float32)
    same_doc = doc_block[:, None] == doc_block[None, :]
    scores = jnp.where(same_doc[None], scores, MASKED_SCORE)
    row_max = jnp.max(scores, axis=-1, keepdims=True)
    exponent = jnp.exp(scores - row_max)
    row_total = jnp.sum(exponent, axis=-1, keepdims=True)
    attn_probs = (exponent / row_total).astype(jnp.bfloat16)
    context = jnp.einsum(
        "hqk,khd->qhd", attn_probs, value_block, preferred_element_type=jnp.float32
    )
    return (context.astype(jnp.bfloat16), (row_max + jnp.log(row_total))[..., 0])


def attend_backward(block_items):
    query_block, key_block, value_block, doc_block, log_total, grad_context = block_items
    scores = jnp.einsum("qhd,khd->hqk", query_block, key_block, preferred_element_type=jnp.float32)
    same_doc = doc_block[:, None] == doc_block[None, :]
    scores = jnp.where(same_doc[None], scores, MASKED_SCORE)
    attn_probs = jnp.exp(scores - log_total[..., None])
    probs_low = attn_probs.astype(jnp.bfloat16)
    grad_probs = jnp.einsum(
        "qhd,khd->hqk", grad_context, value_block, preferred_element_type=jnp.float32
    )
    row_inner = jnp.sum(grad_probs * attn_probs, axis=-1, keepdims=True)
    grad_scores = (attn_probs * (grad_probs - row_inner)).astype(jnp.bfloat16)
    grad_query = jnp.einsum(
        "hqk,khd->qhd", grad_scores, key_block, preferred_element_type=jnp.float32
    ).astype(jnp.bfloat16)
    grad_key = jnp.einsum(
        "hqk,qhd->khd", grad_scores, query_block, preferred_element_type=jnp.float32
    ).astype(jnp.bfloat16)
    grad_value = jnp.einsum(
        "hqk,qhd->khd", probs_low, grad_context, preferred_element_type=jnp.float32
    ).astype(jnp.bfloat16)
    return (grad_query, grad_key, grad_value)


def nesterov(master, moment, average, gradient, step_rate):
    moment_new = 0.5 * moment + gradient
    master_new = master - step_rate * (gradient + 0.5 * moment_new)
    average_new = 0.5 * average + 0.5 * master_new
    return (master_new, moment_new, average_new, master_new.astype(jnp.bfloat16))


def local(
    block_input,
    seg_ids,
    masked,
    out_grad,
    att_master,
    att_moment,
    att_average,
    ffn_master,
    ffn_moment,
    ffn_average,
):
    tok_rows, model_width = block_input.shape
    seq_count, seq_length = seg_ids.shape
    head_count = model_width // HEAD_DIM
    devices = lax.axis_size("fsdp")
    att_rows = att_master.shape[0] * devices
    ffn_rows = ffn_master.shape[0] * devices
    head_shape = (seq_count, seq_length, head_count, HEAD_DIM)
    att_whole = lax.all_gather(att_master.astype(jnp.bfloat16), "fsdp", axis=0, tiled=True)
    att_mats, att_small_low = unpack_attention(att_whole.reshape(-1), model_width)
    att_small = att_small_low.astype(jnp.float32)
    masked_rows = masked.reshape(tok_rows, 1) == 1
    stream_in = jnp.where(masked_rows, att_small[5][None, :], block_input.astype(jnp.float32))
    stream_low = stream_in.astype(jnp.bfloat16)
    projected = jnp.einsum(
        "td,cde->cte", stream_low, att_mats[:3], preferred_element_type=jnp.float32
    )
    queries = ((projected[0] + att_small[0]) * 0.125).astype(jnp.bfloat16).reshape(head_shape)
    key_rows = projected[1].astype(jnp.bfloat16).reshape(head_shape)
    values = (projected[2] + att_small[1]).astype(jnp.bfloat16).reshape(head_shape)
    context, log_total = lax.map(attend_forward, (queries, key_rows, values, seg_ids))
    context_flat = context.reshape(tok_rows, model_width)
    pre_one = (
        stream_in
        + jnp.dot(context_flat, att_mats[3], preferred_element_type=jnp.float32)
        + att_small[2]
    )
    normed_one = layer_norm(pre_one, att_small[3], att_small[4])
    normed_low = normed_one.astype(jnp.bfloat16)
    ffn_whole = lax.all_gather(ffn_master.astype(jnp.bfloat16), "fsdp", axis=0, tiled=True)
    weight_in, weight_out, bias_in_low, ffn_small_low = unpack_ffn(
        ffn_whole.reshape(-1), model_width, FF
    )
    bias_in = bias_in_low.astype(jnp.float32)
    ffn_small = ffn_small_low.astype(jnp.float32)
    hid_pre = jnp.dot(normed_low, weight_in, preferred_element_type=jnp.float32) + bias_in
    hid_act = gelu_exact(hid_pre).astype(jnp.bfloat16)
    pre_two = (
        normed_one + jnp.dot(hid_act, weight_out, preferred_element_type=jnp.float32) + ffn_small[0]
    )
    normed_two, norm_two_pull = jax.vjp(layer_norm, pre_two, ffn_small[1], ffn_small[2])
    block_output = normed_two.astype(jnp.bfloat16)
    ffn_back = lax.all_gather(ffn_master.astype(jnp.bfloat16), "fsdp", axis=0, tiled=True)
    back_in, back_out, bias_unused, small_unused = unpack_ffn(ffn_back.reshape(-1), model_width, FF)
    grad_pre_two, grad_gain_two, grad_shift_two = norm_two_pull(out_grad.astype(jnp.float32))
    grad_branch_two = grad_pre_two.astype(jnp.bfloat16)
    grad_w_out = jnp.einsum(
        "tf,td->fd", hid_act, grad_branch_two, preferred_element_type=jnp.float32
    )
    grad_b_out = jnp.sum(grad_branch_two, axis=0, dtype=jnp.float32)
    grad_act = jnp.einsum(
        "td,fd->tf", grad_branch_two, back_out, preferred_element_type=jnp.float32
    )
    hid_unused, gelu_pull = jax.vjp(gelu_exact, hid_pre)
    grad_hidden = gelu_pull(grad_act)[0].astype(jnp.bfloat16)
    grad_w_in = jnp.einsum("td,tf->df", normed_low, grad_hidden, preferred_element_type=jnp.float32)
    grad_b_in = jnp.sum(grad_hidden, axis=0, dtype=jnp.float32)
    grad_normed_one = grad_pre_two + jnp.einsum(
        "tf,df->td", grad_hidden, back_in, preferred_element_type=jnp.float32
    )
    ffn_flat_grad = pack_rows(
        (
            grad_w_in.reshape(-1),
            grad_w_out.reshape(-1),
            grad_b_in,
            grad_b_out,
            grad_gain_two,
            grad_shift_two,
        ),
        ffn_rows,
    )
    ffn_grad = lax.psum_scatter(ffn_flat_grad, "fsdp", scatter_dimension=0, tiled=True)
    att_back = lax.all_gather(att_master.astype(jnp.bfloat16), "fsdp", axis=0, tiled=True)
    back_mats, small_back = unpack_attention(att_back.reshape(-1), model_width)
    pre_unused, norm_one_pull = jax.vjp(layer_norm, pre_one, att_small[3], att_small[4])
    grad_pre_one, grad_gain_one, grad_shift_one = norm_one_pull(grad_normed_one)
    grad_branch_one = grad_pre_one.astype(jnp.bfloat16)
    grad_w_o = jnp.einsum(
        "td,te->de", context_flat, grad_branch_one, preferred_element_type=jnp.float32
    )
    grad_b_o = jnp.sum(grad_branch_one, axis=0, dtype=jnp.float32)
    grad_context = jnp.einsum(
        "te,de->td", grad_branch_one, back_mats[3], preferred_element_type=jnp.float32
    ).astype(jnp.bfloat16)
    grad_q4, grad_k4, grad_v4 = lax.map(
        attend_backward,
        (queries, key_rows, values, seg_ids, log_total, grad_context.reshape(head_shape)),
    )
    grad_queries = grad_q4.reshape(tok_rows, model_width) * 0.125
    grad_keys = grad_k4.reshape(tok_rows, model_width)
    grad_values = grad_v4.reshape(tok_rows, model_width)
    grad_projected = jnp.stack([grad_queries, grad_keys, grad_values])
    grad_w_qkv = jnp.einsum(
        "td,cte->cde", stream_low, grad_projected, preferred_element_type=jnp.float32
    )
    grad_b_q = jnp.sum(grad_queries, axis=0, dtype=jnp.float32)
    grad_b_v = jnp.sum(grad_values, axis=0, dtype=jnp.float32)
    grad_stream = grad_pre_one + jnp.einsum(
        "cte,cde->td", grad_projected, back_mats[:3], preferred_element_type=jnp.float32
    )
    grad_mask_vector = jnp.sum(jnp.where(masked_rows, grad_stream, 0.0), axis=0)
    input_grad = jnp.where(masked_rows, 0.0, grad_stream)
    att_flat_grad = pack_rows(
        (
            grad_w_qkv.reshape(-1),
            grad_w_o.reshape(-1),
            grad_b_q,
            grad_b_v,
            grad_b_o,
            grad_gain_one,
            grad_shift_one,
            grad_mask_vector,
        ),
        att_rows,
    )
    att_grad = lax.psum_scatter(att_flat_grad, "fsdp", scatter_dimension=0, tiled=True)
    step_rate = 0.05 / math.sqrt(tok_rows * devices)
    att_new = nesterov(att_master, att_moment, att_average, att_grad, step_rate)
    ffn_new = nesterov(ffn_master, ffn_moment, ffn_average, ffn_grad, step_rate)
    return (
        block_output,
        input_grad,
        att_new[0],
        att_new[1],
        att_new[2],
        att_new[3],
        ffn_new[0],
        ffn_new[1],
        ffn_new[2],
        ffn_new[3],
    )


BF = jnp.bfloat16
F32 = jnp.float32
LANES = 128
SLOT = 96
TILE = 256
FFN_TILE = 512
FFN_SPLIT = 2
FWD_PAIRS = 1
BWD_PAIRS = 2
EXTRA = 16
MIB = 1 << 20
BIG = 58


def params(limit):
    return pltpu.CompilerParams(vmem_limit_bytes=limit * MIB)


def spec_any():
    return pl.BlockSpec(memory_space=pl.ANY)


def spec_vmem():
    return pl.BlockSpec(memory_space=pltpu.VMEM)


def spec_whole(shape):
    return pl.BlockSpec(shape, lambda *ids: (0,) * len(shape))


def dot_nn(left, right):
    return lax.dot_general(left, right, (((1,), (0,)), ((), ())), preferred_element_type=F32)


def dot_nt(left, right):
    return lax.dot_general(left, right, (((1,), (1,)), ((), ())), preferred_element_type=F32)


def dot_tn(left, right):
    return lax.dot_general(left, right, (((0,), (0,)), ((), ())), preferred_element_type=F32)


def slot_of(chunk, me, late=False):
    diff = lax.bitwise_xor(me, chunk)
    far_core = lax.bitwise_and(diff, 1)
    x_bit = lax.bitwise_and(lax.shift_right_logical(diff, 1), 1)
    y_bit = lax.bitwise_and(lax.shift_right_logical(diff, 2), 1)
    z_low = lax.bitwise_and(lax.shift_right_logical(diff, 3), 1)
    z_high = lax.shift_right_logical(diff, 4)
    core = lax.bitwise_xor(lax.bitwise_and(me, 1), far_core)
    third = x_bit + core * (y_bit - x_bit)
    fourth = y_bit + core * (x_bit - y_bit)
    if late:
        return far_core, z_high + 2 * third + 4 * z_low + 8 * fourth
    return far_core, z_high + 2 * z_low + 4 * third + 8 * fourth


def bit(value, place):
    return lax.bitwise_and(lax.shift_right_logical(value, place), 1)


def chunk_of(part, slot, me, late=False):
    third, z_low = (bit(slot, 1), bit(slot, 2)) if late else (bit(slot, 2), bit(slot, 1))
    far_core, fourth = part >> 1, part & 1
    rest = far_core + 8 * z_low + 16 * bit(slot, 0)
    first_core = rest + 2 * third + 4 * fourth
    other_core = rest + 4 * third + 2 * fourth
    core = lax.bitwise_xor(bit(me, 0), far_core)
    return lax.bitwise_xor(me, first_core + core * (other_core - first_core))


def stage_perm(stage):
    if stage == 0:
        return [(i, i ^ 16) for i in range(32)]
    if stage == 1:
        return [(i, i ^ 8) for i in range(32)]
    if stage == 2:
        return [(i, i ^ (4 if i & 1 else 2)) for i in range(32)]
    if stage == 3:
        return [(i, i ^ (2 if i & 1 else 4)) for i in range(32)]
    return [(i, i ^ 1) for i in range(32)]


def exchange(array, stage):
    return lax.ppermute(array, "fsdp", stage_perm(stage))


def widen(held, got):
    return jnp.concatenate([held, got])


def widen_small(held, got):
    low = held.shape[0] - EXTRA
    small = held[low:] + got[low:]
    return jnp.concatenate([held[:low], got[:low], small])


def total_of(arrays, first, last):
    total = arrays[0][first:last].astype(F32)
    for array in arrays[1:]:
        total = total + array[first:last].astype(F32)
    return total


def halve(*arrays):
    rows = arrays[0].shape[0]
    low = total_of(arrays, 0, rows // 2).astype(BF)
    return low, total_of(arrays, rows // 2, rows).astype(BF)


def add_small(values, small):
    return jnp.concatenate([values, small.astype(BF)])


def phase(*values):
    return lax.optimization_barrier(values)


def tail_kernel(att_ref, ffn_ref, out_ref, buf, sems):
    refs = (att_ref, ffn_ref)
    starts = [(ref.shape[0] - 64) // 8 * 8 for ref in refs]
    copies = []
    for number in range(2):
        rows = refs[number].shape[0] - starts[number]
        src = refs[number].at[starts[number] :, :]
        copies.append(pltpu.make_async_copy(src, buf.at[number, 0:rows, :], sems.at[number]))
        copies[number].start()
    for number in range(2):
        rows = refs[number].shape[0] - starts[number]
        copies[number].wait()
        out_ref[number * 64 : number * 64 + 64, :] = buf[number, rows - 64 : rows, :]


def row_tails(att_master, ffn_master):
    return pl.pallas_call(
        tail_kernel,
        out_shape=jax.ShapeDtypeStruct((128, LANES), F32),
        in_specs=[spec_any()] * 2,
        out_specs=spec_vmem(),
        scratch_shapes=[pltpu.VMEM((2, 72, LANES), F32), pltpu.SemaphoreType.DMA((2,))],
        compiler_params=params(BIG),
        name="row_tails",
    )(att_master, ffn_master)


def prep_kernel(last, att_mats, ffn_mats, att_ref, ffn_ref, tail_ref, *refs):
    att_out, ffn_a, ffn_b, att_buf, ffn_buf = refs
    me = lax.axis_index("fsdp")
    att_rows = att_ref.shape[0]
    ffn_rows = ffn_ref.shape[0]
    att_buf[0:64, :] = tail_ref[0:64, :]
    att_buf[64 : 64 + att_rows, :] = att_ref[...]
    ffn_buf[0:64, :] = tail_ref[64:128, :]
    ffn_buf[64 : 64 + ffn_rows, :] = ffn_ref[...]
    start = 64 - 2 * me
    for part in range(6):
        cols = slice(part * LANES, (part + 1) * LANES)
        att_out[0:SLOT, cols] = att_buf[pl.ds(start + part, SLOT, stride=6), :].astype(BF)
    att_out[SLOT:, :] = jnp.zeros((EXTRA, att_out.shape[1]), BF)
    first = me < 16

    @pl.when(first)
    def _():
        for block in range(4):
            out = ffn_a if block < 2 else ffn_b
            rows = slice((block % 2) * 48, (block % 2) * 48 + 48)
            for part in range(6):
                cols = slice(part * LANES, (part + 1) * LANES)
                piece = ffn_buf[pl.ds(start + 6 * block + part, 48, stride=24), :]
                out[rows, cols] = piece.astype(BF)

    @pl.when(jnp.logical_not(first))
    def _():
        for part in range(6):
            cols = slice(part * LANES, (part + 1) * LANES)
            ffn_a[:, cols] = ffn_buf[pl.ds(start + part, SLOT, stride=6), :].astype(BF)
            ffn_b[:, cols] = ffn_buf[pl.ds(start + 6 * SLOT + part, SLOT, stride=6), :].astype(BF)

    @pl.when(me == last)
    def _():
        att_at = 64 + att_mats - last * att_rows
        ffn_at = 64 + ffn_mats - last * ffn_rows
        for part in range(6):
            cols = slice(part * LANES, (part + 1) * LANES)
            upper = att_buf[pl.ds(att_at + part, 6, stride=6), :]
            lower = ffn_buf[pl.ds(ffn_at + part, 7, stride=6), :]
            both = jnp.concatenate([upper, lower, jnp.zeros((3, LANES), F32)])
            att_out[SLOT:, cols] = both.astype(BF)


def prepare(att_master, ffn_master, tails, devices, width):
    att_mats = 4 * width * width // LANES
    ffn_mats = 2 * width * FF // LANES
    att_rows, ffn_rows = att_master.shape[0], ffn_master.shape[0]
    body = functools.partial(prep_kernel, devices - 1, att_mats, ffn_mats)
    return pl.pallas_call(
        body,
        out_shape=(
            jax.ShapeDtypeStruct((SLOT + EXTRA, width), BF),
            jax.ShapeDtypeStruct((SLOT, width), BF),
            jax.ShapeDtypeStruct((SLOT, width), BF),
        ),
        in_specs=[spec_vmem()] * 3,
        out_specs=(spec_vmem(),) * 3,
        scratch_shapes=[
            pltpu.VMEM((64 + att_rows + 6, LANES), F32),
            pltpu.VMEM((64 + ffn_rows + 30, LANES), F32),
        ],
        compiler_params=params(16),
        name="prep",
    )(att_master, ffn_master, tails)


def pick(index, refs, use):
    for number in range(len(refs)):

        @pl.when(index == number)
        def _():
            use(refs[number])


def each_slot(body):
    def step(slot, carry):
        for part in range(4):
            body(part, slot)
        return carry

    lax.fori_loop(0, 8, step, 0)


def load_projections(quad, dst, sems):
    me = lax.axis_index("fsdp")

    def body(part, slot):
        chunk = chunk_of(part, slot, me)

        @pl.when(chunk < 24)
        def _():
            at = pl.multiple_of(chunk * SLOT, 32)
            src = quad[part].at[pl.ds(pl.multiple_of(slot * SLOT, 32), SLOT), :]
            sem = sems.at[lax.shift_right_logical(chunk, 3)]
            pltpu.make_async_copy(src, dst.at[pl.ds(at, SLOT), :], sem).start()

    each_slot(body)


def load_output(quad, dst, sem):
    me = lax.axis_index("fsdp")
    planes = (1 - bit(me, 4)) + 2 * (1 - bit(me, 3))

    def step(third, carry):
        slot = planes + 4 * third
        for part in range(4):
            at = pl.multiple_of((chunk_of(part, slot, me) - 24) * SLOT, 32)
            src = quad[part].at[pl.ds(pl.multiple_of(slot * SLOT, 32), SLOT), :]
            pltpu.make_async_copy(src, dst.at[pl.ds(at, SLOT), :], sem).start()
        return carry

    lax.fori_loop(0, 2, step, 0)


def load_ffn(quads, w_in, w_out, sem_in, sem_out):
    me = lax.axis_index("fsdp")
    for unit in range(2):

        def body(part, slot):
            chunk = chunk_of(part, slot, me, unit == 1)
            src = quads[unit][part].at[slot]

            @pl.when(chunk < 16)
            def _():
                at = pl.multiple_of(chunk * 48, 16)
                dst = w_in.at[2 * unit : 2 * unit + 2, pl.ds(at, 48), :]
                pltpu.make_async_copy(src, dst, sem_in.at[unit]).start()

            @pl.when(chunk >= 16)
            def _():
                dst = w_out.at[2 * (chunk - 16) + unit]
                pltpu.make_async_copy(src, dst, sem_out).start()

        each_slot(body)


def wait_whole(ref, sem):
    pltpu.make_async_copy(ref, ref, sem).wait()


def as_column(row):
    return jnp.broadcast_to(row.astype(F32), (8, row.shape[1])).T[:, 0:1]


def head_mask(rows):
    lane = lax.broadcasted_iota(jnp.int32, (rows, LANES), 1)
    return lane < HEAD_DIM


def project_kernel(x_ref, masked_ref, *refs):
    quad = refs[0:4]
    stream_ref, qkv_ref, small_ref, weights, smalls, sems, small_sem = refs[4:]
    width = x_ref.shape[1]

    @pl.when(pl.program_id(0) == 0)
    def _():
        for part in range(4):
            src = quad[part].at[pl.ds(8 * SLOT, EXTRA), :]
            pltpu.make_async_copy(src, smalls.at[part], small_sem).start()
        load_projections(quad, weights, sems)
        wait_whole(smalls, small_sem)
        total = smalls[0].astype(F32)
        for part in range(1, 4):
            total = total + smalls[part].astype(F32)
        small_ref[...] = total

    small = small_ref[...]
    stream = jnp.where(as_column(masked_ref[0]) == 1.0, small[5:6], x_ref[...].astype(F32)).astype(BF)
    stream_ref[...] = stream

    def body(matrix, carry):
        rows = pl.ds(pl.multiple_of(matrix * width, width), width)

        @pl.when(pl.program_id(0) == 0)
        def _():
            wait_whole(weights.at[rows], sems.at[matrix])

        odd = lax.rem(matrix, 2)
        bias = small_ref[pl.ds(lax.div(matrix, 2), 1), :] * (1.0 - odd.astype(F32))
        scale = jnp.where(matrix == 0, 0.125, 1.0)
        product = dot_nn(stream_ref[...], weights[rows])
        qkv_ref[matrix] = ((product + bias) * scale).astype(BF)
        return carry

    lax.fori_loop(0, 3, body, 0)


def project(block_input, masked_row, quad):
    tok, width = block_input.shape
    rows = masked_row.shape[2]
    tile = lambda cols: pl.BlockSpec((rows, cols), lambda s: (s, 0))
    bf = jax.ShapeDtypeStruct((tok, width), BF)
    return pl.pallas_call(
        project_kernel,
        grid=(tok // rows,),
        out_shape=(
            bf,
            jax.ShapeDtypeStruct((3, tok, width), BF),
            jax.ShapeDtypeStruct((EXTRA, width), F32),
        ),
        in_specs=[tile(width), pl.BlockSpec((1, 1, rows), lambda s: (s, 0, 0))] + [spec_any()] * 4,
        out_specs=(
            tile(width),
            pl.BlockSpec((3, rows, width), lambda s: (0, s, 0)),
            spec_whole((EXTRA, width)),
        ),
        scratch_shapes=[
            pltpu.VMEM((3 * width, width), BF),
            pltpu.VMEM((4, EXTRA, width), BF),
            pltpu.SemaphoreType.DMA((3,)),
            pltpu.SemaphoreType.DMA,
        ],
        compiler_params=params(BIG),
        cost_estimate=pl.CostEstimate(
            flops=6 * tok * width * width, bytes_accessed=16 * MIB, transcendentals=0
        ),
        name="project",
    )(block_input, masked_row, *quad)


def forward_kernel(held, q_ref, k_ref, v_ref, seg_row_ref, *refs):
    ctx_ref, lse_ref = refs[held:]
    left = head_mask(q_ref.shape[0])
    same = as_column(seg_row_ref[0]) == seg_row_ref[0].astype(F32)
    for pair in range(FWD_PAIRS):
        cols = slice(pair * LANES, (pair + 1) * LANES)
        queries = q_ref[:, cols]
        keys = k_ref[:, cols]
        values_t = v_ref[:, cols].T
        outs = []
        for head in range(2):
            keep = left if head == 0 else jnp.logical_not(left)
            own = jnp.where(keep, queries, jnp.zeros_like(queries))
            scores = jnp.where(same, dot_nt(keys, own), MASKED_SCORE)
            top = jnp.max(scores, axis=0, keepdims=True)
            exponent = jnp.exp(scores - top)
            total = jnp.sum(exponent, axis=0, keepdims=True)
            probs = (exponent * (1.0 / total)).astype(BF)
            lse_ref[0, pair, head : head + 1, :] = top + jnp.log(total)
            outs.append(dot_nn(values_t[head * HEAD_DIM : (head + 1) * HEAD_DIM], probs))
        ctx_ref[:, cols] = jnp.concatenate(outs).T.astype(BF)


def sequence_specs(at, seq, pairs):
    tile = lambda: pl.BlockSpec((seq, pairs * LANES), lambda i: (at, i))
    row = lambda: pl.BlockSpec((1, 1, seq), lambda i: (at, 0, 0))
    part = lambda which: pl.BlockSpec((None, seq, pairs * LANES), lambda i: (which, at, i))
    stat = lambda: pl.BlockSpec((1, pairs, 2, seq), lambda i: (at, i, 0, 0))
    return tile, row, stat, [part(0), part(1), part(2)]


def attention_forward(at, qkv, seg_row, held=()):
    tok, width = qkv.shape[1:]
    seq_count, seq = seg_row.shape[0], seg_row.shape[2]
    pairs = width // LANES
    tile, row, stat, parts = sequence_specs(at, seq, FWD_PAIRS)
    return pl.pallas_call(
        functools.partial(forward_kernel, len(held)),
        grid=(pairs // FWD_PAIRS,),
        out_shape=(
            jax.ShapeDtypeStruct((tok, width), BF),
            jax.ShapeDtypeStruct((seq_count, pairs, 2, seq), F32),
        ),
        in_specs=parts + [row()] + [spec_any() for _ in held],
        out_specs=(tile(), stat()),
        input_output_aliases={4 + i: i for i in range(len(held))},
        compiler_params=params(BIG),
        cost_estimate=pl.CostEstimate(
            flops=16 * seq * seq * width,
            bytes_accessed=4 * MIB,
            transcendentals=seq * seq * width // HEAD_DIM,
        ),
        name="attention_forward",
    )(qkv, qkv, qkv, seg_row, *held)


def norm_stats(pre_norm):
    center = pre_norm - jnp.mean(pre_norm, axis=-1, keepdims=True)
    scale = lax.rsqrt(jnp.mean(center * center, axis=-1, keepdims=True) + EPSILON)
    return center * scale, scale


def norm_back(grad, gain, normed, scale):
    scaled = grad * gain
    mean_one = jnp.mean(scaled, axis=-1, keepdims=True)
    mean_two = jnp.mean(scaled * normed, axis=-1, keepdims=True)
    return scale * (scaled - mean_one - normed * mean_two)


def column_sum(array):
    return jnp.sum(array, axis=0, keepdims=True)


def gelu_pair(inputs):
    phi_cdf = 0.5 + 0.5 * lax.erf(inputs * math.sqrt(0.5))
    density = jnp.exp(inputs * inputs * -0.5) * (1.0 / math.sqrt(2.0 * math.pi))
    return inputs * phi_cdf, phi_cdf + inputs * density


def ffn_kernel(
    stream_ref,
    ctx_ref,
    grad_ref,
    small_ref,
    *refs,
):
    att_quad, quad_a, quad_b = refs[0:4], refs[4:8], refs[8:12]
    y_ref, x1_ref, hid_ref, dhid_ref, dfb_ref, dob_ref, dctx_ref, sums_ref = refs[12:20]
    w_in, w_out, w_o, slope, sem_in, sem_out, sem_o = refs[20:]
    width = ctx_ref.shape[1]
    step = pl.program_id(0)

    @pl.when(step == 0)
    def _():
        load_output(att_quad, w_o, sem_o)
        load_ffn((quad_a, quad_b), w_in, w_out, sem_in, sem_out)
        sums_ref[...] = jnp.zeros_like(sums_ref)
        wait_whole(w_o, sem_o)

    def block_cols(block):
        return slice(block * width, (block + 1) * width)

    def out_rows(block):
        return w_out[8 * block : 8 * block + 8].reshape(width, width)

    @pl.when(step == 0)
    def _():
        wait_whole(w_in.at[0:2], sem_in.at[0])
        wait_whole(w_in.at[2:4], sem_in.at[1])
        wait_whole(w_out, sem_out)

    small = small_ref[...]
    halves = range(FFN_SPLIT)
    size = FFN_TILE // FFN_SPLIT
    rows = [slice(part * size, (part + 1) * size) for part in halves]
    state = [{} for part in halves]

    def first_norm(part):
        own = state[part]
        pre_one = stream_ref[rows[part]].astype(F32) + dot_nn(ctx_ref[rows[part]], w_o[...])
        normed, own["scale"] = norm_stats(pre_one + small[2:3])
        own["normed"] = normed
        x_one = normed * small[3:4] + small[4:5]
        own["x"] = x_one.astype(BF)
        x1_ref[rows[part]] = own["x"]
        own["total"] = x_one + small[10:11]

    def forward(part, block):
        own = state[part]
        product = dot_nn(own["x"], w_in[block])
        hidden, gate = gelu_pair(product + small[6 + block : 7 + block])
        hidden = hidden.astype(BF)
        hid_ref[rows[part], block_cols(block)] = hidden
        slope[block, rows[part]] = gate
        own["total"] = own["total"] + dot_nn(hidden, out_rows(block))

    def second_norm(part):
        own = state[part]
        normed, scale = norm_stats(own["total"])
        y_ref[rows[part]] = (normed * small[11:12] + small[12:13]).astype(BF)
        grad_out = grad_ref[rows[part]].astype(F32)
        grad_two = norm_back(grad_out, small[11:12], normed, scale)
        own["low"] = grad_two.astype(BF)
        own["grad"] = grad_two
        dfb_ref[rows[part]] = own["low"]
        sums_ref[10:11] += column_sum(own["low"].astype(F32))
        sums_ref[11:12] += column_sum(grad_out * normed)
        sums_ref[12:13] += column_sum(grad_out)

    def backward(part, block):
        own = state[part]
        product = dot_nt(own["low"], out_rows(block))
        dhid = (product * slope[block, rows[part]]).astype(BF)
        dhid_ref[rows[part], block_cols(block)] = dhid
        sums_ref[6 + block : 7 + block] += column_sum(dhid.astype(F32))
        own["grad"] = own["grad"] + dot_nt(dhid, w_in[block])

    def last_norm(part):
        own = state[part]
        grad_one = own["grad"]
        sums_ref[3:4] += column_sum(grad_one * own["normed"])
        sums_ref[4:5] += column_sum(grad_one)
        dob = norm_back(grad_one, small[3:4], own["normed"], own["scale"]).astype(BF)
        dob_ref[rows[part]] = dob
        sums_ref[2:3] += column_sum(dob.astype(F32))
        dctx_ref[rows[part]] = dot_nt(dob, w_o[...]).astype(BF)

    for part in halves:
        first_norm(part)
    for block in range(FF // width):
        for part in halves:
            forward(part, block)
    for part in halves:
        second_norm(part)
    for block in range(FF // width):
        for part in halves:
            backward(part, block)
    for part in halves:
        last_norm(part)


def feed_forward(stream, ctx, out_grad, small, att_quad, quad_a, quad_b):
    tok, width = ctx.shape
    slots = (8, 2, 48, width)
    quad_a = [array.reshape(slots) for array in quad_a]
    quad_b = [array.reshape(slots) for array in quad_b]
    tile = lambda cols: pl.BlockSpec((FFN_TILE, cols), lambda i: (i, 0))
    bf = lambda cols: jax.ShapeDtypeStruct((tok, cols), BF)
    return pl.pallas_call(
        ffn_kernel,
        grid=(tok // FFN_TILE,),
        out_shape=(
            bf(width),
            bf(width),
            bf(FF),
            bf(FF),
            bf(width),
            bf(width),
            bf(width),
            jax.ShapeDtypeStruct((EXTRA, width), F32),
        ),
        in_specs=[tile(width)] * 3 + [spec_whole((EXTRA, width))] + [spec_any()] * 12,
        out_specs=(
            tile(width),
            tile(width),
            tile(FF),
            tile(FF),
            tile(width),
            tile(width),
            tile(width),
            spec_whole((EXTRA, width)),
        ),
        scratch_shapes=[
            pltpu.VMEM((FF // width, width, width), BF),
            pltpu.VMEM((FF // SLOT, 2, 48, width), BF),
            pltpu.VMEM((width, width), BF),
            pltpu.VMEM((FF // width, FFN_TILE, width), F32),
            pltpu.SemaphoreType.DMA((2,)),
            pltpu.SemaphoreType.DMA,
            pltpu.SemaphoreType.DMA,
        ],
        compiler_params=params(BIG),
        cost_estimate=pl.CostEstimate(
            flops=8 * tok * width * FF, bytes_accessed=40 * MIB, transcendentals=2 * tok * FF
        ),
        name="feed_forward",
    )(stream, ctx, out_grad, small, *att_quad, *quad_a, *quad_b)


def send_slot(parts, far_core, slot, offset, src, sem):
    at = pl.multiple_of(lax.bitwise_and(slot, 7) * SLOT + offset, 16)

    def copy(ref):
        pltpu.make_async_copy(src, ref.at[pl.ds(at, src.shape[0]), :], sem).start()

    pick(2 * far_core + lax.shift_right_logical(slot, 3), parts, copy)


def part_shapes(width, small):
    rows = [8 * SLOT, 8 * SLOT, 8 * SLOT, 8 * SLOT + (EXTRA if small else 0)]
    return tuple(jax.ShapeDtypeStruct((count, width), BF) for count in rows)


def wait_reuse(stage, sems, buf, step):
    @pl.when(step >= 2)
    def _():
        wait_whole(stage.at[buf], sems.at[buf])


def wait_last(stage, sems, step, steps):
    @pl.when(step == steps - 1)
    def _():
        for buf in range(2):
            wait_whole(stage.at[buf], sems.at[buf])


def send_in_blocks(parts, me, late, part, stage, buf, sem):
    def body(chunk, carry):
        far_core, slot = slot_of(chunk, me, late)
        src = stage.at[buf, pl.ds(pl.multiple_of(chunk * 48, 16), 48)]
        send_slot(parts, far_core, slot, part * 48, src, sem)
        return carry

    lax.fori_loop(0, 16, body, 0)


def ffn_grad_kernel(x_ref, hid_ref, dhid_ref, dfb_ref, sums_ref, *refs):
    parts_a, parts_b = refs[0:4], refs[4:8]
    held, stage, small_stage, held_sem, sems, small_sem = refs[8:]
    width = x_ref.shape[1]
    me = lax.axis_index("fsdp")
    step = pl.program_id(0)
    buf = lax.rem(step, 2)
    small_rows = parts_b[3].at[pl.ds(8 * SLOT, EXTRA), :]

    def fetch(index):
        into, sem = held.at[2 + lax.rem(index, 2)], held_sem.at[2 + lax.rem(index, 2)]

        def start(ref, block):
            at = pl.multiple_of(block * width, LANES)
            pltpu.make_async_copy(ref.at[:, pl.ds(at, width)], into, sem).start()

        @pl.when(index < 4)
        def _():
            start(hid_ref, index)

        @pl.when(index >= 4)
        def _():
            start(dhid_ref, index - 2)

    @pl.when(step == 0)
    def _():
        pltpu.make_async_copy(dfb_ref, held.at[0], held_sem.at[0]).start()
        fetch(step)
        pltpu.make_async_copy(x_ref, held.at[1], held_sem.at[1]).start()
        small_stage[...] = sums_ref[...].astype(BF)
        pltpu.make_async_copy(small_stage, small_rows, small_sem).start()
        wait_whole(held.at[0], held_sem.at[0])

    @pl.when(step < 5)
    def _():
        fetch(step + 1)

    @pl.when(step == 4)
    def _():
        wait_whole(held.at[1], held_sem.at[1])

    wait_whole(held.at[2 + buf], held_sem.at[2 + buf])
    wait_reuse(stage, sems, buf, step)
    second = lax.div(step, 4)
    left = (2 + buf) * (1 - second) + second
    stage[buf] = dot_tn(held[left], held[(2 + buf) * second]).astype(BF)

    @pl.when(step < 4)
    def _():

        def body(chunk, carry):
            for unit in range(2):
                far_core, slot = slot_of(16 + 4 * step + chunk, me, unit == 1)
                at = pl.multiple_of((2 * chunk + unit) * SLOT, 32)
                src = stage.at[buf, pl.ds(at, SLOT)]
                send_slot((parts_a, parts_b)[unit], far_core, slot, 0, src, sems.at[buf])
            return carry

        lax.fori_loop(0, 4, body, 0)

    @pl.when(step >= 4)
    def _():
        send_in_blocks(parts_b, me, True, step - 4, stage, buf, sems.at[buf])

    @pl.when(step == 5)
    def _():
        wait_whole(small_stage, small_sem)

    wait_last(stage, sems, step, 6)


def ffn_grads(x_low, hidden, dhid, dfb, sums):
    tok, width = x_low.shape
    out = pl.pallas_call(
        ffn_grad_kernel,
        grid=(6,),
        out_shape=part_shapes(width, False) + part_shapes(width, True),
        in_specs=[spec_any()] * 4 + [spec_whole((EXTRA, width))],
        out_specs=(spec_any(),) * 8,
        scratch_shapes=[
            pltpu.VMEM((4, tok, width), BF),
            pltpu.VMEM((2, width, width), BF),
            pltpu.VMEM((EXTRA, width), BF),
            pltpu.SemaphoreType.DMA((4,)),
            pltpu.SemaphoreType.DMA((2,)),
            pltpu.SemaphoreType.DMA,
        ],
        compiler_params=params(BIG),
        cost_estimate=pl.CostEstimate(
            flops=3 * tok * width * FF, bytes_accessed=24 * MIB, transcendentals=0
        ),
        name="ffn_grads",
    )(x_low, hidden, dhid, dfb, sums)
    return out[0:4], out[4:8]


def ffn_rest_kernel(x_ref, dhid_ref, *refs):
    parts = refs[4:8]
    stage, sems = refs[8:]
    me = lax.axis_index("fsdp")
    step = pl.program_id(0)
    stage[step] = dot_tn(x_ref[...], dhid_ref[...]).astype(BF)
    send_in_blocks(parts, me, False, step, stage, step, sems.at[step])
    wait_last(stage, sems, step, 2)


def ffn_rest(x_low, dhid, parts):
    tok, width = x_low.shape
    return pl.pallas_call(
        ffn_rest_kernel,
        grid=(2,),
        out_shape=part_shapes(width, False),
        in_specs=[spec_whole((tok, width)), pl.BlockSpec((tok, width), lambda i: (0, i))]
        + [spec_any()] * 4,
        out_specs=(spec_any(),) * 4,
        input_output_aliases={2 + i: i for i in range(4)},
        scratch_shapes=[pltpu.VMEM((2, width, width), BF), pltpu.SemaphoreType.DMA((2,))],
        compiler_params=params(BIG),
        cost_estimate=pl.CostEstimate(
            flops=tok * width * FF, bytes_accessed=8 * MIB, transcendentals=0
        ),
        name="ffn_rest",
    )(x_low, dhid, *parts)


def backward_kernel(held, q_ref, k_ref, v_ref, dctx_ref, lse_ref, seg_row_ref, *refs):
    dq_ref, dk_ref, dv_ref = refs[held:]
    left = head_mask(q_ref.shape[0])
    same = as_column(seg_row_ref[0]) == seg_row_ref[0].astype(F32)
    heads = 2 * BWD_PAIRS
    held_a, held_b, held_c = {}, {}, {}

    def pair_cols(head):
        return slice(head // 2 * LANES, (head // 2 + 1) * LANES)

    def products(head):
        cols = pair_cols(head)
        keep = left if head % 2 == 0 else jnp.logical_not(left)
        own = jnp.where(keep, q_ref[:, cols], jnp.zeros((keep.shape), BF))
        own_grad = jnp.where(keep, dctx_ref[:, cols], jnp.zeros((keep.shape), BF))
        scores = dot_nt(k_ref[:, cols], own)
        held_a[head] = (own, own_grad, scores, dot_nt(v_ref[:, cols], own_grad))

    def softmax_back(head):
        own, own_grad, scores, grad_probs = held_a.pop(head)
        scores = jnp.where(same, scores, MASKED_SCORE)
        probs = jnp.exp(scores - lse_ref[0, head // 2, head % 2 : head % 2 + 1, :])
        inner = jnp.sum(grad_probs * probs, axis=0, keepdims=True)
        grad_scores = (probs * (grad_probs - inner)).astype(BF)
        held_b[head] = (own, own_grad, probs.astype(BF), grad_scores)

    def outputs(head):
        own, own_grad, probs, grad_scores = held_b.pop(head)
        cols = pair_cols(head)
        keys_t = k_ref[:, cols].T[(head % 2) * HEAD_DIM : (head % 2 + 1) * HEAD_DIM]
        grad_q = dot_nn(keys_t, grad_scores)
        grad_k = dot_nn(grad_scores, own)
        grad_v = dot_nn(probs, own_grad)
        if head % 2 == 0:
            held_c[0] = (grad_q, grad_k, grad_v)
            return
        first_q, first_k, first_v = held_c.pop(0)
        both_q = jnp.concatenate([first_q, grad_q]).T
        dq_ref[:, cols] = (both_q.astype(BF) * 0.125).astype(BF)
        dk_ref[:, cols] = (first_k + grad_k).astype(BF)
        dv_ref[:, cols] = (first_v + grad_v).astype(BF)

    for tick in range(heads + 2):
        if tick < heads:
            products(tick)
        if 0 <= tick - 1 < heads:
            softmax_back(tick - 1)
        if tick >= 2:
            outputs(tick - 2)


def attention_backward(at, qkv, dctx, lse, seg_row, held=()):
    tok, width = qkv.shape[1:]
    seq = seg_row.shape[2]
    tile, row, stat, parts = sequence_specs(at, seq, BWD_PAIRS)
    return pl.pallas_call(
        functools.partial(backward_kernel, len(held)),
        grid=(width // LANES // BWD_PAIRS,),
        out_shape=(jax.ShapeDtypeStruct((tok, width), BF),) * 3,
        in_specs=parts + [tile(), stat(), row()]
        + [spec_any() for _ in held],
        out_specs=(tile(), tile(), tile()),
        input_output_aliases={6 + i: i for i in range(len(held))},
        compiler_params=params(54),
        cost_estimate=pl.CostEstimate(
            flops=40 * seq * seq * width,
            bytes_accessed=6 * MIB,
            transcendentals=seq * seq * width // HEAD_DIM,
        ),
        name="attention_backward",
    )(qkv, qkv, qkv, dctx, lse, seg_row, *held)


def input_grad_kernel(dq_ref, dk_ref, dv_ref, dob_ref, masked_ref, *refs):
    quad = refs[0:4]
    dx_ref, small_ref, weights, sems = refs[4:]
    width = dq_ref.shape[1]
    step = pl.program_id(0)

    @pl.when(step == 0)
    def _():
        load_projections(quad, weights, sems)
        small_ref[...] = jnp.zeros_like(small_ref)

    grad = dob_ref[...].astype(F32)
    for matrix in range(3):
        rows = slice(matrix * width, (matrix + 1) * width)

        @pl.when(step == 0)
        def _():
            wait_whole(weights.at[rows], sems.at[matrix])

        grad = grad + dot_nt((dq_ref, dk_ref, dv_ref)[matrix][...], weights[rows])
    chosen = as_column(masked_ref[0]) == 1.0
    dx_ref[...] = jnp.where(chosen, 0.0, grad)
    small_ref[0:1] += column_sum(dq_ref[...].astype(F32))
    small_ref[1:2] += column_sum(dv_ref[...].astype(F32))
    small_ref[5:6] += column_sum(jnp.where(chosen, grad, 0.0))


def input_grads(dq, dk, dv, dob, masked_row, quad):
    tok, width = dq.shape
    rows = TILE
    per = masked_row.shape[2] // rows
    tile = lambda cols: pl.BlockSpec((rows, cols), lambda i: (i, 0))
    whole = spec_whole((EXTRA, width))
    return pl.pallas_call(
        input_grad_kernel,
        grid=(tok // rows,),
        out_shape=(
            jax.ShapeDtypeStruct((tok, width), F32),
            jax.ShapeDtypeStruct((EXTRA, width), F32),
        ),
        in_specs=[tile(width)] * 4
        + [pl.BlockSpec((1, 1, rows), lambda i: (i // per, 0, i % per))]
        + [spec_any()] * 4,
        out_specs=(tile(width), whole),
        scratch_shapes=[pltpu.VMEM((3 * width, width), BF), pltpu.SemaphoreType.DMA((3,))],
        compiler_params=params(BIG),
        cost_estimate=pl.CostEstimate(
            flops=6 * tok * width * width, bytes_accessed=16 * MIB, transcendentals=0
        ),
        name="input_grads",
    )(dq, dk, dv, dob, masked_row, *quad)


def att_grad_kernel(*refs):
    sources, parts = refs[0:6], refs[6:10]
    held, stage, load_sems, sems = refs[10:]
    me = lax.axis_index("fsdp")
    step = pl.program_id(0)
    buf = lax.rem(step, 2)

    @pl.when(step == 0)
    def _():
        for number in range(6):
            pltpu.make_async_copy(sources[number], held.at[number], load_sems.at[number]).start()

    wait_reuse(stage, sems, buf, step)
    for matrix in range(4):

        @pl.when(step == matrix)
        def _():
            for number in ((0, 1), (2, 3), (4,), (5,))[matrix]:
                wait_whole(held.at[number], load_sems.at[number])

    left = 2 * jnp.minimum(step, 1)
    stage[buf] = dot_tn(held[left], held[left + jnp.maximum(step, 1)]).astype(BF)
    first = lax.rem(step + 3, 4) * 8

    def body(piece, carry):
        far_core, slot = slot_of(first + piece, me)
        src = stage.at[buf, pl.ds(pl.multiple_of(piece * SLOT, 32), SLOT)]
        send_slot(parts, far_core, slot, 0, src, sems.at[buf])
        return carry

    lax.fori_loop(0, 8, body, 0)
    wait_last(stage, sems, step, 4)


def att_grads(ctx, dob, stream, dq, dk, dv):
    tok, width = stream.shape
    return pl.pallas_call(
        att_grad_kernel,
        grid=(4,),
        out_shape=part_shapes(width, False),
        in_specs=[spec_any()] * 6,
        out_specs=(spec_any(),) * 4,
        scratch_shapes=[
            pltpu.VMEM((6, tok, width), BF),
            pltpu.VMEM((2, width, width), BF),
            pltpu.SemaphoreType.DMA((6,)),
            pltpu.SemaphoreType.DMA((2,)),
        ],
        compiler_params=params(BIG),
        cost_estimate=pl.CostEstimate(
            flops=8 * tok * width * width, bytes_accessed=16 * MIB, transcendentals=0
        ),
        name="att_grads",
    )(ctx, dob, stream, dq, dk, dv)


def flat_ffn_kernel(a_ref, b_ref, out_ref):
    first = lax.axis_index("fsdp") < 16

    @pl.when(first)
    def _():
        for block in range(4):
            source = a_ref if block < 2 else b_ref
            rows = slice((block % 2) * 48, (block % 2) * 48 + 48)
            for part in range(6):
                cols = slice(part * LANES, (part + 1) * LANES)
                out_ref[pl.ds(6 * block + part, 48, stride=24), :] = source[rows, cols]

    @pl.when(jnp.logical_not(first))
    def _():
        for part in range(6):
            cols = slice(part * LANES, (part + 1) * LANES)
            out_ref[pl.ds(part, SLOT, stride=6), :] = a_ref[:, cols]
            out_ref[pl.ds(6 * SLOT + part, SLOT, stride=6), :] = b_ref[:, cols]


def flatten_ffn(grad_a, grad_b):
    return pl.pallas_call(
        flat_ffn_kernel,
        out_shape=jax.ShapeDtypeStruct((12 * SLOT, LANES), F32),
        in_specs=[spec_vmem()] * 2,
        out_specs=spec_vmem(),
        compiler_params=params(16),
        name="flatten_ffn",
    )(grad_a, grad_b)


def flat_att_kernel(kept_ref, got_ref, ffn_ref, late_ref, out_ref, head_ref):
    for part in range(6):
        cols = slice(part * LANES, (part + 1) * LANES)
        total = kept_ref[:, cols].astype(F32) + got_ref[0:SLOT, cols].astype(F32)
        out_ref[pl.ds(part, SLOT, stride=6), :] = total
    head_ref[0:64, :] = out_ref[0:64, :]
    head_ref[64:128, :] = ffn_ref[0:64, :]

    @pl.when(lax.axis_index("fsdp") == 0)
    def _():
        for part in range(6):
            cols = slice(part * LANES, (part + 1) * LANES)
            head_ref[pl.ds(part, 6, stride=6), :] = late_ref[0:6, cols]


def flatten_att(kept, got, ffn_flat, late):
    return pl.pallas_call(
        flat_att_kernel,
        out_shape=(
            jax.ShapeDtypeStruct((6 * SLOT, LANES), F32),
            jax.ShapeDtypeStruct((128, LANES), F32),
        ),
        in_specs=[spec_vmem()] * 4,
        out_specs=(spec_vmem(),) * 2,
        compiler_params=params(16),
        name="flatten_att",
    )(kept, got, ffn_flat, late)


def update_kernel(last, rate, *refs):
    inputs, outputs, bufs = refs[0:10], refs[10:18], refs[18:20]
    me = lax.axis_index("fsdp")
    head_ref, small_ref = inputs[2], inputs[3]
    for unit in range(2):
        flat_ref = inputs[unit]
        w_ref, m_ref, a_ref = inputs[4 + 3 * unit : 7 + 3 * unit]
        w_out, m_out, a_out, low_out = outputs[4 * unit : 4 * unit + 4]
        buf = bufs[unit]
        aligned = flat_ref.shape[0]
        first, count = ((0, 6), (6, 7))[unit]
        buf[0:aligned, :] = flat_ref[...]
        buf[aligned : aligned + 64, :] = head_ref[unit * 64 : unit * 64 + 64, :]

        @pl.when(me == last)
        def _():
            buf[aligned : aligned + 64, :] = jnp.zeros((64, LANES), F32)
            for part in range(6):
                cols = slice(part * LANES, (part + 1) * LANES)
                small = small_ref[first : first + count, cols]
                if unit == 0:
                    small = small + head_ref[pl.ds(part, count, stride=6), :]
                buf[pl.ds(aligned + part, count, stride=6), :] = small

        grad = buf[pl.ds(2 * me, w_ref.shape[0]), :]
        moment = 0.5 * m_ref[...] + grad
        master = w_ref[...] - rate * (grad + 0.5 * moment)
        m_out[...] = moment
        w_out[...] = master
        a_out[...] = 0.5 * a_ref[...] + 0.5 * master
        low_out[...] = master.astype(BF)


def update(flats, head, small, rate, devices, att, ffn):
    shapes = []
    for arrays in (att, ffn):
        f32 = jax.ShapeDtypeStruct(arrays[0].shape, F32)
        shapes += [f32, f32, f32, jax.ShapeDtypeStruct(arrays[0].shape, BF)]
    out = pl.pallas_call(
        functools.partial(update_kernel, devices - 1, rate),
        out_shape=tuple(shapes),
        in_specs=[spec_vmem()] * 10,
        out_specs=(spec_vmem(),) * 8,
        scratch_shapes=[pltpu.VMEM((flat.shape[0] + 64, LANES), F32) for flat in flats],
        compiler_params=params(16),
        name="update",
    )(*flats, head, small, *att, *ffn)
    return out


def local_exchange(
    block_input,
    seg_ids,
    masked,
    out_grad,
    att_master,
    att_moment,
    att_average,
    ffn_master,
    ffn_moment,
    ffn_average,
):
    tok, width = block_input.shape
    seq_count, seq = seg_ids.shape
    devices = lax.axis_size("fsdp")
    up = [(i, i + 1) for i in range(devices - 1)]
    down = [(i + 1, i) for i in range(devices - 1)]
    tails = lax.ppermute(row_tails(att_master, ffn_master), "fsdp", up)
    masked_row = masked.reshape(seq_count, 1, seq)
    seg_row = seg_ids.reshape(seq_count, 1, seq)
    att, chunk_a, chunk_b = prepare(att_master, ffn_master, tails, devices, width)
    got, masked_row, seg_row = phase(exchange(att, 0), masked_row, seg_row)
    att = widen_small(att, got)
    got = exchange(att, 1)
    att, unit_a = phase(widen_small(att, got), chunk_a)
    got, got_a = phase(exchange(att, 2), exchange(unit_a, 0))
    att, unit_a, unit_b = phase(widen_small(att, got), widen(unit_a, got_a), chunk_b)
    att_next, att_far, got_a, got_b = phase(
        exchange(att, 3), exchange(att, 4), exchange(unit_a, 1), exchange(unit_b, 0)
    )
    unit_a, unit_b, att_next = phase(widen(unit_a, got_a), widen(unit_b, got_b), att_next)
    att_last, got_b, block_input = phase(exchange(att_next, 4), exchange(unit_b, 2), block_input)
    att = (att, att_next, att_far, att_last)
    unit_a, unit_b, block_input = phase(unit_a, widen(unit_b, got_b), block_input)
    got_b = exchange(unit_b, 1)
    stream, qkv, small = project(block_input, masked_row, att)
    got_a, qkv = phase(exchange(unit_a, 2), qkv)
    unit_a, qkv = phase(widen(unit_a, got_a), qkv)
    held = attention_forward(0, qkv, seg_row)
    a_next, a_far, got_b, held = phase(exchange(unit_a, 3), exchange(unit_a, 4), got_b, held)
    unit_b, a_next, held = phase(widen(unit_b, got_b), a_next, held)
    ctx, lse = attention_forward(1, qkv, seg_row, held)
    b_next, b_far, a_last, ctx = phase(
        exchange(unit_b, 3), exchange(unit_b, 4), exchange(a_next, 4), ctx
    )
    b_last = exchange(b_next, 4)
    block_output, x_low, hidden, dhid, dfb, dob, dctx, sums = feed_forward(
        stream,
        ctx,
        out_grad,
        small,
        att,
        (unit_a, a_next, a_far, a_last),
        (unit_b, b_next, b_far, b_last),
    )
    part_a, part_b = ffn_grads(x_low, hidden, dhid, dfb, sums)
    part_b, dhid = phase(part_b, dhid)
    part_a = ffn_rest(x_low, dhid, part_a)
    high_b, low_b, part_a = phase(exchange(part_b[3], 4), exchange(part_b[2], 4), part_a)
    small_sum = sums + high_b[8 * SLOT :].astype(F32)
    high_b = add_small(total_of((part_b[1], high_b), 0, 8 * SLOT).astype(BF), small_sum)
    high_b, part_a, dctx = phase(high_b, part_a, dctx)
    held = attention_backward(0, qkv, dctx, lse, seg_row)
    got_b, high_a, low_a, held = phase(
        exchange(high_b, 3), exchange(part_a[3], 4), exchange(part_a[2], 4), held
    )
    high_a = total_of((part_a[1], high_a), 0, 8 * SLOT).astype(BF)
    small_sum = small_sum + got_b[8 * SLOT :].astype(F32)
    kept_b, sent_b = halve(part_b[0], low_b, got_b[: 8 * SLOT])
    high_a, sent_b, held = phase(high_a, add_small(sent_b, small_sum), held)
    dq, dk, dv = attention_backward(1, qkv, dctx, lse, seg_row, held)
    got_a, got_b, dq = phase(exchange(high_a, 3), exchange(sent_b, 1), dq)
    kept_a, sent_a = halve(part_a[0], low_a, got_a)
    small_sum = small_sum + got_b[4 * SLOT :].astype(F32)
    kept_b, sent_b = halve(kept_b, got_b[: 4 * SLOT])
    sent_a, sent_b, dq = phase(sent_a, add_small(sent_b, small_sum), dq)
    part = att_grads(ctx, dob, stream, dq, dk, dv)
    high = exchange(part[3], 4)
    got_a, got_b, kept = phase(exchange(sent_a, 2), exchange(sent_b, 2), part[0])
    kept_a, sent_a = halve(kept_a, got_a)
    small_sum = small_sum + got_b[2 * SLOT :].astype(F32)
    kept_b, sent_b = halve(kept_b, got_b[: 2 * SLOT])
    high, sent_a, sent_b = phase(high, sent_a, add_small(sent_b, small_sum))
    got_b = exchange(sent_b, 0)
    high = total_of((part[1], high), 0, 8 * SLOT).astype(BF)
    high, sent_a, dq = phase(high, sent_a, dq)
    input_grad, late = input_grads(dq, dk, dv, dob, masked_row, att)
    got, low, got_a, got_b, late = phase(
        exchange(high, 3), exchange(part[2], 4), exchange(sent_a, 1), got_b, late
    )
    kept, sent = halve(kept, low, got)
    kept_a, sent_a = halve(kept_a, got_a)
    sent, sent_a, late = phase(sent, sent_a, late)
    got, got_a = phase(exchange(add_small(sent, late), 2), exchange(sent_a, 0))
    late = late + got[4 * SLOT :].astype(F32)
    kept, sent = halve(kept, got[: 4 * SLOT])
    sent, late, got_a, got_b = phase(sent, late, got_a, got_b)
    got = exchange(sent, 1)
    late = late + exchange(late.astype(BF), 3).astype(F32)
    late = late + exchange(late.astype(BF), 4).astype(F32)
    kept, sent = halve(kept, got)
    sent, got_a, got_b = phase(add_small(sent, late), got_a, got_b)
    got = exchange(sent, 0)
    small_sum = small_sum + got_b[SLOT:].astype(F32)
    grad_a = total_of((kept_a, got_a), 0, SLOT)
    grad_b = total_of((kept_b, got_b), 0, SLOT)
    ffn_flat = flatten_ffn(grad_a, grad_b)
    got, ffn_flat, small_sum = phase(got, ffn_flat, small_sum)
    late = late + got[SLOT:].astype(F32)
    att_flat, heads = flatten_att(kept, got, ffn_flat, late)
    heads = lax.ppermute(heads, "fsdp", down + [(0, devices - 1)])
    rate = 0.05 / math.sqrt(tok * devices)
    new = update(
        (att_flat, ffn_flat),
        heads,
        small_sum + late,
        rate,
        devices,
        (att_master, att_moment, att_average),
        (ffn_master, ffn_moment, ffn_average),
    )
    return (block_output, input_grad) + tuple(new)


def chunked(mesh):
    return mesh.shape["fsdp"] == 32


def solution(mesh):
    in_specs = (
        P("fsdp", None),
        P("fsdp", None),
        P("fsdp", None),
        P("fsdp", None),
        P("fsdp", None),
        P("fsdp", None),
        P("fsdp", None),
        P("fsdp", None),
        P("fsdp", None),
        P("fsdp", None),
    )
    out_specs = (
        P("fsdp", None),
        P("fsdp", None),
        P("fsdp", None),
        P("fsdp", None),
        P("fsdp", None),
        P("fsdp", None),
        P("fsdp", None),
        P("fsdp", None),
        P("fsdp", None),
        P("fsdp", None),
    )
    body = local_exchange if chunked(mesh) else local
    return jax.shard_map(body, mesh=mesh, in_specs=in_specs, out_specs=out_specs, check_vma=False)
```

```python
import functools
import math

import jax
import jax.numpy as jnp
from jax import lax
from jax.experimental import pallas as pl
from jax.experimental.pallas import tpu as pltpu
from jax.sharding import PartitionSpec as P

HEAD_DIM = 64
FF = 3072


EPSILON = 1e-05
MASKED_SCORE = -1e30


def layer_norm(pre_norm, gain, shift):
    center = pre_norm - jnp.mean(pre_norm, axis=-1, keepdims=True)
    spread = jnp.mean(center * center, axis=-1, keepdims=True)
    return center * lax.rsqrt(spread + EPSILON) * gain + shift


def gelu_exact(inputs):
    return jax.nn.gelu(inputs, approximate=False)


def unpack_attention(flat_att, model_width):
    square = model_width * model_width
    att_mats = flat_att[: 4 * square].reshape(4, model_width, model_width)
    small_params = flat_att[4 * square : 4 * square + 6 * model_width].reshape(6, model_width)
    return (att_mats, small_params)


def unpack_ffn(flat_ffn, model_width, hidden):
    size_in = model_width * hidden
    weight_in = flat_ffn[:size_in].reshape(model_width, hidden)
    weight_out = flat_ffn[size_in : 2 * size_in].reshape(hidden, model_width)
    offset = 2 * size_in
    bias_in = flat_ffn[offset : offset + hidden]
    small_params = flat_ffn[offset + hidden : offset + hidden + 3 * model_width].reshape(
        3, model_width
    )
    return (weight_in, weight_out, bias_in, small_params)


def pack_rows(pieces, row_count):
    filled = sum((piece.shape[0] for piece in pieces))
    padding = jnp.zeros((row_count * 128 - filled,), jnp.float32)
    return jnp.concatenate(list(pieces) + [padding]).reshape(row_count, 128)


def attend_forward(block_items):
    query_block, key_block, value_block, doc_block = block_items
    scores = jnp.einsum("qhd,khd->hqk", query_block, key_block, preferred_element_type=jnp.float32)
    same_doc = doc_block[:, None] == doc_block[None, :]
    scores = jnp.where(same_doc[None], scores, MASKED_SCORE)
    row_max = jnp.max(scores, axis=-1, keepdims=True)
    exponent = jnp.exp(scores - row_max)
    row_total = jnp.sum(exponent, axis=-1, keepdims=True)
    attn_probs = (exponent / row_total).astype(jnp.bfloat16)
    context = jnp.einsum(
        "hqk,khd->qhd", attn_probs, value_block, preferred_element_type=jnp.float32
    )
    return (context.astype(jnp.bfloat16), (row_max + jnp.log(row_total))[..., 0])


def attend_backward(block_items):
    query_block, key_block, value_block, doc_block, log_total, grad_context = block_items
    scores = jnp.einsum("qhd,khd->hqk", query_block, key_block, preferred_element_type=jnp.float32)
    same_doc = doc_block[:, None] == doc_block[None, :]
    scores = jnp.where(same_doc[None], scores, MASKED_SCORE)
    attn_probs = jnp.exp(scores - log_total[..., None])
    probs_low = attn_probs.astype(jnp.bfloat16)
    grad_probs = jnp.einsum(
        "qhd,khd->hqk", grad_context, value_block, preferred_element_type=jnp.float32
    )
    row_inner = jnp.sum(grad_probs * attn_probs, axis=-1, keepdims=True)
    grad_scores = (attn_probs * (grad_probs - row_inner)).astype(jnp.bfloat16)
    grad_query = jnp.einsum(
        "hqk,khd->qhd", grad_scores, key_block, preferred_element_type=jnp.float32
    ).astype(jnp.bfloat16)
    grad_key = jnp.einsum(
        "hqk,qhd->khd", grad_scores, query_block, preferred_element_type=jnp.float32
    ).astype(jnp.bfloat16)
    grad_value = jnp.einsum(
        "hqk,qhd->khd", probs_low, grad_context, preferred_element_type=jnp.float32
    ).astype(jnp.bfloat16)
    return (grad_query, grad_key, grad_value)


def nesterov(master, moment, average, gradient, step_rate):
    moment_new = 0.5 * moment + gradient
    master_new = master - step_rate * (gradient + 0.5 * moment_new)
    average_new = 0.5 * average + 0.5 * master_new
    return (master_new, moment_new, average_new, master_new.astype(jnp.bfloat16))


def local(
    block_input,
    seg_ids,
    masked,
    out_grad,
    att_master,
    att_moment,
    att_average,
    ffn_master,
    ffn_moment,
    ffn_average,
):
    tok_rows, model_width = block_input.shape
    seq_count, seq_length = seg_ids.shape
    head_count = model_width // HEAD_DIM
    devices = lax.axis_size("fsdp")
    att_rows = att_master.shape[0] * devices
    ffn_rows = ffn_master.shape[0] * devices
    head_shape = (seq_count, seq_length, head_count, HEAD_DIM)
    att_whole = lax.all_gather(att_master.astype(jnp.bfloat16), "fsdp", axis=0, tiled=True)
    att_mats, att_small_low = unpack_attention(att_whole.reshape(-1), model_width)
    att_small = att_small_low.astype(jnp.float32)
    masked_rows = masked.reshape(tok_rows, 1) == 1
    stream_in = jnp.where(masked_rows, att_small[5][None, :], block_input.astype(jnp.float32))
    stream_low = stream_in.astype(jnp.bfloat16)
    projected = jnp.einsum(
        "td,cde->cte", stream_low, att_mats[:3], preferred_element_type=jnp.float32
    )
    queries = ((projected[0] + att_small[0]) * 0.125).astype(jnp.bfloat16).reshape(head_shape)
    key_rows = projected[1].astype(jnp.bfloat16).reshape(head_shape)
    values = (projected[2] + att_small[1]).astype(jnp.bfloat16).reshape(head_shape)
    context, log_total = lax.map(attend_forward, (queries, key_rows, values, seg_ids))
    context_flat = context.reshape(tok_rows, model_width)
    pre_one = (
        stream_in
        + jnp.dot(context_flat, att_mats[3], preferred_element_type=jnp.float32)
        + att_small[2]
    )
    normed_one = layer_norm(pre_one, att_small[3], att_small[4])
    normed_low = normed_one.astype(jnp.bfloat16)
    ffn_whole = lax.all_gather(ffn_master.astype(jnp.bfloat16), "fsdp", axis=0, tiled=True)
    weight_in, weight_out, bias_in_low, ffn_small_low = unpack_ffn(
        ffn_whole.reshape(-1), model_width, FF
    )
    bias_in = bias_in_low.astype(jnp.float32)
    ffn_small = ffn_small_low.astype(jnp.float32)
    hid_pre = jnp.dot(normed_low, weight_in, preferred_element_type=jnp.float32) + bias_in
    hid_act = gelu_exact(hid_pre).astype(jnp.bfloat16)
    pre_two = (
        normed_one + jnp.dot(hid_act, weight_out, preferred_element_type=jnp.float32) + ffn_small[0]
    )
    normed_two, norm_two_pull = jax.vjp(layer_norm, pre_two, ffn_small[1], ffn_small[2])
    block_output = normed_two.astype(jnp.bfloat16)
    ffn_back = lax.all_gather(ffn_master.astype(jnp.bfloat16), "fsdp", axis=0, tiled=True)
    back_in, back_out, bias_unused, small_unused = unpack_ffn(ffn_back.reshape(-1), model_width, FF)
    grad_pre_two, grad_gain_two, grad_shift_two = norm_two_pull(out_grad.astype(jnp.float32))
    grad_branch_two = grad_pre_two.astype(jnp.bfloat16)
    grad_w_out = jnp.einsum(
        "tf,td->fd", hid_act, grad_branch_two, preferred_element_type=jnp.float32
    )
    grad_b_out = jnp.sum(grad_branch_two, axis=0, dtype=jnp.float32)
    grad_act = jnp.einsum(
        "td,fd->tf", grad_branch_two, back_out, preferred_element_type=jnp.float32
    )
    hid_unused, gelu_pull = jax.vjp(gelu_exact, hid_pre)
    grad_hidden = gelu_pull(grad_act)[0].astype(jnp.bfloat16)
    grad_w_in = jnp.einsum("td,tf->df", normed_low, grad_hidden, preferred_element_type=jnp.float32)
    grad_b_in = jnp.sum(grad_hidden, axis=0, dtype=jnp.float32)
    grad_normed_one = grad_pre_two + jnp.einsum(
        "tf,df->td", grad_hidden, back_in, preferred_element_type=jnp.float32
    )
    ffn_flat_grad = pack_rows(
        (
            grad_w_in.reshape(-1),
            grad_w_out.reshape(-1),
            grad_b_in,
            grad_b_out,
            grad_gain_two,
            grad_shift_two,
        ),
        ffn_rows,
    )
    ffn_grad = lax.psum_scatter(ffn_flat_grad, "fsdp", scatter_dimension=0, tiled=True)
    att_back = lax.all_gather(att_master.astype(jnp.bfloat16), "fsdp", axis=0, tiled=True)
    back_mats, small_back = unpack_attention(att_back.reshape(-1), model_width)
    pre_unused, norm_one_pull = jax.vjp(layer_norm, pre_one, att_small[3], att_small[4])
    grad_pre_one, grad_gain_one, grad_shift_one = norm_one_pull(grad_normed_one)
    grad_branch_one = grad_pre_one.astype(jnp.bfloat16)
    grad_w_o = jnp.einsum(
        "td,te->de", context_flat, grad_branch_one, preferred_element_type=jnp.float32
    )
    grad_b_o = jnp.sum(grad_branch_one, axis=0, dtype=jnp.float32)
    grad_context = jnp.einsum(
        "te,de->td", grad_branch_one, back_mats[3], preferred_element_type=jnp.float32
    ).astype(jnp.bfloat16)
    grad_q4, grad_k4, grad_v4 = lax.map(
        attend_backward,
        (queries, key_rows, values, seg_ids, log_total, grad_context.reshape(head_shape)),
    )
    grad_queries = grad_q4.reshape(tok_rows, model_width) * 0.125
    grad_keys = grad_k4.reshape(tok_rows, model_width)
    grad_values = grad_v4.reshape(tok_rows, model_width)
    grad_projected = jnp.stack([grad_queries, grad_keys, grad_values])
    grad_w_qkv = jnp.einsum(
        "td,cte->cde", stream_low, grad_projected, preferred_element_type=jnp.float32
    )
    grad_b_q = jnp.sum(grad_queries, axis=0, dtype=jnp.float32)
    grad_b_v = jnp.sum(grad_values, axis=0, dtype=jnp.float32)
    grad_stream = grad_pre_one + jnp.einsum(
        "cte,cde->td", grad_projected, back_mats[:3], preferred_element_type=jnp.float32
    )
    grad_mask_vector = jnp.sum(jnp.where(masked_rows, grad_stream, 0.0), axis=0)
    input_grad = jnp.where(masked_rows, 0.0, grad_stream)
    att_flat_grad = pack_rows(
        (
            grad_w_qkv.reshape(-1),
            grad_w_o.reshape(-1),
            grad_b_q,
            grad_b_v,
            grad_b_o,
            grad_gain_one,
            grad_shift_one,
            grad_mask_vector,
        ),
        att_rows,
    )
    att_grad = lax.psum_scatter(att_flat_grad, "fsdp", scatter_dimension=0, tiled=True)
    step_rate = 0.05 / math.sqrt(tok_rows * devices)
    att_new = nesterov(att_master, att_moment, att_average, att_grad, step_rate)
    ffn_new = nesterov(ffn_master, ffn_moment, ffn_average, ffn_grad, step_rate)
    return (
        block_output,
        input_grad,
        att_new[0],
        att_new[1],
        att_new[2],
        att_new[3],
        ffn_new[0],
        ffn_new[1],
        ffn_new[2],
        ffn_new[3],
    )


BF = jnp.bfloat16
F32 = jnp.float32
LANES = 128
SLOT = 96
TILE = 256
FFN_TILE = 512
FFN_SPLIT = 2
FWD_PAIRS = 1
BWD_PAIRS = 2
EXTRA = 16
MIB = 1 << 20
BIG = 58


def params(limit):
    return pltpu.CompilerParams(vmem_limit_bytes=limit * MIB)


def spec_any():
    return pl.BlockSpec(memory_space=pl.ANY)


def spec_vmem():
    return pl.BlockSpec(memory_space=pltpu.VMEM)


def spec_whole(shape):
    return pl.BlockSpec(shape, lambda *ids: (0,) * len(shape))


def dot_nn(left, right):
    return lax.dot_general(left, right, (((1,), (0,)), ((), ())), preferred_element_type=F32)


def dot_nt(left, right):
    return lax.dot_general(left, right, (((1,), (1,)), ((), ())), preferred_element_type=F32)


def dot_tn(left, right):
    return lax.dot_general(left, right, (((0,), (0,)), ((), ())), preferred_element_type=F32)


def slot_of(chunk, me, late=False):
    diff = lax.bitwise_xor(me, chunk)
    far_core = lax.bitwise_and(diff, 1)
    x_bit = lax.bitwise_and(lax.shift_right_logical(diff, 1), 1)
    y_bit = lax.bitwise_and(lax.shift_right_logical(diff, 2), 1)
    z_low = lax.bitwise_and(lax.shift_right_logical(diff, 3), 1)
    z_high = lax.shift_right_logical(diff, 4)
    core = lax.bitwise_xor(lax.bitwise_and(me, 1), far_core)
    third = x_bit + core * (y_bit - x_bit)
    fourth = y_bit + core * (x_bit - y_bit)
    if late:
        return far_core, z_high + 2 * third + 4 * z_low + 8 * fourth
    return far_core, z_high + 2 * z_low + 4 * third + 8 * fourth


def bit(value, place):
    return lax.bitwise_and(lax.shift_right_logical(value, place), 1)


def chunk_of(part, slot, me, late=False):
    third, z_low = (bit(slot, 1), bit(slot, 2)) if late else (bit(slot, 2), bit(slot, 1))
    far_core, fourth = part >> 1, part & 1
    rest = far_core + 8 * z_low + 16 * bit(slot, 0)
    first_core = rest + 2 * third + 4 * fourth
    other_core = rest + 4 * third + 2 * fourth
    core = lax.bitwise_xor(bit(me, 0), far_core)
    return lax.bitwise_xor(me, first_core + core * (other_core - first_core))


def stage_perm(stage):
    if stage == 0:
        return [(i, i ^ 16) for i in range(32)]
    if stage == 1:
        return [(i, i ^ 8) for i in range(32)]
    if stage == 2:
        return [(i, i ^ (4 if i & 1 else 2)) for i in range(32)]
    if stage == 3:
        return [(i, i ^ (2 if i & 1 else 4)) for i in range(32)]
    return [(i, i ^ 1) for i in range(32)]


def exchange(array, stage):
    return lax.ppermute(array, "fsdp", stage_perm(stage))


def widen(held, got):
    return jnp.concatenate([held, got])


def widen_small(held, got):
    low = held.shape[0] - EXTRA
    small = held[low:] + got[low:]
    return jnp.concatenate([held[:low], got[:low], small])


def total_of(arrays, first, last):
    total = arrays[0][first:last].astype(F32)
    for array in arrays[1:]:
        total = total + array[first:last].astype(F32)
    return total


def halve(*arrays):
    rows = arrays[0].shape[0]
    low = total_of(arrays, 0, rows // 2).astype(BF)
    return low, total_of(arrays, rows // 2, rows).astype(BF)


def add_small(values, small):
    return jnp.concatenate([values, small.astype(BF)])


def phase(*values):
    return lax.optimization_barrier(values)


def tail_kernel(att_ref, ffn_ref, out_ref, buf, sems):
    refs = (att_ref, ffn_ref)
    starts = [(ref.shape[0] - 64) // 8 * 8 for ref in refs]
    copies = []
    for number in range(2):
        rows = refs[number].shape[0] - starts[number]
        src = refs[number].at[starts[number] :, :]
        copies.append(pltpu.make_async_copy(src, buf.at[number, 0:rows, :], sems.at[number]))
        copies[number].start()
    for number in range(2):
        rows = refs[number].shape[0] - starts[number]
        copies[number].wait()
        out_ref[number * 64 : number * 64 + 64, :] = buf[number, rows - 64 : rows, :]


def row_tails(att_master, ffn_master):
    return pl.pallas_call(
        tail_kernel,
        out_shape=jax.ShapeDtypeStruct((128, LANES), F32),
        in_specs=[spec_any()] * 2,
        out_specs=spec_vmem(),
        scratch_shapes=[pltpu.VMEM((2, 72, LANES), F32), pltpu.SemaphoreType.DMA((2,))],
        compiler_params=params(BIG),
        name="row_tails",
    )(att_master, ffn_master)


def prep_kernel(last, att_mats, ffn_mats, att_ref, ffn_ref, tail_ref, *refs):
    att_out, ffn_a, ffn_b, att_buf, ffn_buf = refs
    me = lax.axis_index("fsdp")
    att_rows = att_ref.shape[0]
    ffn_rows = ffn_ref.shape[0]
    att_buf[0:64, :] = tail_ref[0:64, :]
    att_buf[64 : 64 + att_rows, :] = att_ref[...]
    ffn_buf[0:64, :] = tail_ref[64:128, :]
    ffn_buf[64 : 64 + ffn_rows, :] = ffn_ref[...]
    start = 64 - 2 * me
    for part in range(6):
        cols = slice(part * LANES, (part + 1) * LANES)
        att_out[0:SLOT, cols] = att_buf[pl.ds(start + part, SLOT, stride=6), :].astype(BF)
    att_out[SLOT:, :] = jnp.zeros((EXTRA, att_out.shape[1]), BF)
    first = me < 16

    @pl.when(first)
    def _():
        for block in range(4):
            out = ffn_a if block < 2 else ffn_b
            rows = slice((block % 2) * 48, (block % 2) * 48 + 48)
            for part in range(6):
                cols = slice(part * LANES, (part + 1) * LANES)
                piece = ffn_buf[pl.ds(start + 6 * block + part, 48, stride=24), :]
                out[rows, cols] = piece.astype(BF)

    @pl.when(jnp.logical_not(first))
    def _():
        for part in range(6):
            cols = slice(part * LANES, (part + 1) * LANES)
            ffn_a[:, cols] = ffn_buf[pl.ds(start + part, SLOT, stride=6), :].astype(BF)
            ffn_b[:, cols] = ffn_buf[pl.ds(start + 6 * SLOT + part, SLOT, stride=6), :].astype(BF)

    @pl.when(me == last)
    def _():
        att_at = 64 + att_mats - last * att_rows
        ffn_at = 64 + ffn_mats - last * ffn_rows
        for part in range(6):
            cols = slice(part * LANES, (part + 1) * LANES)
            upper = att_buf[pl.ds(att_at + part, 6, stride=6), :]
            lower = ffn_buf[pl.ds(ffn_at + part, 7, stride=6), :]
            both = jnp.concatenate([upper, lower, jnp.zeros((3, LANES), F32)])
            att_out[SLOT:, cols] = both.astype(BF)


def prepare(att_master, ffn_master, tails, devices, width):
    att_mats = 4 * width * width // LANES
    ffn_mats = 2 * width * FF // LANES
    att_rows, ffn_rows = att_master.shape[0], ffn_master.shape[0]
    body = functools.partial(prep_kernel, devices - 1, att_mats, ffn_mats)
    return pl.pallas_call(
        body,
        out_shape=(
            jax.ShapeDtypeStruct((SLOT + EXTRA, width), BF),
            jax.ShapeDtypeStruct((SLOT, width), BF),
            jax.ShapeDtypeStruct((SLOT, width), BF),
        ),
        in_specs=[spec_vmem()] * 3,
        out_specs=(spec_vmem(),) * 3,
        scratch_shapes=[
            pltpu.VMEM((64 + att_rows + 6, LANES), F32),
            pltpu.VMEM((64 + ffn_rows + 30, LANES), F32),
        ],
        compiler_params=params(16),
        name="prep",
    )(att_master, ffn_master, tails)


def pick(index, refs, use):
    for number in range(len(refs)):

        @pl.when(index == number)
        def _():
            use(refs[number])


def each_slot(body):
    def step(slot, carry):
        for part in range(4):
            body(part, slot)
        return carry

    lax.fori_loop(0, 8, step, 0)


def load_projections(quad, dst, sems):
    me = lax.axis_index("fsdp")

    def body(part, slot):
        chunk = chunk_of(part, slot, me)

        @pl.when(chunk < 24)
        def _():
            at = pl.multiple_of(chunk * SLOT, 32)
            src = quad[part].at[pl.ds(pl.multiple_of(slot * SLOT, 32), SLOT), :]
            sem = sems.at[lax.shift_right_logical(chunk, 3)]
            pltpu.make_async_copy(src, dst.at[pl.ds(at, SLOT), :], sem).start()

    each_slot(body)


def load_output(quad, dst, sem):
    me = lax.axis_index("fsdp")
    planes = (1 - bit(me, 4)) + 2 * (1 - bit(me, 3))

    def step(third, carry):
        slot = planes + 4 * third
        for part in range(4):
            at = pl.multiple_of((chunk_of(part, slot, me) - 24) * SLOT, 32)
            src = quad[part].at[pl.ds(pl.multiple_of(slot * SLOT, 32), SLOT), :]
            pltpu.make_async_copy(src, dst.at[pl.ds(at, SLOT), :], sem).start()
        return carry

    lax.fori_loop(0, 2, step, 0)


def load_ffn(quads, w_in, w_out, sem_in, sem_out):
    me = lax.axis_index("fsdp")
    for unit in range(2):

        def body(part, slot):
            chunk = chunk_of(part, slot, me, unit == 1)
            src = quads[unit][part].at[slot]

            @pl.when(chunk < 16)
            def _():
                at = pl.multiple_of(chunk * 48, 16)
                dst = w_in.at[2 * unit : 2 * unit + 2, pl.ds(at, 48), :]
                pltpu.make_async_copy(src, dst, sem_in.at[unit]).start()

            @pl.when(chunk >= 16)
            def _():
                dst = w_out.at[2 * (chunk - 16) + unit]
                pltpu.make_async_copy(src, dst, sem_out).start()

        each_slot(body)


def wait_whole(ref, sem):
    pltpu.make_async_copy(ref, ref, sem).wait()


def as_column(row):
    return jnp.broadcast_to(row.astype(F32), (8, row.shape[1])).T[:, 0:1]


def head_mask(rows):
    lane = lax.broadcasted_iota(jnp.int32, (rows, LANES), 1)
    return lane < HEAD_DIM


def project_kernel(x_ref, masked_ref, *refs):
    quad = refs[0:4]
    stream_ref, qkv_ref, small_ref, weights, smalls, sems, small_sem = refs[4:]
    width = x_ref.shape[1]

    @pl.when(pl.program_id(0) == 0)
    def _():
        for part in range(4):
            src = quad[part].at[pl.ds(8 * SLOT, EXTRA), :]
            pltpu.make_async_copy(src, smalls.at[part], small_sem).start()
        load_projections(quad, weights, sems)
        wait_whole(smalls, small_sem)
        total = smalls[0].astype(F32)
        for part in range(1, 4):
            total = total + smalls[part].astype(F32)
        small_ref[...] = total

    small = small_ref[...]
    stream = jnp.where(as_column(masked_ref[0]) == 1.0, small[5:6], x_ref[...].astype(F32)).astype(BF)
    stream_ref[...] = stream

    def body(matrix, carry):
        rows = pl.ds(pl.multiple_of(matrix * width, width), width)

        @pl.when(pl.program_id(0) == 0)
        def _():
            wait_whole(weights.at[rows], sems.at[matrix])

        odd = lax.rem(matrix, 2)
        bias = small_ref[pl.ds(lax.div(matrix, 2), 1), :] * (1.0 - odd.astype(F32))
        scale = jnp.where(matrix == 0, 0.125, 1.0)
        product = dot_nn(stream_ref[...], weights[rows])
        qkv_ref[matrix] = ((product + bias) * scale).astype(BF)
        return carry

    lax.fori_loop(0, 3, body, 0)


def project(block_input, masked_row, quad):
    tok, width = block_input.shape
    rows = masked_row.shape[2]
    tile = lambda cols: pl.BlockSpec((rows, cols), lambda s: (s, 0))
    bf = jax.ShapeDtypeStruct((tok, width), BF)
    return pl.pallas_call(
        project_kernel,
        grid=(tok // rows,),
        out_shape=(
            bf,
            jax.ShapeDtypeStruct((3, tok, width), BF),
            jax.ShapeDtypeStruct((EXTRA, width), F32),
        ),
        in_specs=[tile(width), pl.BlockSpec((1, 1, rows), lambda s: (s, 0, 0))] + [spec_any()] * 4,
        out_specs=(
            tile(width),
            pl.BlockSpec((3, rows, width), lambda s: (0, s, 0)),
            spec_whole((EXTRA, width)),
        ),
        scratch_shapes=[
            pltpu.VMEM((3 * width, width), BF),
            pltpu.VMEM((4, EXTRA, width), BF),
            pltpu.SemaphoreType.DMA((3,)),
            pltpu.SemaphoreType.DMA,
        ],
        compiler_params=params(BIG),
        cost_estimate=pl.CostEstimate(
            flops=6 * tok * width * width, bytes_accessed=16 * MIB, transcendentals=0
        ),
        name="project",
    )(block_input, masked_row, *quad)


def forward_kernel(held, q_ref, k_ref, v_ref, seg_row_ref, *refs):
    ctx_ref, lse_ref = refs[held:]
    left = head_mask(q_ref.shape[0])
    same = as_column(seg_row_ref[0]) == seg_row_ref[0].astype(F32)
    for pair in range(FWD_PAIRS):
        cols = slice(pair * LANES, (pair + 1) * LANES)
        queries = q_ref[:, cols]
        keys = k_ref[:, cols]
        values_t = v_ref[:, cols].T
        outs = []
        for head in range(2):
            keep = left if head == 0 else jnp.logical_not(left)
            own = jnp.where(keep, queries, jnp.zeros_like(queries))
            scores = jnp.where(same, dot_nt(keys, own), MASKED_SCORE)
            top = jnp.max(scores, axis=0, keepdims=True)
            exponent = jnp.exp(scores - top)
            total = jnp.sum(exponent, axis=0, keepdims=True)
            probs = (exponent * (1.0 / total)).astype(BF)
            lse_ref[0, pair, head : head + 1, :] = top + jnp.log(total)
            outs.append(dot_nn(values_t[head * HEAD_DIM : (head + 1) * HEAD_DIM], probs))
        ctx_ref[:, cols] = jnp.concatenate(outs).T.astype(BF)


def sequence_specs(at, seq, pairs):
    tile = lambda: pl.BlockSpec((seq, pairs * LANES), lambda i: (at, i))
    row = lambda: pl.BlockSpec((1, 1, seq), lambda i: (at, 0, 0))
    part = lambda which: pl.BlockSpec((None, seq, pairs * LANES), lambda i: (which, at, i))
    stat = lambda: pl.BlockSpec((1, pairs, 2, seq), lambda i: (at, i, 0, 0))
    return tile, row, stat, [part(0), part(1), part(2)]


def attention_forward(at, qkv, seg_row, held=()):
    tok, width = qkv.shape[1:]
    seq_count, seq = seg_row.shape[0], seg_row.shape[2]
    pairs = width // LANES
    tile, row, stat, parts = sequence_specs(at, seq, FWD_PAIRS)
    return pl.pallas_call(
        functools.partial(forward_kernel, len(held)),
        grid=(pairs // FWD_PAIRS,),
        out_shape=(
            jax.ShapeDtypeStruct((tok, width), BF),
            jax.ShapeDtypeStruct((seq_count, pairs, 2, seq), F32),
        ),
        in_specs=parts + [row()] + [spec_any() for _ in held],
        out_specs=(tile(), stat()),
        input_output_aliases={4 + i: i for i in range(len(held))},
        compiler_params=params(BIG),
        cost_estimate=pl.CostEstimate(
            flops=16 * seq * seq * width,
            bytes_accessed=4 * MIB,
            transcendentals=seq * seq * width // HEAD_DIM,
        ),
        name="attention_forward",
    )(qkv, qkv, qkv, seg_row, *held)


def norm_stats(pre_norm):
    center = pre_norm - jnp.mean(pre_norm, axis=-1, keepdims=True)
    scale = lax.rsqrt(jnp.mean(center * center, axis=-1, keepdims=True) + EPSILON)
    return center * scale, scale


def norm_back(grad, gain, normed, scale):
    scaled = grad * gain
    mean_one = jnp.mean(scaled, axis=-1, keepdims=True)
    mean_two = jnp.mean(scaled * normed, axis=-1, keepdims=True)
    return scale * (scaled - mean_one - normed * mean_two)


def column_sum(array):
    return jnp.sum(array, axis=0, keepdims=True)


def gelu_pair(inputs):
    phi_cdf = 0.5 + 0.5 * lax.erf(inputs * math.sqrt(0.5))
    density = jnp.exp(inputs * inputs * -0.5) * (1.0 / math.sqrt(2.0 * math.pi))
    return inputs * phi_cdf, phi_cdf + inputs * density


def ffn_kernel(
    stream_ref,
    ctx_ref,
    grad_ref,
    small_ref,
    *refs,
):
    att_quad, quad_a, quad_b = refs[0:4], refs[4:8], refs[8:12]
    y_ref, x1_ref, hid_ref, dhid_ref, dfb_ref, dob_ref, dctx_ref, sums_ref = refs[12:20]
    w_in, w_out, w_o, slope, sem_in, sem_out, sem_o = refs[20:]
    width = ctx_ref.shape[1]
    step = pl.program_id(0)

    @pl.when(step == 0)
    def _():
        load_output(att_quad, w_o, sem_o)
        load_ffn((quad_a, quad_b), w_in, w_out, sem_in, sem_out)
        sums_ref[...] = jnp.zeros_like(sums_ref)
        wait_whole(w_o, sem_o)

    def block_cols(block):
        return slice(block * width, (block + 1) * width)

    def out_rows(block):
        return w_out[8 * block : 8 * block + 8].reshape(width, width)

    @pl.when(step == 0)
    def _():
        wait_whole(w_in.at[0:2], sem_in.at[0])
        wait_whole(w_in.at[2:4], sem_in.at[1])
        wait_whole(w_out, sem_out)

    small = small_ref[...]
    halves = range(FFN_SPLIT)
    size = FFN_TILE // FFN_SPLIT
    rows = [slice(part * size, (part + 1) * size) for part in halves]
    state = [{} for part in halves]

    def first_norm(part):
        own = state[part]
        pre_one = stream_ref[rows[part]].astype(F32) + dot_nn(ctx_ref[rows[part]], w_o[...])
        normed, own["scale"] = norm_stats(pre_one + small[2:3])
        own["normed"] = normed
        x_one = normed * small[3:4] + small[4:5]
        own["x"] = x_one.astype(BF)
        x1_ref[rows[part]] = own["x"]
        own["total"] = x_one + small[10:11]

    def forward(part, block):
        own = state[part]
        product = dot_nn(own["x"], w_in[block])
        hidden, gate = gelu_pair(product + small[6 + block : 7 + block])
        hidden = hidden.astype(BF)
        hid_ref[rows[part], block_cols(block)] = hidden
        slope[block, rows[part]] = gate
        own["total"] = own["total"] + dot_nn(hidden, out_rows(block))

    def second_norm(part):
        own = state[part]
        normed, scale = norm_stats(own["total"])
        y_ref[rows[part]] = (normed * small[11:12] + small[12:13]).astype(BF)
        grad_out = grad_ref[rows[part]].astype(F32)
        grad_two = norm_back(grad_out, small[11:12], normed, scale)
        own["low"] = grad_two.astype(BF)
        own["grad"] = grad_two
        dfb_ref[rows[part]] = own["low"]
        sums_ref[10:11] += column_sum(own["low"].astype(F32))
        sums_ref[11:12] += column_sum(grad_out * normed)
        sums_ref[12:13] += column_sum(grad_out)

    def backward(part, block):
        own = state[part]
        product = dot_nt(own["low"], out_rows(block))
        dhid = (product * slope[block, rows[part]]).astype(BF)
        dhid_ref[rows[part], block_cols(block)] = dhid
        sums_ref[6 + block : 7 + block] += column_sum(dhid.astype(F32))
        own["grad"] = own["grad"] + dot_nt(dhid, w_in[block])

    def last_norm(part):
        own = state[part]
        grad_one = own["grad"]
        sums_ref[3:4] += column_sum(grad_one * own["normed"])
        sums_ref[4:5] += column_sum(grad_one)
        dob = norm_back(grad_one, small[3:4], own["normed"], own["scale"]).astype(BF)
        dob_ref[rows[part]] = dob
        sums_ref[2:3] += column_sum(dob.astype(F32))
        dctx_ref[rows[part]] = dot_nt(dob, w_o[...]).astype(BF)

    for part in halves:
        first_norm(part)
    for block in range(FF // width):
        for part in halves:
            forward(part, block)
    for part in halves:
        second_norm(part)
    for block in range(FF // width):
        for part in halves:
            backward(part, block)
    for part in halves:
        last_norm(part)


def feed_forward(stream, ctx, out_grad, small, att_quad, quad_a, quad_b):
    tok, width = ctx.shape
    slots = (8, 2, 48, width)
    quad_a = [array.reshape(slots) for array in quad_a]
    quad_b = [array.reshape(slots) for array in quad_b]
    tile = lambda cols: pl.BlockSpec((FFN_TILE, cols), lambda i: (i, 0))
    bf = lambda cols: jax.ShapeDtypeStruct((tok, cols), BF)
    return pl.pallas_call(
        ffn_kernel,
        grid=(tok // FFN_TILE,),
        out_shape=(
            bf(width),
            bf(width),
            bf(FF),
            bf(FF),
            bf(width),
            bf(width),
            bf(width),
            jax.ShapeDtypeStruct((EXTRA, width), F32),
        ),
        in_specs=[tile(width)] * 3 + [spec_whole((EXTRA, width))] + [spec_any()] * 12,
        out_specs=(
            tile(width),
            tile(width),
            tile(FF),
            tile(FF),
            tile(width),
            tile(width),
            tile(width),
            spec_whole((EXTRA, width)),
        ),
        scratch_shapes=[
            pltpu.VMEM((FF // width, width, width), BF),
            pltpu.VMEM((FF // SLOT, 2, 48, width), BF),
            pltpu.VMEM((width, width), BF),
            pltpu.VMEM((FF // width, FFN_TILE, width), F32),
            pltpu.SemaphoreType.DMA((2,)),
            pltpu.SemaphoreType.DMA,
            pltpu.SemaphoreType.DMA,
        ],
        compiler_params=params(BIG),
        cost_estimate=pl.CostEstimate(
            flops=8 * tok * width * FF, bytes_accessed=40 * MIB, transcendentals=2 * tok * FF
        ),
        name="feed_forward",
    )(stream, ctx, out_grad, small, *att_quad, *quad_a, *quad_b)


def send_slot(parts, far_core, slot, offset, src, sem):
    at = pl.multiple_of(lax.bitwise_and(slot, 7) * SLOT + offset, 16)

    def copy(ref):
        pltpu.make_async_copy(src, ref.at[pl.ds(at, src.shape[0]), :], sem).start()

    pick(2 * far_core + lax.shift_right_logical(slot, 3), parts, copy)


def part_shapes(width, small):
    rows = [8 * SLOT, 8 * SLOT, 8 * SLOT, 8 * SLOT + (EXTRA if small else 0)]
    return tuple(jax.ShapeDtypeStruct((count, width), BF) for count in rows)


def wait_reuse(stage, sems, buf, step):
    @pl.when(step >= 2)
    def _():
        wait_whole(stage.at[buf], sems.at[buf])


def wait_last(stage, sems, step, steps):
    @pl.when(step == steps - 1)
    def _():
        for buf in range(2):
            wait_whole(stage.at[buf], sems.at[buf])


def send_in_blocks(parts, me, late, part, stage, buf, sem):
    def body(chunk, carry):
        far_core, slot = slot_of(chunk, me, late)
        src = stage.at[buf, pl.ds(pl.multiple_of(chunk * 48, 16), 48)]
        send_slot(parts, far_core, slot, part * 48, src, sem)
        return carry

    lax.fori_loop(0, 16, body, 0)


def ffn_grad_kernel(x_ref, hid_ref, dhid_ref, dfb_ref, sums_ref, *refs):
    parts_a, parts_b = refs[0:4], refs[4:8]
    held, stage, small_stage, held_sem, sems, small_sem = refs[8:]
    width = x_ref.shape[1]
    me = lax.axis_index("fsdp")
    step = pl.program_id(0)
    buf = lax.rem(step, 2)
    small_rows = parts_b[3].at[pl.ds(8 * SLOT, EXTRA), :]

    def fetch(index):
        into, sem = held.at[2 + lax.rem(index, 2)], held_sem.at[2 + lax.rem(index, 2)]

        def start(ref, block):
            at = pl.multiple_of(block * width, LANES)
            pltpu.make_async_copy(ref.at[:, pl.ds(at, width)], into, sem).start()

        @pl.when(index < 4)
        def _():
            start(hid_ref, index)

        @pl.when(index >= 4)
        def _():
            start(dhid_ref, index - 2)

    @pl.when(step == 0)
    def _():
        pltpu.make_async_copy(dfb_ref, held.at[0], held_sem.at[0]).start()
        fetch(step)
        pltpu.make_async_copy(x_ref, held.at[1], held_sem.at[1]).start()
        small_stage[...] = sums_ref[...].astype(BF)
        pltpu.make_async_copy(small_stage, small_rows, small_sem).start()
        wait_whole(held.at[0], held_sem.at[0])

    @pl.when(step < 5)
    def _():
        fetch(step + 1)

    @pl.when(step == 4)
    def _():
        wait_whole(held.at[1], held_sem.at[1])

    wait_whole(held.at[2 + buf], held_sem.at[2 + buf])
    wait_reuse(stage, sems, buf, step)
    second = lax.div(step, 4)
    left = (2 + buf) * (1 - second) + second
    stage[buf] = dot_tn(held[left], held[(2 + buf) * second]).astype(BF)

    @pl.when(step < 4)
    def _():

        def body(chunk, carry):
            for unit in range(2):
                far_core, slot = slot_of(16 + 4 * step + chunk, me, unit == 1)
                at = pl.multiple_of((2 * chunk + unit) * SLOT, 32)
                src = stage.at[buf, pl.ds(at, SLOT)]
                send_slot((parts_a, parts_b)[unit], far_core, slot, 0, src, sems.at[buf])
            return carry

        lax.fori_loop(0, 4, body, 0)

    @pl.when(step >= 4)
    def _():
        send_in_blocks(parts_b, me, True, step - 4, stage, buf, sems.at[buf])

    @pl.when(step == 5)
    def _():
        wait_whole(small_stage, small_sem)

    wait_last(stage, sems, step, 6)


def ffn_grads(x_low, hidden, dhid, dfb, sums):
    tok, width = x_low.shape
    out = pl.pallas_call(
        ffn_grad_kernel,
        grid=(6,),
        out_shape=part_shapes(width, False) + part_shapes(width, True),
        in_specs=[spec_any()] * 4 + [spec_whole((EXTRA, width))],
        out_specs=(spec_any(),) * 8,
        scratch_shapes=[
            pltpu.VMEM((4, tok, width), BF),
            pltpu.VMEM((2, width, width), BF),
            pltpu.VMEM((EXTRA, width), BF),
            pltpu.SemaphoreType.DMA((4,)),
            pltpu.SemaphoreType.DMA((2,)),
            pltpu.SemaphoreType.DMA,
        ],
        compiler_params=params(BIG),
        cost_estimate=pl.CostEstimate(
            flops=3 * tok * width * FF, bytes_accessed=24 * MIB, transcendentals=0
        ),
        name="ffn_grads",
    )(x_low, hidden, dhid, dfb, sums)
    return out[0:4], out[4:8]


def ffn_rest_kernel(x_ref, dhid_ref, *refs):
    parts = refs[4:8]
    stage, sems = refs[8:]
    me = lax.axis_index("fsdp")
    step = pl.program_id(0)
    stage[step] = dot_tn(x_ref[...], dhid_ref[...]).astype(BF)
    send_in_blocks(parts, me, False, step, stage, step, sems.at[step])
    wait_last(stage, sems, step, 2)


def ffn_rest(x_low, dhid, parts):
    tok, width = x_low.shape
    return pl.pallas_call(
        ffn_rest_kernel,
        grid=(2,),
        out_shape=part_shapes(width, False),
        in_specs=[spec_whole((tok, width)), pl.BlockSpec((tok, width), lambda i: (0, i))]
        + [spec_any()] * 4,
        out_specs=(spec_any(),) * 4,
        input_output_aliases={2 + i: i for i in range(4)},
        scratch_shapes=[pltpu.VMEM((2, width, width), BF), pltpu.SemaphoreType.DMA((2,))],
        compiler_params=params(BIG),
        cost_estimate=pl.CostEstimate(
            flops=tok * width * FF, bytes_accessed=8 * MIB, transcendentals=0
        ),
        name="ffn_rest",
    )(x_low, dhid, *parts)


def backward_kernel(held, q_ref, k_ref, v_ref, dctx_ref, lse_ref, seg_row_ref, *refs):
    dq_ref, dk_ref, dv_ref = refs[held:]
    left = head_mask(q_ref.shape[0])
    same = as_column(seg_row_ref[0]) == seg_row_ref[0].astype(F32)
    heads = 2 * BWD_PAIRS
    held_a, held_b, held_c = {}, {}, {}

    def pair_cols(head):
        return slice(head // 2 * LANES, (head // 2 + 1) * LANES)

    def products(head):
        cols = pair_cols(head)
        keep = left if head % 2 == 0 else jnp.logical_not(left)
        own = jnp.where(keep, q_ref[:, cols], jnp.zeros((keep.shape), BF))
        own_grad = jnp.where(keep, dctx_ref[:, cols], jnp.zeros((keep.shape), BF))
        scores = dot_nt(k_ref[:, cols], own)
        held_a[head] = (own, own_grad, scores, dot_nt(v_ref[:, cols], own_grad))

    def softmax_back(head):
        own, own_grad, scores, grad_probs = held_a.pop(head)
        scores = jnp.where(same, scores, MASKED_SCORE)
        probs = jnp.exp(scores - lse_ref[0, head // 2, head % 2 : head % 2 + 1, :])
        inner = jnp.sum(grad_probs * probs, axis=0, keepdims=True)
        grad_scores = (probs * (grad_probs - inner)).astype(BF)
        held_b[head] = (own, own_grad, probs.astype(BF), grad_scores)

    def outputs(head):
        own, own_grad, probs, grad_scores = held_b.pop(head)
        cols = pair_cols(head)
        keys_t = k_ref[:, cols].T[(head % 2) * HEAD_DIM : (head % 2 + 1) * HEAD_DIM]
        grad_q = dot_nn(keys_t, grad_scores)
        grad_k = dot_nn(grad_scores, own)
        grad_v = dot_nn(probs, own_grad)
        if head % 2 == 0:
            held_c[0] = (grad_q, grad_k, grad_v)
            return
        first_q, first_k, first_v = held_c.pop(0)
        both_q = jnp.concatenate([first_q, grad_q]).T
        dq_ref[:, cols] = (both_q.astype(BF) * 0.125).astype(BF)
        dk_ref[:, cols] = (first_k + grad_k).astype(BF)
        dv_ref[:, cols] = (first_v + grad_v).astype(BF)

    for tick in range(heads + 2):
        if tick < heads:
            products(tick)
        if 0 <= tick - 1 < heads:
            softmax_back(tick - 1)
        if tick >= 2:
            outputs(tick - 2)


def attention_backward(at, qkv, dctx, lse, seg_row, held=()):
    tok, width = qkv.shape[1:]
    seq = seg_row.shape[2]
    tile, row, stat, parts = sequence_specs(at, seq, BWD_PAIRS)
    return pl.pallas_call(
        functools.partial(backward_kernel, len(held)),
        grid=(width // LANES // BWD_PAIRS,),
        out_shape=(jax.ShapeDtypeStruct((tok, width), BF),) * 3,
        in_specs=parts + [tile(), stat(), row()]
        + [spec_any() for _ in held],
        out_specs=(tile(), tile(), tile()),
        input_output_aliases={6 + i: i for i in range(len(held))},
        compiler_params=params(54),
        cost_estimate=pl.CostEstimate(
            flops=40 * seq * seq * width,
            bytes_accessed=6 * MIB,
            transcendentals=seq * seq * width // HEAD_DIM,
        ),
        name="attention_backward",
    )(qkv, qkv, qkv, dctx, lse, seg_row, *held)


def input_grad_kernel(dq_ref, dk_ref, dv_ref, dob_ref, masked_ref, *refs):
    quad = refs[0:4]
    dx_ref, small_ref, weights, sems = refs[4:]
    width = dq_ref.shape[1]
    step = pl.program_id(0)

    @pl.when(step == 0)
    def _():
        load_projections(quad, weights, sems)
        small_ref[...] = jnp.zeros_like(small_ref)

    grad = dob_ref[...].astype(F32)
    for matrix in range(3):
        rows = slice(matrix * width, (matrix + 1) * width)

        @pl.when(step == 0)
        def _():
            wait_whole(weights.at[rows], sems.at[matrix])

        grad = grad + dot_nt((dq_ref, dk_ref, dv_ref)[matrix][...], weights[rows])
    chosen = as_column(masked_ref[0]) == 1.0
    dx_ref[...] = jnp.where(chosen, 0.0, grad)
    small_ref[0:1] += column_sum(dq_ref[...].astype(F32))
    small_ref[1:2] += column_sum(dv_ref[...].astype(F32))
    small_ref[5:6] += column_sum(jnp.where(chosen, grad, 0.0))


def input_grads(dq, dk, dv, dob, masked_row, quad):
    tok, width = dq.shape
    rows = TILE
    per = masked_row.shape[2] // rows
    tile = lambda cols: pl.BlockSpec((rows, cols), lambda i: (i, 0))
    whole = spec_whole((EXTRA, width))
    return pl.pallas_call(
        input_grad_kernel,
        grid=(tok // rows,),
        out_shape=(
            jax.ShapeDtypeStruct((tok, width), F32),
            jax.ShapeDtypeStruct((EXTRA, width), F32),
        ),
        in_specs=[tile(width)] * 4
        + [pl.BlockSpec((1, 1, rows), lambda i: (i // per, 0, i % per))]
        + [spec_any()] * 4,
        out_specs=(tile(width), whole),
        scratch_shapes=[pltpu.VMEM((3 * width, width), BF), pltpu.SemaphoreType.DMA((3,))],
        compiler_params=params(BIG),
        cost_estimate=pl.CostEstimate(
            flops=6 * tok * width * width, bytes_accessed=16 * MIB, transcendentals=0
        ),
        name="input_grads",
    )(dq, dk, dv, dob, masked_row, *quad)


def att_grad_kernel(*refs):
    sources, parts = refs[0:6], refs[6:10]
    held, stage, load_sems, sems = refs[10:]
    me = lax.axis_index("fsdp")
    step = pl.program_id(0)
    buf = lax.rem(step, 2)

    @pl.when(step == 0)
    def _():
        for number in range(6):
            pltpu.make_async_copy(sources[number], held.at[number], load_sems.at[number]).start()

    wait_reuse(stage, sems, buf, step)
    for matrix in range(4):

        @pl.when(step == matrix)
        def _():
            for number in ((0, 1), (2, 3), (4,), (5,))[matrix]:
                wait_whole(held.at[number], load_sems.at[number])

    left = 2 * jnp.minimum(step, 1)
    stage[buf] = dot_tn(held[left], held[left + jnp.maximum(step, 1)]).astype(BF)
    first = lax.rem(step + 3, 4) * 8

    def body(piece, carry):
        far_core, slot = slot_of(first + piece, me)
        src = stage.at[buf, pl.ds(pl.multiple_of(piece * SLOT, 32), SLOT)]
        send_slot(parts, far_core, slot, 0, src, sems.at[buf])
        return carry

    lax.fori_loop(0, 8, body, 0)
    wait_last(stage, sems, step, 4)


def att_grads(ctx, dob, stream, dq, dk, dv):
    tok, width = stream.shape
    return pl.pallas_call(
        att_grad_kernel,
        grid=(4,),
        out_shape=part_shapes(width, False),
        in_specs=[spec_any()] * 6,
        out_specs=(spec_any(),) * 4,
        scratch_shapes=[
            pltpu.VMEM((6, tok, width), BF),
            pltpu.VMEM((2, width, width), BF),
            pltpu.SemaphoreType.DMA((6,)),
            pltpu.SemaphoreType.DMA((2,)),
        ],
        compiler_params=params(BIG),
        cost_estimate=pl.CostEstimate(
            flops=8 * tok * width * width, bytes_accessed=16 * MIB, transcendentals=0
        ),
        name="att_grads",
    )(ctx, dob, stream, dq, dk, dv)


def flat_ffn_kernel(a_ref, b_ref, out_ref):
    first = lax.axis_index("fsdp") < 16

    @pl.when(first)
    def _():
        for block in range(4):
            source = a_ref if block < 2 else b_ref
            rows = slice((block % 2) * 48, (block % 2) * 48 + 48)
            for part in range(6):
                cols = slice(part * LANES, (part + 1) * LANES)
                out_ref[pl.ds(6 * block + part, 48, stride=24), :] = source[rows, cols]

    @pl.when(jnp.logical_not(first))
    def _():
        for part in range(6):
            cols = slice(part * LANES, (part + 1) * LANES)
            out_ref[pl.ds(part, SLOT, stride=6), :] = a_ref[:, cols]
            out_ref[pl.ds(6 * SLOT + part, SLOT, stride=6), :] = b_ref[:, cols]


def flatten_ffn(grad_a, grad_b):
    return pl.pallas_call(
        flat_ffn_kernel,
        out_shape=jax.ShapeDtypeStruct((12 * SLOT, LANES), F32),
        in_specs=[spec_vmem()] * 2,
        out_specs=spec_vmem(),
        compiler_params=params(16),
        name="flatten_ffn",
    )(grad_a, grad_b)


def flat_att_kernel(kept_ref, got_ref, ffn_ref, late_ref, out_ref, head_ref):
    for part in range(6):
        cols = slice(part * LANES, (part + 1) * LANES)
        total = kept_ref[:, cols].astype(F32) + got_ref[0:SLOT, cols].astype(F32)
        out_ref[pl.ds(part, SLOT, stride=6), :] = total
    head_ref[0:64, :] = out_ref[0:64, :]
    head_ref[64:128, :] = ffn_ref[0:64, :]

    @pl.when(lax.axis_index("fsdp") == 0)
    def _():
        for part in range(6):
            cols = slice(part * LANES, (part + 1) * LANES)
            head_ref[pl.ds(part, 6, stride=6), :] = late_ref[0:6, cols]


def flatten_att(kept, got, ffn_flat, late):
    return pl.pallas_call(
        flat_att_kernel,
        out_shape=(
            jax.ShapeDtypeStruct((6 * SLOT, LANES), F32),
            jax.ShapeDtypeStruct((128, LANES), F32),
        ),
        in_specs=[spec_vmem()] * 4,
        out_specs=(spec_vmem(),) * 2,
        compiler_params=params(16),
        name="flatten_att",
    )(kept, got, ffn_flat, late)


def update_kernel(last, rate, *refs):
    inputs, outputs, bufs = refs[0:10], refs[10:18], refs[18:20]
    me = lax.axis_index("fsdp")
    head_ref, small_ref = inputs[2], inputs[3]
    for unit in range(2):
        flat_ref = inputs[unit]
        w_ref, m_ref, a_ref = inputs[4 + 3 * unit : 7 + 3 * unit]
        w_out, m_out, a_out, low_out = outputs[4 * unit : 4 * unit + 4]
        buf = bufs[unit]
        aligned = flat_ref.shape[0]
        first, count = ((0, 6), (6, 7))[unit]
        buf[0:aligned, :] = flat_ref[...]
        buf[aligned : aligned + 64, :] = head_ref[unit * 64 : unit * 64 + 64, :]

        @pl.when(me == last)
        def _():
            buf[aligned : aligned + 64, :] = jnp.zeros((64, LANES), F32)
            for part in range(6):
                cols = slice(part * LANES, (part + 1) * LANES)
                small = small_ref[first : first + count, cols]
                if unit == 0:
                    small = small + head_ref[pl.ds(part, count, stride=6), :]
                buf[pl.ds(aligned + part, count, stride=6), :] = small

        grad = buf[pl.ds(2 * me, w_ref.shape[0]), :]
        moment = 0.5 * m_ref[...] + grad
        master = w_ref[...] - rate * (grad + 0.5 * moment)
        m_out[...] = moment
        w_out[...] = master
        a_out[...] = 0.5 * a_ref[...] + 0.5 * master
        low_out[...] = master.astype(BF)


def update(flats, head, small, rate, devices, att, ffn):
    shapes = []
    for arrays in (att, ffn):
        f32 = jax.ShapeDtypeStruct(arrays[0].shape, F32)
        shapes += [f32, f32, f32, jax.ShapeDtypeStruct(arrays[0].shape, BF)]
    out = pl.pallas_call(
        functools.partial(update_kernel, devices - 1, rate),
        out_shape=tuple(shapes),
        in_specs=[spec_vmem()] * 10,
        out_specs=(spec_vmem(),) * 8,
        scratch_shapes=[pltpu.VMEM((flat.shape[0] + 64, LANES), F32) for flat in flats],
        compiler_params=params(16),
        name="update",
    )(*flats, head, small, *att, *ffn)
    return out


def local_exchange(
    block_input,
    seg_ids,
    masked,
    out_grad,
    att_master,
    att_moment,
    att_average,
    ffn_master,
    ffn_moment,
    ffn_average,
):
    tok, width = block_input.shape
    seq_count, seq = seg_ids.shape
    devices = lax.axis_size("fsdp")
    up = [(i, i + 1) for i in range(devices - 1)]
    down = [(i + 1, i) for i in range(devices - 1)]
    tails = lax.ppermute(row_tails(att_master, ffn_master), "fsdp", up)
    masked_row = masked.reshape(seq_count, 1, seq)
    seg_row = seg_ids.reshape(seq_count, 1, seq)
    att, chunk_a, chunk_b = prepare(att_master, ffn_master, tails, devices, width)
    got, masked_row, seg_row = phase(exchange(att, 0), masked_row, seg_row)
    att = widen_small(att, got)
    got = exchange(att, 1)
    att, unit_a = phase(widen_small(att, got), chunk_a)
    got, got_a = phase(exchange(att, 2), exchange(unit_a, 0))
    att, unit_a, unit_b = phase(widen_small(att, got), widen(unit_a, got_a), chunk_b)
    att_next, att_far, got_a, got_b = phase(
        exchange(att, 3), exchange(att, 4), exchange(unit_a, 1), exchange(unit_b, 0)
    )
    unit_a, unit_b, att_next = phase(widen(unit_a, got_a), widen(unit_b, got_b), att_next)
    att_last, got_b, block_input = phase(exchange(att_next, 4), exchange(unit_b, 2), block_input)
    att = (att, att_next, att_far, att_last)
    unit_a, unit_b, block_input = phase(unit_a, widen(unit_b, got_b), block_input)
    got_b = exchange(unit_b, 1)
    stream, qkv, small = project(block_input, masked_row, att)
    got_a, qkv = phase(exchange(unit_a, 2), qkv)
    unit_a, qkv = phase(widen(unit_a, got_a), qkv)
    held = attention_forward(0, qkv, seg_row)
    a_next, a_far, got_b, held = phase(exchange(unit_a, 3), exchange(unit_a, 4), got_b, held)
    unit_b, a_next, held = phase(widen(unit_b, got_b), a_next, held)
    ctx, lse = attention_forward(1, qkv, seg_row, held)
    b_next, b_far, a_last, ctx = phase(
        exchange(unit_b, 3), exchange(unit_b, 4), exchange(a_next, 4), ctx
    )
    b_last = exchange(b_next, 4)
    block_output, x_low, hidden, dhid, dfb, dob, dctx, sums = feed_forward(
        stream,
        ctx,
        out_grad,
        small,
        att,
        (unit_a, a_next, a_far, a_last),
        (unit_b, b_next, b_far, b_last),
    )
    part_a, part_b = ffn_grads(x_low, hidden, dhid, dfb, sums)
    part_b, dhid = phase(part_b, dhid)
    part_a = ffn_rest(x_low, dhid, part_a)
    high_b, low_b, part_a = phase(exchange(part_b[3], 4), exchange(part_b[2], 4), part_a)
    small_sum = sums + high_b[8 * SLOT :].astype(F32)
    high_b = add_small(total_of((part_b[1], high_b), 0, 8 * SLOT).astype(BF), small_sum)
    high_b, part_a, dctx = phase(high_b, part_a, dctx)
    held = attention_backward(0, qkv, dctx, lse, seg_row)
    got_b, high_a, low_a, held = phase(
        exchange(high_b, 3), exchange(part_a[3], 4), exchange(part_a[2], 4), held
    )
    high_a = total_of((part_a[1], high_a), 0, 8 * SLOT).astype(BF)
    small_sum = small_sum + got_b[8 * SLOT :].astype(F32)
    kept_b, sent_b = halve(part_b[0], low_b, got_b[: 8 * SLOT])
    high_a, sent_b, held = phase(high_a, add_small(sent_b, small_sum), held)
    dq, dk, dv = attention_backward(1, qkv, dctx, lse, seg_row, held)
    got_a, got_b, dq = phase(exchange(high_a, 3), exchange(sent_b, 1), dq)
    kept_a, sent_a = halve(part_a[0], low_a, got_a)
    small_sum = small_sum + got_b[4 * SLOT :].astype(F32)
    kept_b, sent_b = halve(kept_b, got_b[: 4 * SLOT])
    joined, dq = phase(jnp.concatenate([sent_a, sent_b, small_sum.astype(BF)]), dq)
    part = att_grads(ctx, dob, stream, dq, dk, dv)
    high = exchange(part[3], 4)
    got, kept = phase(exchange(joined, 2), part[0])
    got_a, got_b = got[: 4 * SLOT], got[4 * SLOT :]
    kept_a, sent_a = halve(kept_a, got_a)
    small_sum = small_sum + got_b[2 * SLOT :].astype(F32)
    kept_b, sent_b = halve(kept_b, got_b[: 2 * SLOT])
    high, sent_a, sent_b = phase(high, sent_a, add_small(sent_b, small_sum))
    got_b = exchange(sent_b, 0)
    high = total_of((part[1], high), 0, 8 * SLOT).astype(BF)
    high, sent_a, dq = phase(high, sent_a, dq)
    input_grad, late = input_grads(dq, dk, dv, dob, masked_row, att)
    got, low, got_a, got_b, late = phase(
        exchange(high, 3), exchange(part[2], 4), exchange(sent_a, 1), got_b, late
    )
    kept, sent = halve(kept, low, got)
    kept_a, sent_a = halve(kept_a, got_a)
    sent, sent_a, late = phase(sent, sent_a, late)
    got, got_a = phase(exchange(add_small(sent, late), 2), exchange(sent_a, 0))
    late = late + got[4 * SLOT :].astype(F32)
    kept, sent = halve(kept, got[: 4 * SLOT])
    sent, late, got_a, got_b = phase(sent, late, got_a, got_b)
    got = exchange(sent, 1)
    late = late + exchange(late.astype(BF), 3).astype(F32)
    late = late + exchange(late.astype(BF), 4).astype(F32)
    kept, sent = halve(kept, got)
    sent, got_a, got_b = phase(add_small(sent, late), got_a, got_b)
    got = exchange(sent, 0)
    small_sum = small_sum + got_b[SLOT:].astype(F32)
    grad_a = total_of((kept_a, got_a), 0, SLOT)
    grad_b = total_of((kept_b, got_b), 0, SLOT)
    ffn_flat = flatten_ffn(grad_a, grad_b)
    got, ffn_flat, small_sum = phase(got, ffn_flat, small_sum)
    late = late + got[SLOT:].astype(F32)
    att_flat, heads = flatten_att(kept, got, ffn_flat, late)
    heads = lax.ppermute(heads, "fsdp", down + [(0, devices - 1)])
    rate = 0.05 / math.sqrt(tok * devices)
    new = update(
        (att_flat, ffn_flat),
        heads,
        small_sum + late,
        rate,
        devices,
        (att_master, att_moment, att_average),
        (ffn_master, ffn_moment, ffn_average),
    )
    return (block_output, input_grad) + tuple(new)


def chunked(mesh):
    return mesh.shape["fsdp"] == 32


def solution(mesh):
    in_specs = (
        P("fsdp", None),
        P("fsdp", None),
        P("fsdp", None),
        P("fsdp", None),
        P("fsdp", None),
        P("fsdp", None),
        P("fsdp", None),
        P("fsdp", None),
        P("fsdp", None),
        P("fsdp", None),
    )
    out_specs = (
        P("fsdp", None),
        P("fsdp", None),
        P("fsdp", None),
        P("fsdp", None),
        P("fsdp", None),
        P("fsdp", None),
        P("fsdp", None),
        P("fsdp", None),
        P("fsdp", None),
        P("fsdp", None),
    )
    body = local_exchange if chunked(mesh) else local
    return jax.shard_map(body, mesh=mesh, in_specs=in_specs, out_specs=out_specs, check_vma=False)
```
